32 devices in a mesh: grp: 2 (over x), px: 4 (over y, core), pz: 4 (over z).
Axes of the slice: x: 2, y: 2, z: 4, core: 2. Of those that a mesh axis runs over, the one named last changes fastest.
Arguments:
- cell_index: int32 [1024, 512], P(('px', 'pz')), may hold values from 0 to 255
- block_index: int32 [1024], P(('px', 'pz')), may hold values from 0 to 255
- volume: float32 [1024, 512], P(('px', 'pz')), may hold values from 0.2 to 2
- response_rate: float32 [1024, 512], P(('px', 'pz')), may hold values from 0.2 to 2
- spanwise_position: float32 [1024, 512], P(('px', 'pz')), may hold values from -3.140625 to 3.140625
- particle_velocity: float32 [3, 1024, 512], P(None, ('px', 'pz')), may hold values from -6 to 6
- seen_velocity: float32 [3, 1024, 512], P(None, ('px', 'pz')), may hold values from -6 to 6
- fluid_velocity: float32 [512, 3, 8, 2, 1024], P(None, None, ('grp', 'pz'), None, 'px'), may hold values from -6 to 6
- eigen_basis: float32 [512, 512], replicated, may hold values from -1 to 2, as said below
- eigen_inverse: float32 [512, 512], replicated, may hold values from -8 to 8, as said below
- eigenvalues: float32 [512], replicated, may hold values from 1 to 100000
Outputs:
- velocity_planes: bfloat16 [512, 3, 8, 2, 2048], P(('px', 'pz'), None, 'grp')
- updated_velocity: float32 [3, 1024, 512], P(None, ('px', 'pz'))
The draws below stay inside these ranges and needn't reach their ends.
Inputs may be any that keep to these rules, and one draw needn't show every extreme that they name: eigen_inverse is the inverse of eigen_basis. eigen_basis has a dominant unit diagonal.
All inputs are finite; a program needn't handle non-finite values.
Results may differ from the reference program's by a relative error of at most 0.007.
Values may be sent and summed in bfloat16 or wider, within the bound.
No kernel may reach another device: no remote copies, remote signals or barrier semaphores. Data moves between devices by JAX's collectives and lax.ppermute only.
A program may use at most 128 MiB of HBM per device.

```python
import math
import jax
import jax.numpy as jnp
from jax import lax

NX = 2048
KX = 1024
NY = 512
CB = 256
PT = 512
TILE_DEV = 64
MZ = 8
NB = 256
TILES = 1024
N_PX = 4
N_PZ = 4


def basis_matrix(key):
    sub_key = jax.random.fold_in(key, 17)
    noise = jax.random.normal(sub_key, (NY, NY), jnp.float32)
    return jnp.eye(NY, dtype=jnp.float32) + 0.5 * noise / math.sqrt(NY)


def draw_eigen_basis(key, part):
    return basis_matrix(key)


def draw_eigen_inverse(key, part):
    return jnp.linalg.inv(basis_matrix(key))


def plant(values, key, low, high):
    index_at = [jax.random.randint(jax.random.fold_in(key, axis), (), 0, length) for axis, length in enumerate(values.shape)]
    widest = values.shape.index(max(values.shape))
    neighbour = index_at[:widest] + [(index_at[widest] + 1) % values.shape[widest]] + index_at[widest + 1:]
    return values.at[tuple(index_at)].set(low).at[tuple(neighbour)].set(high)


def block_scale(rng, extent, cuts, least, top_value):
    gain, own = 1.0, jax.random.fold_in(rng, 6)
    for dim, parts in cuts:
        steps = jnp.exp(jax.random.uniform(jax.random.fold_in(own, dim), (parts,), jnp.float32, least / len(cuts), top_value / len(cuts)))
        gain = gain * jnp.repeat(steps, extent[dim] // parts).reshape([-1 if axis == dim else 1 for axis in range(len(extent))])
    return gain


def normal_values(own_key, dims, spread, most, cuts=(), kind=jnp.bfloat16):
    entries = spread * jax.random.normal(own_key, dims, jnp.float32)
    if cuts:
        entries = entries * block_scale(own_key, dims, cuts, -0.22, 0.18)
    return jnp.clip(entries, -most, most).astype(kind)


def setup_inputs(seed: int = 0) -> dict:
    seeds = jax.random.split(jax.random.key(seed), 12)
    cell_index = plant(jax.random.randint(seeds[0], (TILES, PT), 0, CB), jax.random.fold_in(seeds[0], 1), 0, CB - 1).astype(jnp.int32)
    block_index = plant(jax.random.randint(seeds[1], (TILES,), 0, NB), jax.random.fold_in(seeds[1], 1), 0, NB - 1).astype(jnp.int32)
    volume = jnp.clip(jnp.exp(math.log(2.0) - 2.3025851 * jax.random.uniform(seeds[2], (TILES, PT), jnp.float32) ** block_scale(seeds[2], (TILES, PT), ((0, 16),), -0.2, 0.2)), 0.2, 2.0)
    response_rate = jnp.clip(jnp.exp(math.log(2.0) - 2.3025851 * jax.random.uniform(seeds[3], (TILES, PT), jnp.float32) ** block_scale(seeds[3], (TILES, PT), ((0, 16),), -0.2, 0.2)), 0.2, 2.0)
    spanwise_position = jnp.clip(jax.random.uniform(seeds[4], (TILES, PT), jnp.float32, -3.140625, 3.140625), -3.140625, 3.140625)
    particle_velocity = normal_values(seeds[5], (3, TILES, PT), 1.0, 6.0, ((1, 16),), jnp.float32)
    seen_velocity = normal_values(seeds[6], (3, TILES, PT), 1.0, 6.0, ((1, 16),), jnp.float32)
    fluid_velocity = normal_values(seeds[7], (NY, 3, MZ, 2, KX), 1.0, 6.0, ((2, 8), (4, 4)), jnp.float32)
    eigen_basis = draw_eigen_basis(jax.random.fold_in(seeds[11], 71), 0)
    eigen_inverse = draw_eigen_inverse(jax.random.fold_in(seeds[11], 71), 0)
    eigenvalues = jnp.clip(jnp.exp(jax.random.uniform(seeds[10], (NY,), jnp.float32, math.log(1.0), math.log(100000.0))), 1.0, 100000.0)
    return dict(cell_index=cell_index, block_index=block_index, volume=volume, response_rate=response_rate, spanwise_position=spanwise_position, particle_velocity=particle_velocity, seen_velocity=seen_velocity, fluid_velocity=fluid_velocity, eigen_basis=eigen_basis, eigen_inverse=eigen_inverse, eigenvalues=eigenvalues)


time_step = 0.5
gravity = 0.8
viscosity = 0.0001

def wave_table():
    positions = jnp.arange(NX, dtype=jnp.int32)
    stream_waves = jnp.arange(KX, dtype=jnp.int32) - KX // 2
    phase_turns = jnp.mod(positions[:, None] * stream_waves[None, :], NX)
    angles = phase_turns.astype(jnp.float32) * (2.0 * math.pi / NX)
    factor = 1.0 / math.sqrt(NX)
    return jnp.stack([jnp.cos(angles) * factor, jnp.sin(angles) * factor], axis=1).astype(jnp.bfloat16)

def reference(cell_index, block_index, volume, response_rate, spanwise_position, particle_velocity, seen_velocity, fluid_velocity, eigen_basis, eigen_inverse, eigenvalues):
    slabs = N_PX * N_PZ
    slab_rows = NY // slabs
    strips = NX // CB
    highest = lax.Precision.HIGHEST
    forward_waves = wave_table()
    forward_float = forward_waves.astype(jnp.float32).reshape(strips, CB, 2, KX)
    inverse_float = jnp.transpose(forward_waves, (2, 1, 0)).astype(jnp.float32)
    spanwise_waves = (jnp.arange(MZ) + 1).astype(jnp.float32)
    lanes = jnp.arange(CB, dtype=jnp.int32)
    cell_slabs = cell_index.reshape(slabs, TILE_DEV, PT)
    block_slabs = block_index.reshape(slabs, TILE_DEV)
    volume_slabs = volume.reshape(slabs, TILE_DEV, PT)
    rate_slabs = response_rate.reshape(slabs, TILE_DEV, PT)
    place_slabs = spanwise_position.reshape(slabs, TILE_DEV, PT)
    motion_slabs = jnp.moveaxis(particle_velocity.reshape(3, slabs, TILE_DEV, PT), 1, 0)
    seen_slabs = jnp.moveaxis(seen_velocity.reshape(3, slabs, TILE_DEV, PT), 1, 0)

    def slab_forcing(inputs):
        cell_slot, block_slot, amount, rate, place, motion, seen = inputs
        angles = place[..., None] * spanwise_waves
        phases = jnp.stack([jnp.cos(angles), -jnp.sin(angles)], axis=-2)
        drag_force = amount * rate * (seen - motion)
        amounts = jnp.moveaxis(jnp.concatenate([amount[None], drag_force], axis=0), 0, -1)
        payload = (amounts[..., :, None, None] * phases[..., None, :, :]).astype(jnp.bfloat16)
        payload = payload.reshape(TILE_DEV, PT, 8 * MZ).astype(jnp.float32)
        one_hot = (cell_slot[..., None] == lanes).astype(jnp.float32)
        shares = jnp.einsum('tpc,tpw->twc', one_hot, payload, precision=highest)
        totals = jnp.zeros((slab_rows * strips, 8 * MZ, CB), jnp.float32).at[block_slot].add(shares)
        field = totals.astype(jnp.bfloat16).astype(jnp.float32).reshape(slab_rows, strips, 8 * MZ, CB)
        product = jnp.einsum('ybwc,bcsi->ywsi', field, forward_float, precision=highest)
        product = product.reshape(slab_rows, 4, 2, MZ, 2, KX)
        real_part = product[:, :, 0, :, 0] + product[:, :, 1, :, 1]
        imag_part = product[:, :, 1, :, 0] - product[:, :, 0, :, 1]
        return jnp.stack([real_part, imag_part], axis=3).astype(jnp.bfloat16)
    forcing = lax.map(slab_forcing, (cell_slabs, block_slabs, volume_slabs, rate_slabs, place_slabs, motion_slabs, seen_slabs))
    forcing = forcing.reshape(NY, 4, MZ, 2, KX)
    stream_wave = (jnp.arange(KX) - KX // 2).astype(jnp.float32) * 0.5
    vertical = (jnp.arange(3) == 1).astype(jnp.float32)[None, :, None, None]

    def solve_mode(inputs):
        forcing_mode, state_mode, span_wave = inputs
        force = forcing_mode[:, 1:].astype(jnp.float32) - gravity * vertical * forcing_mode[:, :1].astype(jnp.float32)
        wave_square = stream_wave * stream_wave + span_wave * span_wave
        damping = 1.0 / (1.0 + viscosity * (eigenvalues[:, None, None, None] + wave_square[None, None, None, :]))
        modal = jnp.einsum('ij,jcrk->icrk', eigen_inverse, state_mode + time_step * force, precision=highest)
        return jnp.einsum('ij,jcrk->icrk', eigen_basis, modal * damping, precision=highest).astype(jnp.bfloat16)
    solved = lax.map(solve_mode, (jnp.moveaxis(forcing, 2, 0), jnp.moveaxis(fluid_velocity, 2, 0), spanwise_waves))
    solved = jnp.moveaxis(solved, 0, 2).reshape(slabs, slab_rows, 3, MZ, 2, KX)
    upward = (jnp.arange(3) == 1).astype(jnp.float32)[:, None, None]

    def slab_velocity(inputs):
        solved_slab, cell_slot, block_slot, rate, place, motion = inputs
        product = jnp.einsum('ycmri,isx->ycmrsx', solved_slab.astype(jnp.float32), inverse_float, precision=highest)
        real_part = product[:, :, :, 0, 0] - product[:, :, :, 1, 1]
        imag_part = product[:, :, :, 0, 1] + product[:, :, :, 1, 0]
        planes = jnp.stack([real_part, imag_part], axis=3).astype(jnp.bfloat16)
        block_view = planes.reshape(slab_rows, 6 * MZ, strips, CB)
        block_rows = block_view[block_slot // strips, :, block_slot % strips, :].astype(jnp.float32)
        one_hot = (cell_slot[..., None] == lanes).astype(jnp.float32)
        picked = jnp.einsum('tpc,twc->tpw', one_hot, block_rows, precision=highest).reshape(TILE_DEV, PT, 3, MZ, 2)
        angles = place[..., None] * spanwise_waves
        along = lax.optimization_barrier(jnp.sum(picked[..., 0] * jnp.cos(angles)[:, :, None, :] - picked[..., 1] * jnp.sin(angles)[:, :, None, :], axis=-1))
        fluid_at = jnp.moveaxis(along, -1, 0)
        updated = motion + time_step * rate * (fluid_at - motion) - time_step * gravity * upward
        return (planes, updated)
    planes, updated = lax.map(slab_velocity, (solved, cell_slabs, block_slabs, rate_slabs, place_slabs, motion_slabs))
    velocity_planes = planes.reshape(NY, 3, MZ, 2, NX)
    updated_velocity = jnp.moveaxis(updated, 0, 1).reshape(3, slabs * TILE_DEV, PT)
    return (velocity_planes, updated_velocity)
```

```python
import functools
import math

import jax
import jax.numpy as jnp
import numpy as np
from jax import lax
from jax.experimental import pallas as pl
from jax.experimental.pallas import tpu as pltpu
from jax.sharding import PartitionSpec as P

NX = 2048
KX = 1024
CB = 256
HALF = NX // 2
PAIR = KX // 2

time_step = 0.5
gravity = 0.8
viscosity = 0.0001


def turns(rows, columns):
    phase = np.mod(np.asarray(rows)[:, None] * np.asarray(columns)[None, :], NX)
    angles = phase.astype(np.float64) * (2.0 * math.pi / NX)
    return np.cos(angles).astype(np.float32), np.sin(angles).astype(np.float32)


def forward_seeds():
    waves = np.concatenate([2 * np.arange(PAIR) - KX // 2, 2 * np.arange(PAIR) + 1 - KX // 2])
    base = turns(np.arange(8), waves)
    steps = turns(8 * 2 ** np.arange(8), waves)
    scale = np.float32(1.0 / math.sqrt(NX))
    return [base[0] * scale, base[1] * scale, steps[0], steps[1]]


def inverse_seeds():
    points = np.arange(HALF)
    bases = [turns(2 * np.arange(8) + parity - KX // 2, points) for parity in range(2)]
    steps = turns(16 * 2 ** np.arange(8), points)
    scale = np.float32(1.0 / math.sqrt(NX))
    cosines = np.stack([b[0] for b in bases]) * scale
    sines = np.stack([b[1] for b in bases]) * scale
    return [cosines, sines, steps[0], steps[1]]


def order_matrix():
    matrix = np.zeros((256, 256), np.float32)
    natural = np.arange(256)
    matrix[(natural % 2) * 128 + natural // 2, natural] = 1.0
    return matrix


def grow(cos_ref, sin_ref, base, steps, rows):
    cos_ref[0:8, :] = base[0]
    sin_ref[0:8, :] = base[1]
    done = 8
    level = 0
    while done < rows:
        turn_cos = steps[0][level : level + 1, :]
        turn_sin = steps[1][level : level + 1, :]

        def block(index, carry, done=done, turn_cos=turn_cos, turn_sin=turn_sin):
            start = pl.multiple_of(index * 8, 8)
            old_cos = cos_ref[pl.ds(start, 8), :]
            old_sin = sin_ref[pl.ds(start, 8), :]
            cos_ref[pl.ds(done + start, 8), :] = old_cos * turn_cos - old_sin * turn_sin
            sin_ref[pl.ds(done + start, 8), :] = old_sin * turn_cos + old_cos * turn_sin
            return carry

        lax.fori_loop(0, done // 8, block, 0)
        done *= 2
        level += 1


def spread_kernel(
    block_ref,
    group_ref,
    cell_ref,
    volume_ref,
    rate_ref,
    place_ref,
    motion_ref,
    seen_ref,
    base_cos_ref,
    base_sin_ref,
    step_cos_ref,
    step_sin_ref,
    order_ref,
    out_ref,
    phase_ref,
    field,
    table_cos,
    table_sin,
    table,
    left,
    *,
    half_modes,
    pencil_modes,
    pencil_waves,
):
    tiles, size = cell_ref.shape
    strips = NX // CB
    group_rows = 2 * half_modes
    width = 3 * group_rows
    slab_rows = field.shape[1] // width

    place = place_ref[...]
    first = (group_ref[0] * half_modes + 1).astype(jnp.float32)
    cos_one = jnp.cos(place)
    sin_one = jnp.sin(place)
    cos_now = jnp.cos(place * first)
    sin_now = jnp.sin(place * first)
    for mode in range(half_modes):
        for piece in range(size // 128):
            lanes = slice(piece * 128, (piece + 1) * 128)
            spot = pl.ds(mode, tiles, stride=group_rows)
            phase_ref[piece, spot, :] = cos_now[:, lanes]
            spot = pl.ds(half_modes + mode, tiles, stride=group_rows)
            phase_ref[piece, spot, :] = -sin_now[:, lanes]
        if mode + 1 < half_modes:
            cos_now, sin_now = (
                cos_now * cos_one - sin_now * sin_one,
                sin_now * cos_one + cos_now * sin_one,
            )

    grow(
        table_cos,
        table_sin,
        (base_cos_ref[...], base_sin_ref[...]),
        (step_cos_ref, step_sin_ref),
        HALF,
    )
    for parity in range(2):
        lanes = slice(parity * PAIR, (parity + 1) * PAIR)
        table[parity, 0:HALF, :] = table_cos[:, lanes].astype(jnp.bfloat16)
        table[parity, HALF:NX, :] = table_sin[:, lanes].astype(jnp.bfloat16)

    def clear(index, carry):
        field[index] = jnp.zeros(field.shape[1:], jnp.float32)
        return carry

    lax.fori_loop(0, field.shape[0], clear, 0)

    cells = lax.broadcasted_iota(jnp.int32, (CB, size), 0)

    def tile_step(tile, carry):
        row = pl.ds(tile, 1)
        volume = volume_ref[row, :]
        pull = volume * rate_ref[row, :]
        first_row = pl.ds(pl.multiple_of(tile * group_rows, 8), group_rows)
        phases = jnp.concatenate(
            [phase_ref[piece, first_row, :] for piece in range(size // 128)], axis=1
        )
        rows = []
        for component in range(3):
            amount = pull * (seen_ref[component, row, :] - motion_ref[component, row, :])
            if component == 1:
                amount = amount - gravity * volume
            rows.append(amount * phases)
        payload = jnp.concatenate(rows, axis=0).astype(jnp.bfloat16)
        one_hot = (cell_ref[row, :] == cells).astype(jnp.float32).astype(jnp.bfloat16)
        shares = lax.dot_general(
            payload, one_hot, (((1,), (1,)), ((), ())), preferred_element_type=jnp.float32
        )
        block = block_ref[tile]
        strip = block % strips
        start = pl.multiple_of((block // strips) * width, 8)
        for half in range(2):
            field[strip * 2 + half, pl.ds(start, width), :] += shares[
                :, half * 128 : (half + 1) * 128
            ]
        return carry

    lax.fori_loop(0, tiles, tile_step, 0, unroll=2)

    order = order_ref[...]
    for component in range(3):
        products = []
        for parity in range(2):
            sign = 1.0 - 2.0 * parity
            for part in range(2):
                for mode in range(half_modes):
                    column = (component * 2 + part) * half_modes + mode
                    other = (component * 2 + 1 - part) * half_modes + mode
                    rows = pl.ds(column, slab_rows, stride=width)
                    other_row = ((1 - part) * half_modes + mode) * slab_rows
                    own_row = (part * half_modes + mode) * slab_rows
                    for strip in range(HALF // 128):
                        low = field[strip, rows, :]
                        high = field[strip + HALF // 128, rows, :]
                        value = low + high if parity == 0 else low - high
                        lanes = slice(strip * 128, (strip + 1) * 128)
                        left[own_row : own_row + slab_rows, lanes] = value.astype(jnp.bfloat16)
                        turned = value if part == 1 else -value
                        lanes = slice(HALF + strip * 128, HALF + (strip + 1) * 128)
                        left[other_row : other_row + slab_rows, lanes] = turned.astype(jnp.bfloat16)
            products.append(
                jnp.dot(left[...], table[parity], preferred_element_type=jnp.float32).astype(
                    jnp.bfloat16
                )
            )
        for block in range(PAIR // 128):
            lanes = slice(block * 128, (block + 1) * 128)
            mixed = jnp.concatenate([products[0][:, lanes], products[1][:, lanes]], axis=1)
            natural = jnp.dot(mixed, order, preferred_element_type=jnp.float32).astype(jnp.bfloat16)
            for piece in range(256 // min(256, pencil_waves)):
                span = min(256, pencil_waves)
                wave = block * 256 + piece * span
                owner_px = wave // pencil_waves
                inside = wave % pencil_waves
                for part in range(2):
                    for mode in range(half_modes):
                        owner_pz = mode // pencil_modes
                        column = (
                            (component * pencil_modes + mode % pencil_modes) * 2 + part
                        ) * pencil_waves + inside
                        row = (part * half_modes + mode) * slab_rows
                        out_ref[
                            owner_px * (half_modes // pencil_modes) + owner_pz,
                            :,
                            column : column + span,
                        ] = natural[row : row + slab_rows, piece * span : (piece + 1) * span]


def table_kernel(base_cos_ref, base_sin_ref, step_cos_ref, step_sin_ref, out_ref, work_cos, work_sin):
    for parity in range(2):
        grow(
            work_cos,
            work_sin,
            (base_cos_ref[parity], base_sin_ref[parity]),
            (step_cos_ref, step_sin_ref),
            PAIR,
        )
        out_ref[parity, 0:PAIR, :] = work_cos[...].astype(jnp.bfloat16)
        out_ref[parity, PAIR:KX, :] = work_sin[...].astype(jnp.bfloat16)


def split(value):
    high = value.astype(jnp.bfloat16)
    return high, (value - high.astype(jnp.float32)).astype(jnp.bfloat16)


def dot32(a, b):
    return jnp.dot(a, b, preferred_element_type=jnp.float32)


def project_kernel(high_ref, low_ref, state_ref, out_ref):
    state_high, state_low = split(state_ref[...])
    out_ref[...] = (
        dot32(high_ref[...], state_high)
        + dot32(high_ref[...], state_low)
        + dot32(low_ref[...], state_high)
    )


def solve_kernel(
    inverse_high, inverse_low, basis_high, basis_low, damping_ref, state_ref, force_ref, out_ref
):
    force = force_ref[...]
    modal = state_ref[...] + time_step * (
        dot32(inverse_high[...], force) + dot32(inverse_low[...], force)
    )
    modal_high, modal_low = split(modal * damping_ref[...])
    solved = (
        dot32(basis_high[...], modal_high)
        + dot32(basis_high[...], modal_low)
        + dot32(basis_low[...], modal_high)
    )
    out_ref[...] = solved.astype(jnp.bfloat16)


def gather_kernel(
    block_ref,
    cell_ref,
    phase_ref,
    table_ref,
    order_ref,
    back_ref,
    planes_ref,
    part_ref,
    left,
    values,
    sampled,
    *,
    half_modes,
    pencil_modes,
    pencil_waves,
):
    tiles, size = cell_ref.shape
    strips = NX // CB
    group_rows = 2 * half_modes
    slab_rows = back_ref.shape[1]
    pz_count = half_modes // pencil_modes
    order = order_ref[...]
    component_rows = group_rows * slab_rows
    for component in range(3):
        for block in range(KX // 256):
            rows = []
            for part in range(2):
                for mode in range(half_modes):
                    pieces = []
                    span = min(256, pencil_waves)
                    for piece in range(256 // span):
                        wave = block * 256 + piece * span
                        column = (
                            (component * pencil_modes + mode % pencil_modes) * 2 + part
                        ) * pencil_waves + wave % pencil_waves
                        source = (wave // pencil_waves) * pz_count + mode // pencil_modes
                        pieces.append(back_ref[source, :, column : column + span])
                    rows.append(pieces[0] if len(pieces) == 1 else jnp.concatenate(pieces, axis=1))
            natural = jnp.concatenate(rows, axis=0)
            mixed = lax.dot_general(
                natural, order, (((1,), (1,)), ((), ())), preferred_element_type=jnp.float32
            )
            half_rows = half_modes * slab_rows
            real = mixed[:half_rows]
            imag = mixed[half_rows:]
            for parity in range(2):
                lanes = slice(parity * 128, (parity + 1) * 128)
                first = slice(block * 128, (block + 1) * 128)
                second = slice(PAIR + block * 128, PAIR + (block + 1) * 128)
                left[parity, 0:half_rows, first] = real[:, lanes].astype(jnp.bfloat16)
                left[parity, 0:half_rows, second] = (-imag[:, lanes]).astype(jnp.bfloat16)
                left[parity, half_rows:, first] = imag[:, lanes].astype(jnp.bfloat16)
                left[parity, half_rows:, second] = real[:, lanes].astype(jnp.bfloat16)
        even = dot32(left[0], table_ref[0])
        odd = dot32(left[1], table_ref[1])
        for side in range(2):
            plane = (even + odd if side == 0 else even - odd).astype(jnp.bfloat16)
            whole = plane.astype(jnp.float32)
            for mode in range(half_modes):
                for part in range(2):
                    row = (part * half_modes + mode) * slab_rows
                    planes_ref[component, mode, part, :, side * HALF : (side + 1) * HALF] = plane[
                        row : row + slab_rows
                    ]
            for strip in range(HALF // 128):
                values[
                    side * (HALF // 128) + strip,
                    component * component_rows : (component + 1) * component_rows,
                    :,
                ] = whole[:, strip * 128 : (strip + 1) * 128]

    def tile_step(tile, carry):
        block = block_ref[tile]
        strip = block % strips
        y = block // strips
        cell = jnp.broadcast_to(cell_ref[pl.ds(tile, 1), :], (group_rows, size))
        spot = cell % 128
        upper = cell >= 128
        first_row = pl.ds(pl.multiple_of(tile * group_rows, 8), group_rows)
        for component in range(3):
            rows = pl.ds(component * component_rows + y, group_rows, stride=slab_rows)
            left_half = values[strip * 2, rows, :]
            right_half = values[strip * 2 + 1, rows, :]
            pieces = []
            for piece in range(size // 128):
                lanes = slice(piece * 128, (piece + 1) * 128)
                low = jnp.take_along_axis(left_half, spot[:, lanes], axis=1)
                high = jnp.take_along_axis(right_half, spot[:, lanes], axis=1)
                picked = jnp.where(upper[:, lanes], high, low)
                pieces.append(
                    jnp.sum(picked * phase_ref[piece, first_row, :], axis=0, keepdims=True)
                )
            sampled[component, pl.ds(tile, 1), :] = jnp.concatenate(pieces, axis=1)
        return carry

    lax.fori_loop(0, tiles, tile_step, 0, unroll=2)
    part_ref[...] = sampled[...].astype(jnp.bfloat16)


def on_device(
    cell_index,
    block_index,
    volume,
    response_rate,
    spanwise_position,
    particle_velocity,
    seen_velocity,
    fluid_velocity,
    eigen_basis,
    eigen_inverse,
    eigenvalues,
):
    group_index = lax.axis_index("grp")
    px_count = lax.axis_size("px")
    pz_count = lax.axis_size("pz")
    rows = fluid_velocity.shape[0]
    pencil_modes = fluid_velocity.shape[2]
    pencil_waves = fluid_velocity.shape[4]
    half_modes = pencil_modes * pz_count
    slabs = px_count * pz_count
    slab_rows = rows // slabs
    strips = NX // CB
    tiles, size = cell_index.shape
    width = 6 * half_modes
    columns = 6 * pencil_modes * pencil_waves
    sizes = dict(half_modes=half_modes, pencil_modes=pencil_modes, pencil_waves=pencil_waves)

    vmem = pl.BlockSpec(memory_space=pltpu.VMEM)
    smem = pl.BlockSpec(memory_space=pltpu.SMEM)
    order = jnp.asarray(order_matrix(), jnp.bfloat16)

    outgoing, phases = pl.pallas_call(
        functools.partial(spread_kernel, **sizes),
        out_shape=(
            jax.ShapeDtypeStruct((slabs, slab_rows, columns), jnp.bfloat16),
            jax.ShapeDtypeStruct((size // 128, tiles * 2 * half_modes, 128), jnp.float32),
        ),
        in_specs=[smem, smem] + [vmem] * 11,
        out_specs=(vmem, vmem),
        scratch_shapes=[
            pltpu.VMEM((NX // 128, slab_rows * width, 128), jnp.float32),
            pltpu.VMEM((HALF, KX), jnp.float32),
            pltpu.VMEM((HALF, KX), jnp.float32),
            pltpu.VMEM((2, NX, PAIR), jnp.bfloat16),
            pltpu.VMEM((2 * half_modes * slab_rows, NX), jnp.bfloat16),
        ],
        name="spread",
    )(
        block_index,
        group_index.reshape(1).astype(jnp.int32),
        cell_index,
        volume,
        response_rate,
        spanwise_position,
        particle_velocity,
        seen_velocity,
        *[jnp.asarray(seed) for seed in forward_seeds()],
        order,
    )
    force = lax.all_to_all(outgoing, ("px", "pz"), split_axis=0, concat_axis=0, tiled=True)
    force = force.reshape(rows, columns)

    def halves(matrix):
        high = lax.reduce_precision(matrix, 8, 7)
        return high.astype(jnp.bfloat16), (matrix - high).astype(jnp.bfloat16)

    inverse_high, inverse_low = halves(eigen_inverse)
    basis_high, basis_low = halves(eigen_basis)
    state = jnp.transpose(fluid_velocity, (0, 1, 2, 3, 4)).reshape(rows, columns)
    square = pl.BlockSpec((rows, rows), lambda i: (0, 0))
    strip_spec = pl.BlockSpec((rows, pencil_waves), lambda i: (0, i))
    steps = columns // pencil_waves
    projected = pl.pallas_call(
        project_kernel,
        grid=(steps,),
        out_shape=jax.ShapeDtypeStruct((rows, columns), jnp.float32),
        in_specs=[square, square, strip_spec],
        out_specs=strip_spec,
        name="project",
    )(inverse_high, inverse_low, state)
    stream_wave = (lax.axis_index("px") * pencil_waves + jnp.arange(pencil_waves) - KX // 2).astype(
        jnp.float32
    ) * 0.5
    span_wave = (
        group_index * half_modes
        + lax.axis_index("pz") * pencil_modes
        + jnp.arange(pencil_modes)
        + 1
    ).astype(jnp.float32)
    wave_square = (
        stream_wave[None, :] * stream_wave[None, :] + span_wave[:, None] * span_wave[:, None]
    ).reshape(1, pencil_modes * pencil_waves)
    damping = 1.0 / (1.0 + viscosity * (eigenvalues[:, None] + wave_square))
    table = pl.pallas_call(
        table_kernel,
        out_shape=jax.ShapeDtypeStruct((2, KX, HALF), jnp.bfloat16),
        in_specs=[vmem] * 4,
        out_specs=vmem,
        scratch_shapes=[pltpu.VMEM((PAIR, HALF), jnp.float32)] * 2,
        name="waves",
    )(*[jnp.asarray(seed) for seed in inverse_seeds()])

    solved = pl.pallas_call(
        solve_kernel,
        grid=(steps,),
        out_shape=jax.ShapeDtypeStruct((rows, columns), jnp.bfloat16),
        in_specs=[
            square,
            square,
            square,
            square,
            pl.BlockSpec((rows, pencil_waves), lambda i: (0, (i // 2) % pencil_modes)),
            strip_spec,
            strip_spec,
        ],
        out_specs=strip_spec,
        name="solve",
    )(inverse_high, inverse_low, basis_high, basis_low, damping, projected, force)
    returned = lax.all_to_all(
        solved.reshape(slabs, slab_rows, columns),
        ("px", "pz"),
        split_axis=0,
        concat_axis=0,
        tiled=True,
    )
    planes, mode_part = pl.pallas_call(
        functools.partial(gather_kernel, **sizes),
        out_shape=(
            jax.ShapeDtypeStruct((3, half_modes, 2, slab_rows, NX), jnp.bfloat16),
            jax.ShapeDtypeStruct((3, tiles, size), jnp.bfloat16),
        ),
        in_specs=[smem] + [vmem] * 5,
        out_specs=(vmem, vmem),
        scratch_shapes=[
            pltpu.VMEM((2, 2 * half_modes * slab_rows, KX), jnp.bfloat16),
            pltpu.VMEM((NX // 128, slab_rows * width, 128), jnp.float32),
            pltpu.VMEM((3, tiles, size), jnp.float32),
        ],
        name="gather",
    )(block_index, cell_index, phases, table, order, returned)
    velocity_planes = jnp.transpose(planes, (3, 0, 1, 2, 4))
    other_part = lax.ppermute(mode_part, "grp", [(0, 1), (1, 0)])
    fluid_at = mode_part.astype(jnp.float32) + other_part.astype(jnp.float32)
    upward = (jnp.arange(3) == 1).astype(jnp.float32)[:, None, None]
    updated_velocity = (
        particle_velocity
        + time_step * response_rate * (fluid_at - particle_velocity)
        - time_step * gravity * upward
    )
    return (velocity_planes, updated_velocity)


def solution(mesh):
    in_specs = (
        P(("px", "pz"), None),
        P(("px", "pz")),
        P(("px", "pz"), None),
        P(("px", "pz"), None),
        P(("px", "pz"), None),
        P(None, ("px", "pz"), None),
        P(None, ("px", "pz"), None),
        P(None, None, ("grp", "pz"), None, "px"),
        P(),
        P(),
        P(),
    )
    out_specs = (P(("px", "pz"), None, "grp", None, None), P(None, ("px", "pz"), None))
    return jax.shard_map(
        on_device, mesh=mesh, in_specs=in_specs, out_specs=out_specs, check_vma=False
    )
```

```python
import functools
import math

import jax
import jax.numpy as jnp
import numpy as np
from jax import lax
from jax.experimental import pallas as pl
from jax.experimental.pallas import tpu as pltpu
from jax.sharding import PartitionSpec as P

NX = 2048
KX = 1024
CB = 256
HALF = NX // 2
PAIR = KX // 2
TILE_GROUP = 8

time_step = 0.5
gravity = 0.8
viscosity = 0.0001


def turns(rows, columns):
    phase = np.mod(np.asarray(rows)[:, None] * np.asarray(columns)[None, :], NX)
    angles = phase.astype(np.float64) * (2.0 * math.pi / NX)
    return np.cos(angles).astype(np.float32), np.sin(angles).astype(np.float32)


def forward_seeds():
    waves = np.concatenate([2 * np.arange(PAIR) - KX // 2, 2 * np.arange(PAIR) + 1 - KX // 2])
    base = turns(np.arange(8), waves)
    steps = turns(8 * 2 ** np.arange(8), waves)
    scale = np.float32(1.0 / math.sqrt(NX))
    return [base[0] * scale, base[1] * scale, steps[0], steps[1]]


def inverse_seeds():
    points = np.arange(HALF)
    bases = [turns(2 * np.arange(8) + parity - KX // 2, points) for parity in range(2)]
    steps = turns(16 * 2 ** np.arange(8), points)
    scale = np.float32(1.0 / math.sqrt(NX))
    cosines = np.stack([b[0] for b in bases]) * scale
    sines = np.stack([b[1] for b in bases]) * scale
    return [cosines, sines, steps[0], steps[1]]


def order_matrix(waves):
    matrix = np.zeros((waves, waves), np.float32)
    lanes = np.arange(waves)
    half = waves // 2
    matrix[2 * (lanes % half) + lanes // half, lanes] = 1.0
    return matrix


def spread_rows(half_modes, slab_rows):
    part, mode, y = np.meshgrid(
        np.arange(2), np.arange(half_modes), np.arange(slab_rows), indexing="ij"
    )
    count = part.size
    matrix = np.zeros((count, count), np.float32)
    source = (y * 2 + part) * half_modes + mode
    matrix[np.arange(count), source.ravel()] = 1.0
    return matrix


def gather_rows(half_modes, slab_rows):
    y, mode, part = np.meshgrid(
        np.arange(slab_rows), np.arange(half_modes), np.arange(2), indexing="ij"
    )
    count = part.size
    matrix = np.zeros((2 * count, count), np.float32)
    source = (part * half_modes + mode) * slab_rows + y
    other = ((1 - part) * half_modes + mode) * slab_rows + y
    matrix[np.arange(count), source.ravel()] = 1.0
    matrix[count + np.arange(count), other.ravel()] = np.where(part.ravel() == 0, -1.0, 1.0)
    return matrix


def grow(cos_ref, sin_ref, base, steps, rows):
    cos_ref[0:8, :] = base[0]
    sin_ref[0:8, :] = base[1]
    done = 8
    level = 0
    while done < rows:
        turn_cos = steps[0][level : level + 1, :]
        turn_sin = steps[1][level : level + 1, :]

        def block(index, carry, done=done, turn_cos=turn_cos, turn_sin=turn_sin):
            start = pl.multiple_of(index * 8, 8)
            old_cos = cos_ref[pl.ds(start, 8), :]
            old_sin = sin_ref[pl.ds(start, 8), :]
            cos_ref[pl.ds(done + start, 8), :] = old_cos * turn_cos - old_sin * turn_sin
            sin_ref[pl.ds(done + start, 8), :] = old_sin * turn_cos + old_cos * turn_sin
            return carry

        lax.fori_loop(0, done // 8, block, 0)
        done *= 2
        level += 1


def dot32(a, b):
    return jnp.dot(a, b, preferred_element_type=jnp.float32)


def spread_kernel(
    block_ref,
    group_ref,
    cell_ref,
    volume_ref,
    rate_ref,
    place_ref,
    motion_ref,
    seen_ref,
    base_cos_ref,
    base_sin_ref,
    step_cos_ref,
    step_sin_ref,
    order_ref,
    out_ref,
    phase_out_ref,
    field,
    table_cos,
    table_sin,
    table,
    left,
    amounts,
    phases,
    phases_out,
    packed,
    phase_sem,
    out_sem,
    *,
    half_modes,
    pencil_modes,
    pencil_waves,
):
    tiles, size = cell_ref.shape
    strips = NX // CB
    group_rows = 2 * half_modes
    slab_rows = field.shape[1] // (3 * group_rows)
    component_rows = slab_rows * group_rows
    pz_count = half_modes // pencil_modes

    place = place_ref[...]
    first = (group_ref[0] * half_modes + 1).astype(jnp.float32)
    cos_one = jnp.cos(place)
    sin_one = jnp.sin(place)
    cos_now = jnp.cos(place * first)
    sin_now = jnp.sin(place * first)
    for mode in range(half_modes):
        for piece in range(size // 128):
            lanes = slice(piece * 128, (piece + 1) * 128)
            for part, value in ((0, cos_now[:, lanes]), (1, -sin_now[:, lanes])):
                phases[piece, pl.ds(part * half_modes + mode, tiles, stride=group_rows), :] = value
                phases_out[piece, pl.ds(2 * mode + part, tiles, stride=group_rows), :] = value
        if mode + 1 < half_modes:
            cos_now, sin_now = (
                cos_now * cos_one - sin_now * sin_one,
                sin_now * cos_one + cos_now * sin_one,
            )
    phase_copy = pltpu.make_async_copy(phases_out, phase_out_ref, phase_sem)
    phase_copy.start()

    upper = cell_ref[...] >= 128
    volume = volume_ref[...]
    pull = volume * rate_ref[...]
    for component in range(3):
        amount = pull * (seen_ref[component] - motion_ref[component])
        if component == 1:
            amount = amount - gravity * volume
        amounts[component] = jnp.where(upper, 0.0, amount)
        amounts[3 + component] = jnp.where(upper, amount, 0.0)

    grow(
        table_cos,
        table_sin,
        (base_cos_ref[...], base_sin_ref[...]),
        (step_cos_ref, step_sin_ref),
        HALF,
    )
    for parity in range(2):
        lanes = slice(parity * PAIR, (parity + 1) * PAIR)
        table[parity, :, 0:PAIR] = table_cos[:, lanes].astype(jnp.bfloat16)
        table[parity, :, PAIR:KX] = table_sin[:, lanes].astype(jnp.bfloat16)

    def clear(index, carry):
        field[index] = jnp.zeros(field.shape[1:], jnp.float32)
        return carry

    lax.fori_loop(0, field.shape[0], clear, 0)

    cells = lax.broadcasted_iota(jnp.int32, (128, size), 0)

    def tile_group(group, carry):
        shares = []
        for offset in range(TILE_GROUP):
            tile = group * TILE_GROUP + offset
            row = pl.ds(tile, 1)
            rows_of_tile = pl.ds(pl.multiple_of(tile * group_rows, 8), group_rows)
            phase = jnp.concatenate(
                [phases[piece, rows_of_tile, :] for piece in range(size // 128)], axis=1
            )
            payload = jnp.concatenate([amounts[k, row, :] * phase for k in range(6)], axis=0)
            spot = cell_ref[row, :] % 128
            one_hot = (spot == cells).astype(jnp.float32).astype(jnp.bfloat16)
            shares.append(
                lax.dot_general(
                    payload.astype(jnp.bfloat16),
                    one_hot,
                    (((1,), (1,)), ((), ())),
                    preferred_element_type=jnp.float32,
                )
            )
        for offset in range(TILE_GROUP):
            block = block_ref[group * TILE_GROUP + offset]
            strip = block % strips
            y = block // strips
            for half in range(2):
                for component in range(3):
                    start = pl.multiple_of(component * component_rows + y * group_rows, 8)
                    own = (half * 3 + component) * group_rows
                    field[strip * 2 + half, pl.ds(start, group_rows), :] += shares[offset][
                        own : own + group_rows
                    ]
        return carry

    lax.fori_loop(0, tiles // TILE_GROUP, tile_group, 0)

    order = order_ref[...]
    part_sign = jnp.where(
        lax.broadcasted_iota(jnp.int32, (slab_rows, group_rows, PAIR), 1) < half_modes, 1.0, -1.0
    )
    half_waves = pencil_waves // 2
    copies = []
    for component in range(3):
        rows = slice(component * component_rows, (component + 1) * component_rows)
        for strip in range(HALF // 128):
            low = field[strip, rows, :]
            high = field[strip + HALF // 128, rows, :]
            lanes = slice(strip * 128, (strip + 1) * 128)
            left[0, :, lanes] = (low + high).astype(jnp.bfloat16)
            left[1, :, lanes] = (low - high).astype(jnp.bfloat16)
        for parity in range(2):
            product = dot32(left[parity], table[parity])
            turned = product[:, PAIR:].reshape(slab_rows, group_rows, PAIR)
            turned = pltpu.roll(turned, half_modes, 1) * part_sign
            spectrum = (product[:, :PAIR] + turned.reshape(component_rows, PAIR)).astype(
                jnp.bfloat16
            )
            spectrum = dot32(order, spectrum).astype(jnp.bfloat16)
            for owner_px in range(KX // pencil_waves):
                for part in range(2):
                    for mode in range(half_modes):
                        column = (
                            (component * pencil_modes + mode % pencil_modes) * 2 + part
                        ) * pencil_waves + parity * half_waves
                        row = (part * half_modes + mode) * slab_rows
                        packed[
                            owner_px * pz_count + mode // pencil_modes,
                            :,
                            column : column + half_waves,
                        ] = spectrum[
                            row : row + slab_rows,
                            owner_px * half_waves : (owner_px + 1) * half_waves,
                        ]
        span = 2 * pencil_modes * pencil_waves
        lanes = pl.ds(component * span, span)
        copy = pltpu.make_async_copy(
            packed.at[:, :, lanes], out_ref.at[:, :, lanes], out_sem.at[component]
        )
        copy.start()
        copies.append(copy)
    for copy in copies:
        copy.wait()
    phase_copy.wait()


def table_kernel(base_cos_ref, base_sin_ref, step_cos_ref, step_sin_ref, out_ref, work_cos, work_sin):
    for parity in range(2):
        grow(
            work_cos,
            work_sin,
            (base_cos_ref[parity], base_sin_ref[parity]),
            (step_cos_ref, step_sin_ref),
            PAIR,
        )
        out_ref[parity, 0:PAIR, :] = work_cos[...].astype(jnp.bfloat16)
        out_ref[parity, PAIR:KX, :] = work_sin[...].astype(jnp.bfloat16)


def split(value):
    high = value.astype(jnp.bfloat16)
    return high, (value - high.astype(jnp.float32)).astype(jnp.bfloat16)


def project_kernel(high_ref, low_ref, order_ref, state_ref, out_ref):
    order = order_ref[...]
    state_high, state_low = [
        dot32(value, order).astype(jnp.bfloat16) for value in split(state_ref[...])
    ]
    out_ref[...] = (
        dot32(high_ref[...], state_high)
        + dot32(high_ref[...], state_low)
        + dot32(low_ref[...], state_high)
    )


def solve_kernel(
    inverse_high_ref,
    inverse_low_ref,
    basis_high_ref,
    basis_low_ref,
    damping_ref,
    state_ref,
    force_ref,
    out_ref,
    matrices,
    damping,
    state,
    sems,
):
    rows, step = damping_ref.shape
    columns = force_ref.shape[-1]
    force_rows = force_ref[...].reshape(rows, columns)
    slab_shape = out_ref.shape[:2]
    spans = [pl.ds(start, step) for start in range(0, columns, step)]
    loads = [
        (inverse_high_ref, matrices.at[0]),
        (inverse_low_ref, matrices.at[1]),
        (state_ref.at[:, spans[0]], state.at[:, spans[0]]),
        (damping_ref, damping),
        (basis_high_ref, matrices.at[2]),
        (basis_low_ref, matrices.at[3]),
    ] + [(state_ref.at[:, span], state.at[:, span]) for span in spans[1:]]
    copies = [
        pltpu.make_async_copy(source, target, sems.at[index])
        for index, (source, target) in enumerate(loads)
    ]
    for copy in copies:
        copy.start()
    for index, start in enumerate(range(0, columns, step)):
        lanes = slice(start, start + step)
        force = force_rows[:, lanes]
        if index == 0:
            copies[0].wait()
            copies[1].wait()
        pushed = dot32(matrices[0], force) + dot32(matrices[1], force)
        copies[2 if index == 0 else 5 + index].wait()
        if index == 0:
            copies[3].wait()
        modal = (state[:, lanes] + time_step * pushed) * damping[...]
        modal_high, modal_low = split(modal)
        if index == 0:
            copies[4].wait()
            copies[5].wait()
        solved = (
            dot32(matrices[2], modal_high)
            + dot32(matrices[2], modal_low)
            + dot32(matrices[3], modal_high)
        )
        out_ref[:, :, lanes] = solved.astype(jnp.bfloat16).reshape(slab_shape + (step,))


def merge_rows(values):
    sublane = lax.broadcasted_iota(jnp.int32, (8, 128), 0)
    for bit in (4, 2, 1):
        keep = (sublane & bit) == 0
        half = len(values) // 2
        merged = []
        for index in range(half):
            a, b = values[index], values[index + half]
            own = jnp.where(keep, a, b)
            other = jnp.where(keep, b, a)
            if bit == 4:
                moved = pltpu.roll(other, 4, 0)
            else:
                moved = jnp.where(
                    keep, pltpu.roll(other, 8 - bit, 0), pltpu.roll(other, bit, 0)
                )
            merged.append(own + moved)
        values = merged
    return values[0]


def gather_kernel(
    block_ref,
    cell_ref,
    order_ref,
    table_ref,
    back_ref,
    phase_ref,
    planes_ref,
    part_ref,
    left,
    values,
    planes,
    sampled,
    phases,
    table,
    table_sem,
    phase_sem,
    plane_sem,
    *,
    half_modes,
    pencil_modes,
    pencil_waves,
):
    tiles, size = cell_ref.shape
    strips = NX // CB
    group_rows = 2 * half_modes
    slab_rows = back_ref.shape[1]
    pz_count = half_modes // pencil_modes
    half_waves = pencil_waves // 2
    component_rows = group_rows * slab_rows
    table_copies = [
        pltpu.make_async_copy(table_ref.at[parity], table.at[parity], table_sem.at[parity])
        for parity in range(2)
    ]
    for copy in table_copies:
        copy.start()
    phase_copy = pltpu.make_async_copy(phase_ref, phases, phase_sem)
    phase_copy.start()
    copies = []
    for component in range(3):
        rows = []
        for part in range(2):
            for mode in range(half_modes):
                column = (
                    (component * pencil_modes + mode % pencil_modes) * 2 + part
                ) * pencil_waves
                pieces = []
                for parity in range(2):
                    for px in range(KX // pencil_waves):
                        first = column + parity * half_waves
                        pieces.append(
                            back_ref[
                                px * pz_count + mode // pencil_modes,
                                :,
                                first : first + half_waves,
                            ]
                        )
                rows.append(jnp.concatenate(pieces, axis=1))
        turned = dot32(order_ref[...], jnp.concatenate(rows, axis=0)).astype(jnp.bfloat16)
        for parity in range(2):
            lanes = slice(parity * PAIR, (parity + 1) * PAIR)
            left[parity, :, 0:PAIR] = turned[0:component_rows, lanes]
            left[parity, :, PAIR:KX] = turned[component_rows:, lanes]
        if component == 0:
            table_copies[0].wait()
        even = dot32(left[0], table[0])
        if component == 0:
            table_copies[1].wait()
        odd = dot32(left[1], table[1])
        for side in range(2):
            plane = (even + odd if side == 0 else even - odd).astype(jnp.bfloat16)
            whole = plane.astype(jnp.float32)
            planes[:, component, :, :, side * HALF : (side + 1) * HALF] = plane.reshape(
                slab_rows, half_modes, 2, HALF
            )
            for strip in range(HALF // 128):
                values[
                    side * (HALF // 128) + strip,
                    component * component_rows : (component + 1) * component_rows,
                    :,
                ] = whole[:, strip * 128 : (strip + 1) * 128]
        copy = pltpu.make_async_copy(
            planes.at[:, component], planes_ref.at[:, component], plane_sem.at[component]
        )
        copy.start()
        copies.append(copy)
    phase_copy.wait()

    def tile_group(group, carry):
        first_tile = pl.multiple_of(group * 8, 8)
        places = []
        for offset in range(8):
            block = block_ref[first_tile + offset]
            places.append((block % strips, block // strips))
        cells = cell_ref[pl.ds(first_tile, 8), :]
        for piece in range(size // 128):
            lanes = slice(piece * 128, (piece + 1) * 128)
            weighted = [[], [], []]
            for offset in range(8):
                strip, y = places[offset]
                cell = jnp.broadcast_to(cells[offset : offset + 1, lanes], (group_rows, 128))
                spot = cell % 128
                upper = cell >= 128
                rows_of_tile = pl.multiple_of((first_tile + offset) * group_rows, 8)
                phase = phases[piece, pl.ds(rows_of_tile, group_rows), :]
                for component in range(3):
                    start = pl.multiple_of(component * component_rows + y * group_rows, 8)
                    rows = pl.ds(start, group_rows)
                    low = jnp.take_along_axis(values[strip * 2, rows, :], spot, axis=1)
                    high = jnp.take_along_axis(values[strip * 2 + 1, rows, :], spot, axis=1)
                    product = jnp.where(upper, high, low) * phase
                    total = product[0:8]
                    for more in range(8, group_rows, 8):
                        total = total + product[more : more + 8]
                    weighted[component].append(total)
            for component in range(3):
                sampled[component, pl.ds(first_tile, 8), lanes] = merge_rows(weighted[component])
        return carry

    lax.fori_loop(0, tiles // 8, tile_group, 0)
    part_ref[...] = sampled[...].astype(jnp.bfloat16)
    for copy in copies:
        copy.wait()


def on_device(
    cell_index,
    block_index,
    volume,
    response_rate,
    spanwise_position,
    particle_velocity,
    seen_velocity,
    fluid_velocity,
    eigen_basis,
    eigen_inverse,
    eigenvalues,
):
    group_index = lax.axis_index("grp")
    px_count = lax.axis_size("px")
    pz_count = lax.axis_size("pz")
    rows = fluid_velocity.shape[0]
    pencil_modes = fluid_velocity.shape[2]
    pencil_waves = fluid_velocity.shape[4]
    half_modes = pencil_modes * pz_count
    slabs = px_count * pz_count
    slab_rows = rows // slabs
    strips = NX // CB
    tiles, size = cell_index.shape
    width = 6 * half_modes
    component_rows = 2 * half_modes * slab_rows
    columns = 6 * pencil_modes * pencil_waves
    pencil = pencil_modes * pencil_waves
    sizes = dict(half_modes=half_modes, pencil_modes=pencil_modes, pencil_waves=pencil_waves)

    vmem = pl.BlockSpec(memory_space=pltpu.VMEM)
    smem = pl.BlockSpec(memory_space=pltpu.SMEM)
    hbm = pl.BlockSpec(memory_space=pltpu.HBM)
    in_hbm = functools.partial(pltpu.with_memory_space_constraint, memory_space=pltpu.HBM)
    phase_shape = (size // 128, tiles * 2 * half_modes, 128)

    outgoing, phases = pl.pallas_call(
        functools.partial(spread_kernel, **sizes),
        out_shape=(
            jax.ShapeDtypeStruct((slabs, slab_rows, columns), jnp.bfloat16),
            jax.ShapeDtypeStruct(phase_shape, jnp.float32),
        ),
        in_specs=[smem, smem] + [vmem] * 11,
        out_specs=(hbm, hbm),
        scratch_shapes=[
            pltpu.VMEM((NX // 128, slab_rows * width, 128), jnp.float32),
            pltpu.VMEM((HALF, KX), jnp.float32),
            pltpu.VMEM((HALF, KX), jnp.float32),
            pltpu.VMEM((2, HALF, KX), jnp.bfloat16),
            pltpu.VMEM((2, component_rows, HALF), jnp.bfloat16),
            pltpu.VMEM((6, tiles, size), jnp.float32),
            pltpu.VMEM(phase_shape, jnp.float32),
            pltpu.VMEM(phase_shape, jnp.float32),
            pltpu.VMEM((slabs, slab_rows, columns), jnp.bfloat16),
            pltpu.SemaphoreType.DMA,
            pltpu.SemaphoreType.DMA((3,)),
        ],
        name="spread",
    )(
        block_index,
        group_index.reshape(1).astype(jnp.int32),
        cell_index,
        volume,
        response_rate,
        spanwise_position,
        particle_velocity,
        seen_velocity,
        *[jnp.asarray(seed) for seed in forward_seeds()],
        jnp.asarray(spread_rows(half_modes, slab_rows), jnp.bfloat16),
    )
    force = lax.all_to_all(outgoing, ("px", "pz"), split_axis=0, concat_axis=0, tiled=True)

    def halves(matrix):
        high = lax.reduce_precision(matrix, 8, 7)
        return high.astype(jnp.bfloat16), (matrix - high).astype(jnp.bfloat16)

    inverse_high, inverse_low = halves(eigen_inverse)
    basis_high, basis_low = halves(eigen_basis)
    state = fluid_velocity.transpose(0, 1, 2, 3, 4).reshape(rows, columns)
    square = pl.BlockSpec((rows, rows), lambda i: (0, 0))
    strip_spec = pl.BlockSpec((rows, pencil_waves), lambda i: (0, i))
    projected = pl.pallas_call(
        project_kernel,
        grid=(columns // pencil_waves,),
        out_shape=jax.ShapeDtypeStruct((rows, columns), jnp.float32),
        in_specs=[
            square,
            square,
            pl.BlockSpec((pencil_waves, pencil_waves), lambda i: (0, 0)),
            strip_spec,
        ],
        out_specs=strip_spec,
        compiler_params=pltpu.CompilerParams(vmem_limit_bytes=24 << 20),
        name="project",
    )(inverse_high, inverse_low, jnp.asarray(order_matrix(pencil_waves), jnp.bfloat16), state)
    lane = jnp.arange(pencil_waves)
    half_waves = pencil_waves // 2
    wave = 2 * (lane % half_waves) + lane // half_waves
    stream_wave = (lax.axis_index("px") * pencil_waves + wave - KX // 2).astype(jnp.float32) * 0.5
    span_wave = (
        group_index * half_modes
        + lax.axis_index("pz") * pencil_modes
        + jnp.arange(pencil_modes)
        + 1
    ).astype(jnp.float32)
    wave_square = (
        stream_wave[None, :] * stream_wave[None, :] + span_wave[:, None] * span_wave[:, None]
    )
    wave_square = jnp.broadcast_to(wave_square[:, None, :], (pencil_modes, 2, pencil_waves))
    damping = 1.0 / (
        1.0 + viscosity * (eigenvalues[:, None] + wave_square.reshape(1, 2 * pencil))
    )
    table = pl.pallas_call(
        table_kernel,
        out_shape=jax.ShapeDtypeStruct((2, KX, HALF), jnp.bfloat16),
        in_specs=[vmem] * 4,
        out_specs=vmem,
        scratch_shapes=[pltpu.VMEM((PAIR, HALF), jnp.float32)] * 2,
        compiler_params=pltpu.CompilerParams(vmem_limit_bytes=24 << 20),
        name="waves",
    )(*[jnp.asarray(seed) for seed in inverse_seeds()])

    solved = pl.pallas_call(
        solve_kernel,
        out_shape=jax.ShapeDtypeStruct((slabs, slab_rows, columns), jnp.bfloat16),
        in_specs=[hbm] * 6 + [vmem],
        out_specs=vmem,
        scratch_shapes=[
            pltpu.VMEM((4, rows, rows), jnp.bfloat16),
            pltpu.VMEM((rows, 2 * pencil), jnp.float32),
            pltpu.VMEM((rows, columns), jnp.float32),
            pltpu.SemaphoreType.DMA((8,)),
        ],
        compiler_params=pltpu.CompilerParams(vmem_limit_bytes=32 << 20),
        name="solve",
    )(
        in_hbm(inverse_high),
        in_hbm(inverse_low),
        in_hbm(basis_high),
        in_hbm(basis_low),
        in_hbm(damping),
        in_hbm(projected),
        force,
    )
    returned = lax.all_to_all(solved, ("px", "pz"), split_axis=0, concat_axis=0, tiled=True)
    velocity_planes, mode_part = pl.pallas_call(
        functools.partial(gather_kernel, **sizes),
        out_shape=(
            jax.ShapeDtypeStruct((slab_rows, 3, half_modes, 2, NX), jnp.bfloat16),
            jax.ShapeDtypeStruct((3, tiles, size), jnp.bfloat16),
        ),
        in_specs=[smem, vmem, vmem, hbm, vmem, hbm],
        out_specs=(hbm, vmem),
        scratch_shapes=[
            pltpu.VMEM((2, component_rows, KX), jnp.bfloat16),
            pltpu.VMEM((NX // 128, slab_rows * width, 128), jnp.float32),
            pltpu.VMEM((slab_rows, 3, half_modes, 2, NX), jnp.bfloat16),
            pltpu.VMEM((3, tiles, size), jnp.float32),
            pltpu.VMEM(phase_shape, jnp.float32),
            pltpu.VMEM((2, KX, HALF), jnp.bfloat16),
            pltpu.SemaphoreType.DMA((2,)),
            pltpu.SemaphoreType.DMA,
            pltpu.SemaphoreType.DMA((3,)),
        ],
        compiler_params=pltpu.CompilerParams(vmem_limit_bytes=40 << 20),
        name="gather",
    )(
        block_index,
        cell_index,
        jnp.asarray(gather_rows(half_modes, slab_rows), jnp.bfloat16),
        in_hbm(table),
        returned,
        in_hbm(phases),
    )
    other_part = lax.ppermute(mode_part, "grp", [(0, 1), (1, 0)])
    fluid_at = mode_part.astype(jnp.float32) + other_part.astype(jnp.float32)
    upward = (jnp.arange(3) == 1).astype(jnp.float32)[:, None, None]
    updated_velocity = (
        particle_velocity
        + time_step * response_rate * (fluid_at - particle_velocity)
        - time_step * gravity * upward
    )
    return (velocity_planes, updated_velocity)


def solution(mesh):
    in_specs = (
        P(("px", "pz"), None),
        P(("px", "pz")),
        P(("px", "pz"), None),
        P(("px", "pz"), None),
        P(("px", "pz"), None),
        P(None, ("px", "pz"), None),
        P(None, ("px", "pz"), None),
        P(None, None, ("grp", "pz"), None, "px"),
        P(),
        P(),
        P(),
    )
    out_specs = (P(("px", "pz"), None, "grp", None, None), P(None, ("px", "pz"), None))
    return jax.shard_map(
        on_device, mesh=mesh, in_specs=in_specs, out_specs=out_specs, check_vma=False
    )
```

```python
import functools
import math

import jax
import jax.numpy as jnp
import numpy as np
from jax import lax
from jax.experimental import pallas as pl
from jax.experimental.pallas import tpu as pltpu
from jax.sharding import PartitionSpec as P


NX = 2048
KX = 1024
CB = 256
HALF = NX // 2
PAIR = KX // 2
TILE_GROUP = 8

time_step = 0.5
gravity = 0.8
viscosity = 0.0001


def turns(rows, columns):
    phase = np.mod(np.asarray(rows)[:, None] * np.asarray(columns)[None, :], NX)
    angles = phase.astype(np.float64) * (2.0 * math.pi / NX)
    return np.cos(angles).astype(np.float32), np.sin(angles).astype(np.float32)


def forward_seeds():
    waves = np.concatenate([2 * np.arange(PAIR) - KX // 2, 2 * np.arange(PAIR) + 1 - KX // 2])
    base = turns(np.arange(8), waves)
    steps = turns(8 * 2 ** np.arange(8), waves)
    scale = np.float32(1.0 / math.sqrt(NX))
    return [base[0] * scale, base[1] * scale, steps[0], steps[1]]


def inverse_seeds():
    points = np.arange(HALF)
    bases = [turns(2 * np.arange(8) + parity - KX // 2, points) for parity in range(2)]
    steps = turns(16 * 2 ** np.arange(8), points)
    scale = np.float32(1.0 / math.sqrt(NX))
    cosines = np.stack([b[0] for b in bases]) * scale
    sines = np.stack([b[1] for b in bases]) * scale
    return [cosines, sines, steps[0], steps[1]]


def order_matrix(waves):
    matrix = np.zeros((waves, waves), np.float32)
    lanes = np.arange(waves)
    half = waves // 2
    matrix[2 * (lanes % half) + lanes // half, lanes] = 1.0
    return matrix


def spread_rows(modes, slab_rows, width):
    component, part, mode, y = np.meshgrid(
        np.arange(3), np.arange(2), np.arange(modes), np.arange(slab_rows), indexing="ij"
    )
    matrix = np.zeros((part.size, slab_rows * width), np.float32)
    source = y * width + (component * 2 + part) * modes + mode
    matrix[np.arange(part.size), source.ravel()] = 1.0
    return matrix


def gather_rows(half_modes, slab_rows):
    y, mode, part = np.meshgrid(
        np.arange(slab_rows), np.arange(half_modes), np.arange(2), indexing="ij"
    )
    count = part.size
    matrix = np.zeros((2 * count, count), np.float32)
    source = (part * half_modes + mode) * slab_rows + y
    other = ((1 - part) * half_modes + mode) * slab_rows + y
    matrix[np.arange(count), source.ravel()] = 1.0
    matrix[count + np.arange(count), other.ravel()] = np.where(part.ravel() == 0, -1.0, 1.0)
    return matrix


def grow(cos_ref, sin_ref, base, steps, rows):
    cos_ref[0:8, :] = base[0]
    sin_ref[0:8, :] = base[1]
    done = 8
    level = 0
    while done < rows:
        turn_cos = steps[0][level : level + 1, :]
        turn_sin = steps[1][level : level + 1, :]

        def block(index, carry, done=done, turn_cos=turn_cos, turn_sin=turn_sin):
            start = pl.multiple_of(index * 8, 8)
            old_cos = cos_ref[pl.ds(start, 8), :]
            old_sin = sin_ref[pl.ds(start, 8), :]
            cos_ref[pl.ds(done + start, 8), :] = old_cos * turn_cos - old_sin * turn_sin
            sin_ref[pl.ds(done + start, 8), :] = old_sin * turn_cos + old_cos * turn_sin
            return carry

        lax.fori_loop(0, done // 8, block, 0)
        done *= 2
        level += 1


def dot32(a, b):
    return jnp.dot(a, b, preferred_element_type=jnp.float32)


def pack_kernel(cell_ref, volume_ref, rate_ref, place_ref, motion_ref, seen_ref, out_ref):
    out_ref[0] = cell_ref[...].astype(jnp.float32).astype(jnp.bfloat16)
    volume = volume_ref[...]
    pull = volume * rate_ref[...]
    for component in range(3):
        amount = pull * (seen_ref[component] - motion_ref[component])
        if component == 1:
            amount = amount - gravity * volume
        out_ref[1 + component] = amount.astype(jnp.bfloat16)
    out_ref[4], out_ref[5] = split(place_ref[...])


def turn_modes(place, first, modes):
    cos_one = jnp.cos(place)
    sin_one = jnp.sin(place)
    cos_now = jnp.cos(place * first)
    sin_now = jnp.sin(place * first)
    turned = [(cos_now, sin_now)]
    for _ in range(modes - 1):
        cos_now, sin_now = (
            cos_now * cos_one - sin_now * sin_one,
            sin_now * cos_one + cos_now * sin_one,
        )
        turned.append((cos_now, sin_now))
    return turned


def phase_kernel(first_ref, place_ref, out_ref, *, half_modes):
    tiles, size = place_ref.shape
    first = first_ref[0].astype(jnp.float32)
    for mode, (cosine, sine) in enumerate(turn_modes(place_ref[...], first, half_modes)):
        for piece in range(size // 128):
            lanes = slice(piece * 128, (piece + 1) * 128)
            for part, value in ((0, cosine), (1, -sine)):
                rows = pl.ds(2 * mode + part, tiles, stride=2 * half_modes)
                out_ref[piece, rows, :] = value[:, lanes]


def spread_kernel(*refs, modes, pencil_modes, pencil_waves, slab_rows, width, makes_table):
    if makes_table:
        block_ref, first_ref, pack_ref, order_ref = refs[:4]
        base_cos_ref, base_sin_ref, step_cos_ref, step_sin_ref, out_ref, table_out_ref = refs[4:10]
        field, left, amounts, spots, phases, table, table_sem, table_cos, table_sin = refs[10:]
    else:
        block_ref, first_ref, pack_ref, order_ref, table_in_ref, out_ref = refs[:6]
        field, left, amounts, spots, phases, table, table_sem = refs[6:]
    _, tiles, size = pack_ref.shape
    strips = NX // CB
    count = 2 * modes
    zl_count = modes // pencil_modes
    half_waves = pencil_waves // 2

    if makes_table:
        grow(
            table_cos,
            table_sin,
            (base_cos_ref[...], base_sin_ref[...]),
            (step_cos_ref, step_sin_ref),
            HALF,
        )
        for parity in range(2):
            lanes = slice(parity * PAIR, (parity + 1) * PAIR)
            table[parity, :, 0:PAIR] = table_cos[:, lanes].astype(jnp.bfloat16)
            table[parity, :, PAIR:KX] = table_sin[:, lanes].astype(jnp.bfloat16)
        table_copy = pltpu.make_async_copy(table, table_out_ref, table_sem)
    else:
        table_copy = pltpu.make_async_copy(table_in_ref, table, table_sem)
    table_copy.start()

    def clear(index, carry):
        field[index] = jnp.zeros(field.shape[1:], jnp.float32)
        return carry

    lax.fori_loop(0, field.shape[0], clear, 0)

    place = pack_ref[4].astype(jnp.float32) + pack_ref[5].astype(jnp.float32)
    first = first_ref[0].astype(jnp.float32)
    for mode, (cosine, sine) in enumerate(turn_modes(place, first, modes)):
        for piece in range(size // 128):
            lanes = slice(piece * 128, (piece + 1) * 128)
            for part, value in ((0, cosine), (1, -sine)):
                for component in range(width // count):
                    row = component * count + part * modes + mode
                    phases[piece, pl.ds(row, tiles, stride=width), :] = value[:, lanes]
    cell = pack_ref[0].astype(jnp.float32).astype(jnp.int32)
    spots[...] = cell % 128
    upper = cell >= 128
    for component in range(3):
        amount = pack_ref[1 + component].astype(jnp.float32)
        amounts[component] = jnp.where(upper, 0.0, amount)
        amounts[3 + component] = jnp.where(upper, amount, 0.0)

    cells = lax.broadcasted_iota(jnp.int32, (128, size), 0)
    row_component = lax.broadcasted_iota(jnp.int32, (width, size), 0) // count

    def tile_group(group, carry):
        shares = []
        for offset in range(TILE_GROUP):
            tile = group * TILE_GROUP + offset
            row = pl.ds(tile, 1)
            rows_of_tile = pl.ds(pl.multiple_of(tile * width, 8), width)
            phase = jnp.concatenate(
                [phases[piece, rows_of_tile, :] for piece in range(size // 128)], axis=1
            )
            payload = []
            for half in range(2):
                spread = jnp.where(
                    row_component == 0,
                    amounts[3 * half, row, :],
                    jnp.where(
                        row_component == 1,
                        amounts[3 * half + 1, row, :],
                        jnp.where(row_component == 2, amounts[3 * half + 2, row, :], 0.0),
                    ),
                )
                payload.append(spread * phase)
            payload = jnp.concatenate(payload, axis=0).astype(jnp.bfloat16)
            one_hot = (spots[row, :] == cells).astype(jnp.float32).astype(jnp.bfloat16)
            shares.append(
                lax.dot_general(
                    payload,
                    one_hot,
                    (((1,), (1,)), ((), ())),
                    preferred_element_type=jnp.float32,
                )
            )
        for offset in range(TILE_GROUP):
            block = block_ref[group * TILE_GROUP + offset]
            strip = block % strips
            start = pl.multiple_of((block // strips) * width, 8)
            for half in range(2):
                field[strip * 2 + half, pl.ds(start, width), :] += shares[offset][
                    half * width : (half + 1) * width
                ]
        return carry

    lax.fori_loop(0, tiles // TILE_GROUP, tile_group, 0)

    for strip in range(HALF // 128):
        low = field[strip]
        high = field[strip + HALF // 128]
        lanes = slice(strip * 128, (strip + 1) * 128)
        left[0, :, lanes] = (low + high).astype(jnp.bfloat16)
        left[1, :, lanes] = (low - high).astype(jnp.bfloat16)
    order = order_ref[...]
    sublane = lax.broadcasted_iota(jnp.int32, (slab_rows * width // 8, 8, PAIR), 1)
    is_real = sublane % count < modes
    if not makes_table:
        table_copy.wait()
    for parity in range(2):
        product = dot32(left[parity], table[parity])
        sines = product[:, PAIR:].reshape(slab_rows * width // 8, 8, PAIR)
        turned = jnp.where(is_real, pltpu.roll(sines, 8 - modes, 1), -pltpu.roll(sines, modes, 1))
        spectrum = product[:, :PAIR] + turned.reshape(slab_rows * width, PAIR)
        spectrum = dot32(order, spectrum.astype(jnp.bfloat16)).astype(jnp.bfloat16)
        for owner_px in range(KX // pencil_waves):
            for component in range(3):
                for part in range(2):
                    for mode in range(modes):
                        column = (
                            (component * pencil_modes + mode % pencil_modes) * 2 + part
                        ) * pencil_waves + parity * half_waves
                        row = ((component * 2 + part) * modes + mode) * slab_rows
                        out_ref[
                            owner_px * zl_count + mode // pencil_modes,
                            :,
                            column : column + half_waves,
                        ] = spectrum[
                            row : row + slab_rows,
                            owner_px * half_waves : (owner_px + 1) * half_waves,
                        ]
    if makes_table:
        table_copy.wait()


def table_kernel(base_cos_ref, base_sin_ref, step_cos_ref, step_sin_ref, out_ref, work_cos, work_sin):
    for parity in range(2):
        grow(
            work_cos,
            work_sin,
            (base_cos_ref[parity], base_sin_ref[parity]),
            (step_cos_ref, step_sin_ref),
            PAIR,
        )
        out_ref[parity, 0:PAIR, :] = work_cos[...].astype(jnp.bfloat16)
        out_ref[parity, PAIR:KX, :] = work_sin[...].astype(jnp.bfloat16)


def split(value):
    high = value.astype(jnp.bfloat16)
    return high, (value - high.astype(jnp.float32)).astype(jnp.bfloat16)


def project_kernel(high_ref, low_ref, order_ref, state_ref, out_ref):
    order = order_ref[...]
    state_high, state_low = [
        dot32(value, order).astype(jnp.bfloat16) for value in split(state_ref[...])
    ]
    out_ref[...] = (
        dot32(high_ref[...], state_high)
        + dot32(high_ref[...], state_low)
        + dot32(low_ref[...], state_high)
    )


def solve_kernel(
    inverse_high_ref,
    inverse_low_ref,
    basis_high_ref,
    basis_low_ref,
    damping_ref,
    state_ref,
    own_force_ref,
    other_force_ref,
    out_ref,
    matrices,
    damping,
    state,
    sems,
):
    rows, step = damping_ref.shape
    columns = own_force_ref.shape[-1]
    slab_shape = out_ref.shape[:2]
    spans = [pl.ds(start, step) for start in range(0, columns, step)]
    loads = [
        (inverse_high_ref, matrices.at[0]),
        (inverse_low_ref, matrices.at[1]),
        (state_ref.at[:, spans[0]], state.at[:, spans[0]]),
        (damping_ref, damping),
        (basis_high_ref, matrices.at[2]),
        (basis_low_ref, matrices.at[3]),
    ] + [(state_ref.at[:, span], state.at[:, span]) for span in spans[1:]]
    copies = [
        pltpu.make_async_copy(source, target, sems.at[index])
        for index, (source, target) in enumerate(loads)
    ]
    for copy in copies:
        copy.start()
    for index, start in enumerate(range(0, columns, step)):
        lanes = slice(start, start + step)
        force = jnp.concatenate(
            [
                own_force_ref[:, :, lanes].reshape(rows // 2, step),
                other_force_ref[:, :, lanes].reshape(rows // 2, step),
            ],
            axis=0,
        )
        if index == 0:
            copies[0].wait()
            copies[1].wait()
        pushed = dot32(matrices[0], force) + dot32(matrices[1], force)
        copies[2 if index == 0 else 5 + index].wait()
        if index == 0:
            copies[3].wait()
        modal = (state[:, lanes] + time_step * pushed) * damping[...]
        modal_high, modal_low = split(modal)
        if index == 0:
            copies[4].wait()
            copies[5].wait()
        solved = (
            dot32(matrices[2], modal_high)
            + dot32(matrices[2], modal_low)
            + dot32(matrices[3], modal_high)
        )
        out_ref[:, :, lanes] = solved.astype(jnp.bfloat16).reshape(slab_shape + (step,))


def merge_rows(values):
    sublane = lax.broadcasted_iota(jnp.int32, (8, 128), 0)
    for bit in (4, 2, 1):
        keep = (sublane & bit) == 0
        half = len(values) // 2
        merged = []
        for index in range(half):
            a, b = values[index], values[index + half]
            own = jnp.where(keep, a, b)
            other = jnp.where(keep, b, a)
            if bit == 4:
                moved = pltpu.roll(other, 4, 0)
            else:
                moved = jnp.where(
                    keep, pltpu.roll(other, 8 - bit, 0), pltpu.roll(other, bit, 0)
                )
            merged.append(own + moved)
        values = merged
    return values[0]


def gather_kernel(
    block_ref,
    cell_ref,
    order_ref,
    table_ref,
    back_ref,
    phase_ref,
    planes_ref,
    part_ref,
    left,
    values,
    planes,
    sampled,
    phases,
    table,
    table_sem,
    phase_sem,
    plane_sem,
    *,
    half_modes,
    pencil_modes,
    pencil_waves,
):
    tiles, size = cell_ref.shape
    strips = NX // CB
    group_rows = 2 * half_modes
    slab_rows = back_ref.shape[1]
    pz_count = half_modes // pencil_modes
    half_waves = pencil_waves // 2
    component_rows = group_rows * slab_rows
    table_copies = [
        pltpu.make_async_copy(table_ref.at[parity], table.at[parity], table_sem.at[parity])
        for parity in range(2)
    ]
    for copy in table_copies:
        copy.start()
    phase_copy = pltpu.make_async_copy(phase_ref, phases, phase_sem)
    phase_copy.start()
    copies = []
    for component in range(3):
        rows = []
        for part in range(2):
            for mode in range(half_modes):
                column = (
                    (component * pencil_modes + mode % pencil_modes) * 2 + part
                ) * pencil_waves
                pieces = []
                for parity in range(2):
                    for px in range(KX // pencil_waves):
                        first = column + parity * half_waves
                        pieces.append(
                            back_ref[
                                px * pz_count + mode // pencil_modes,
                                :,
                                first : first + half_waves,
                            ]
                        )
                rows.append(jnp.concatenate(pieces, axis=1))
        turned = dot32(order_ref[...], jnp.concatenate(rows, axis=0)).astype(jnp.bfloat16)
        for parity in range(2):
            lanes = slice(parity * PAIR, (parity + 1) * PAIR)
            left[parity, :, 0:PAIR] = turned[0:component_rows, lanes]
            left[parity, :, PAIR:KX] = turned[component_rows:, lanes]
        if component == 0:
            table_copies[0].wait()
        even = dot32(left[0], table[0])
        if component == 0:
            table_copies[1].wait()
        odd = dot32(left[1], table[1])
        for side in range(2):
            plane = (even + odd if side == 0 else even - odd).astype(jnp.bfloat16)
            whole = plane.astype(jnp.float32)
            planes[:, component, :, :, side * HALF : (side + 1) * HALF] = plane.reshape(
                slab_rows, half_modes, 2, HALF
            )
            for strip in range(HALF // 128):
                values[
                    side * (HALF // 128) + strip,
                    component * component_rows : (component + 1) * component_rows,
                    :,
                ] = whole[:, strip * 128 : (strip + 1) * 128]
        copy = pltpu.make_async_copy(
            planes.at[:, component], planes_ref.at[:, component], plane_sem.at[component]
        )
        copy.start()
        copies.append(copy)
    phase_copy.wait()

    def tile_group(group, carry):
        first_tile = pl.multiple_of(group * 8, 8)
        places = []
        for offset in range(8):
            block = block_ref[first_tile + offset]
            places.append((block % strips, block // strips))
        cells = cell_ref[pl.ds(first_tile, 8), :]
        for piece in range(size // 128):
            lanes = slice(piece * 128, (piece + 1) * 128)
            weighted = [[], [], []]
            for offset in range(8):
                strip, y = places[offset]
                cell = jnp.broadcast_to(cells[offset : offset + 1, lanes], (group_rows, 128))
                spot = cell % 128
                upper = cell >= 128
                rows_of_tile = pl.multiple_of((first_tile + offset) * group_rows, 8)
                phase = phases[piece, pl.ds(rows_of_tile, group_rows), :]
                for component in range(3):
                    start = pl.multiple_of(component * component_rows + y * group_rows, 8)
                    rows = pl.ds(start, group_rows)
                    low = jnp.take_along_axis(values[strip * 2, rows, :], spot, axis=1)
                    high = jnp.take_along_axis(values[strip * 2 + 1, rows, :], spot, axis=1)
                    product = jnp.where(upper, high, low) * phase
                    total = product[0:8]
                    for more in range(8, group_rows, 8):
                        total = total + product[more : more + 8]
                    weighted[component].append(total)
            for component in range(3):
                sampled[component, pl.ds(first_tile, 8), lanes] = merge_rows(weighted[component])
        return carry

    lax.fori_loop(0, tiles // 8, tile_group, 0)
    part_ref[...] = sampled[...].astype(jnp.bfloat16)
    for copy in copies:
        copy.wait()


def on_device(
    cell_index,
    block_index,
    volume,
    response_rate,
    spanwise_position,
    particle_velocity,
    seen_velocity,
    fluid_velocity,
    eigen_basis,
    eigen_inverse,
    eigenvalues,
):
    group_index = lax.axis_index("grp")
    px_count = lax.axis_size("px")
    zh_count = lax.axis_size("zh")
    zl_count = lax.axis_size("zl")
    pz_count = zh_count * zl_count
    half_index = lax.axis_index("zh")
    pz_index = half_index * zl_count + lax.axis_index("zl")
    rows = fluid_velocity.shape[0]
    pencil_modes = fluid_velocity.shape[2]
    pencil_waves = fluid_velocity.shape[4]
    half_modes = pencil_modes * pz_count
    slabs = px_count * pz_count
    slab_rows = rows // slabs
    tiles, size = cell_index.shape
    width = 6 * half_modes
    component_rows = 2 * half_modes * slab_rows
    columns = 6 * pencil_modes * pencil_waves
    pencil = pencil_modes * pencil_waves
    sizes = dict(half_modes=half_modes, pencil_modes=pencil_modes, pencil_waves=pencil_waves)

    vmem = pl.BlockSpec(memory_space=pltpu.VMEM)
    smem = pl.BlockSpec(memory_space=pltpu.SMEM)
    hbm = pl.BlockSpec(memory_space=pltpu.HBM)
    in_hbm = functools.partial(pltpu.with_memory_space_constraint, memory_space=pltpu.HBM)
    phase_shape = (size // 128, tiles * 2 * half_modes, 128)

    modes = half_modes // zh_count
    row_width = -(-6 * modes // 8) * 8
    spread_shape = (px_count * zl_count, slab_rows, columns)
    table_shape = (2, HALF, KX)
    pack = pl.pallas_call(
        pack_kernel,
        out_shape=jax.ShapeDtypeStruct((6, tiles, size), jnp.bfloat16),
        in_specs=[vmem] * 6,
        out_specs=vmem,
        name="pack",
    )(
        cell_index,
        volume,
        response_rate,
        spanwise_position,
        particle_velocity,
        seen_velocity,
    )
    swap = [(0, 1), (1, 0)]
    other_pack = lax.ppermute(pack, "zh", swap)
    other_block = lax.ppermute(block_index, "zh", swap)
    first_wave = (group_index * half_modes + half_index * modes + 1).reshape(1).astype(jnp.int32)
    spread_order = jnp.asarray(spread_rows(modes, slab_rows, row_width), jnp.bfloat16)
    spread_scratch = [
        pltpu.VMEM((NX // 128, slab_rows * row_width, 128), jnp.float32),
        pltpu.VMEM((2, slab_rows * row_width, HALF), jnp.bfloat16),
        pltpu.VMEM((6, tiles, size), jnp.float32),
        pltpu.VMEM((tiles, size), jnp.int32),
        pltpu.VMEM((size // 128, tiles * row_width, 128), jnp.float32),
        pltpu.VMEM(table_shape, jnp.bfloat16),
        pltpu.SemaphoreType.DMA,
    ]
    spread_sizes = dict(
        modes=modes,
        pencil_modes=pencil_modes,
        pencil_waves=pencil_waves,
        slab_rows=slab_rows,
        width=row_width,
    )
    spread_own = pl.pallas_call(
        functools.partial(spread_kernel, makes_table=True, **spread_sizes),
        out_shape=(
            jax.ShapeDtypeStruct(spread_shape, jnp.bfloat16),
            jax.ShapeDtypeStruct(table_shape, jnp.bfloat16),
        ),
        in_specs=[smem, smem] + [vmem] * 6,
        out_specs=(vmem, hbm),
        scratch_shapes=spread_scratch + [pltpu.VMEM((HALF, KX), jnp.float32)] * 2,
        name="spread",
    )
    seeds = [jnp.asarray(seed) for seed in forward_seeds()]
    outgoing, wave_table = spread_own(block_index, first_wave, pack, spread_order, *seeds)
    own_force = lax.all_to_all(outgoing, ("px", "zl"), split_axis=0, concat_axis=0, tiled=True)
    other_outgoing = pl.pallas_call(
        functools.partial(spread_kernel, makes_table=False, **spread_sizes),
        out_shape=jax.ShapeDtypeStruct(spread_shape, jnp.bfloat16),
        in_specs=[smem, smem, vmem, vmem, hbm],
        out_specs=vmem,
        scratch_shapes=spread_scratch,
        name="spread_other",
    )(other_block, first_wave, other_pack, spread_order, in_hbm(wave_table))
    other_force = lax.all_to_all(
        other_outgoing, ("px", "zl"), split_axis=0, concat_axis=0, tiled=True
    )
    phases = pl.pallas_call(
        functools.partial(phase_kernel, half_modes=half_modes),
        out_shape=jax.ShapeDtypeStruct(phase_shape, jnp.float32),
        in_specs=[smem, vmem],
        out_specs=vmem,
        compiler_params=pltpu.CompilerParams(vmem_limit_bytes=24 << 20),
        name="phases",
    )((group_index * half_modes + 1).reshape(1).astype(jnp.int32), spanwise_position)

    def halves(matrix):
        high = lax.reduce_precision(matrix, 8, 7)
        return high.astype(jnp.bfloat16), (matrix - high).astype(jnp.bfloat16)

    inverse_high, inverse_low = halves(eigen_inverse)
    basis_high, basis_low = halves(eigen_basis)
    by_half = eigen_inverse.reshape(rows, px_count, zh_count, zl_count * slab_rows)
    own_columns = lax.dynamic_slice_in_dim(by_half, half_index, 1, 2).reshape(rows, rows // 2)
    other_columns = lax.dynamic_slice_in_dim(by_half, 1 - half_index, 1, 2).reshape(
        rows, rows // 2
    )
    turned_high, turned_low = halves(jnp.concatenate([own_columns, other_columns], axis=1))
    state = fluid_velocity.transpose(0, 1, 2, 3, 4).reshape(rows, columns)
    square = pl.BlockSpec((rows, rows), lambda i: (0, 0))
    strip_spec = pl.BlockSpec((rows, pencil_waves), lambda i: (0, i))
    projected = pl.pallas_call(
        project_kernel,
        grid=(columns // pencil_waves,),
        out_shape=jax.ShapeDtypeStruct((rows, columns), jnp.float32),
        in_specs=[
            square,
            square,
            pl.BlockSpec((pencil_waves, pencil_waves), lambda i: (0, 0)),
            strip_spec,
        ],
        out_specs=strip_spec,
        compiler_params=pltpu.CompilerParams(vmem_limit_bytes=24 << 20),
        name="project",
    )(inverse_high, inverse_low, jnp.asarray(order_matrix(pencil_waves), jnp.bfloat16), state)
    lane = jnp.arange(pencil_waves)
    half_waves = pencil_waves // 2
    wave = 2 * (lane % half_waves) + lane // half_waves
    stream_wave = (lax.axis_index("px") * pencil_waves + wave - KX // 2).astype(jnp.float32) * 0.5
    span_wave = (
        group_index * half_modes
        + pz_index * pencil_modes
        + jnp.arange(pencil_modes)
        + 1
    ).astype(jnp.float32)
    wave_square = (
        stream_wave[None, :] * stream_wave[None, :] + span_wave[:, None] * span_wave[:, None]
    )
    wave_square = jnp.broadcast_to(wave_square[:, None, :], (pencil_modes, 2, pencil_waves))
    damping = 1.0 / (
        1.0 + viscosity * (eigenvalues[:, None] + wave_square.reshape(1, 2 * pencil))
    )
    table = pl.pallas_call(
        table_kernel,
        out_shape=jax.ShapeDtypeStruct((2, KX, HALF), jnp.bfloat16),
        in_specs=[vmem] * 4,
        out_specs=vmem,
        scratch_shapes=[pltpu.VMEM((PAIR, HALF), jnp.float32)] * 2,
        compiler_params=pltpu.CompilerParams(vmem_limit_bytes=24 << 20),
        name="waves",
    )(*[jnp.asarray(seed) for seed in inverse_seeds()])

    solved = pl.pallas_call(
        solve_kernel,
        out_shape=jax.ShapeDtypeStruct((slabs, slab_rows, columns), jnp.bfloat16),
        in_specs=[hbm] * 6 + [vmem] * 2,
        out_specs=vmem,
        scratch_shapes=[
            pltpu.VMEM((4, rows, rows), jnp.bfloat16),
            pltpu.VMEM((rows, 2 * pencil), jnp.float32),
            pltpu.VMEM((rows, columns), jnp.float32),
            pltpu.SemaphoreType.DMA((8,)),
        ],
        compiler_params=pltpu.CompilerParams(vmem_limit_bytes=32 << 20),
        name="solve",
    )(
        in_hbm(turned_high),
        in_hbm(turned_low),
        in_hbm(basis_high),
        in_hbm(basis_low),
        in_hbm(damping),
        in_hbm(projected),
        own_force,
        other_force,
    )
    returned = lax.all_to_all(solved, ("px", "zh", "zl"), split_axis=0, concat_axis=0, tiled=True)
    velocity_planes, mode_part = pl.pallas_call(
        functools.partial(gather_kernel, **sizes),
        out_shape=(
            jax.ShapeDtypeStruct((slab_rows, 3, half_modes, 2, NX), jnp.bfloat16),
            jax.ShapeDtypeStruct((3, tiles, size), jnp.bfloat16),
        ),
        in_specs=[smem, vmem, vmem, hbm, vmem, hbm],
        out_specs=(hbm, vmem),
        scratch_shapes=[
            pltpu.VMEM((2, component_rows, KX), jnp.bfloat16),
            pltpu.VMEM((NX // 128, slab_rows * width, 128), jnp.float32),
            pltpu.VMEM((slab_rows, 3, half_modes, 2, NX), jnp.bfloat16),
            pltpu.VMEM((3, tiles, size), jnp.float32),
            pltpu.VMEM(phase_shape, jnp.float32),
            pltpu.VMEM((2, KX, HALF), jnp.bfloat16),
            pltpu.SemaphoreType.DMA((2,)),
            pltpu.SemaphoreType.DMA,
            pltpu.SemaphoreType.DMA((3,)),
        ],
        compiler_params=pltpu.CompilerParams(vmem_limit_bytes=40 << 20),
        name="gather",
    )(
        block_index,
        cell_index,
        jnp.asarray(gather_rows(half_modes, slab_rows), jnp.bfloat16),
        in_hbm(table),
        returned,
        in_hbm(phases),
    )
    other_part = lax.ppermute(mode_part, "grp", [(0, 1), (1, 0)])
    fluid_at = mode_part.astype(jnp.float32) + other_part.astype(jnp.float32)
    upward = (jnp.arange(3) == 1).astype(jnp.float32)[:, None, None]
    updated_velocity = (
        particle_velocity
        + time_step * response_rate * (fluid_at - particle_velocity)
        - time_step * gravity * upward
    )
    return (velocity_planes, updated_velocity)


def solution(mesh):
    groups, px_count, pz_count = mesh.devices.shape
    halves = jax.sharding.Mesh(
        mesh.devices.reshape(groups, px_count, 2, pz_count // 2), ("grp", "px", "zh", "zl")
    )
    slab = ("px", "zh", "zl")
    in_specs = (
        P(slab, None),
        P(slab),
        P(slab, None),
        P(slab, None),
        P(slab, None),
        P(None, slab, None),
        P(None, slab, None),
        P(None, None, ("grp", "zh", "zl"), None, "px"),
        P(),
        P(),
        P(),
    )
    out_specs = (P(slab, None, "grp", None, None), P(None, slab, None))
    return jax.shard_map(
        on_device, mesh=halves, in_specs=in_specs, out_specs=out_specs, check_vma=False
    )
```

```python
import functools
import math

import jax
import jax.numpy as jnp
import numpy as np
from jax import lax
from jax.experimental import pallas as pl
from jax.experimental.pallas import tpu as pltpu
from jax.sharding import PartitionSpec as P

NX = 2048
KX = 1024
CB = 256
SPLIT = 4
POINTS = NX // SPLIT
WAVES = KX // SPLIT
TILE_GROUP = 8

time_step = 0.5
gravity = 0.8
viscosity = 0.0001


def turns(rows, columns):
    phase = np.mod(np.asarray(rows)[:, None] * np.asarray(columns)[None, :], NX)
    angles = phase.astype(np.float64) * (2.0 * math.pi / NX)
    return np.cos(angles).astype(np.float32), np.sin(angles).astype(np.float32)


def forward_seeds():
    waves = np.concatenate([SPLIT * np.arange(WAVES) + rest - KX // 2 for rest in range(SPLIT)])
    base = turns(np.arange(8), waves)
    steps = turns(8 * 2 ** np.arange(8), waves)
    scale = np.float32(1.0 / math.sqrt(NX))
    return [base[0] * scale, base[1] * scale, steps[0], steps[1]]


def inverse_seeds():
    points = np.arange(POINTS)
    bases = [
        turns(SPLIT * np.arange(8) + rest - KX // 2, points) for rest in range(SPLIT)
    ]
    steps = turns(8 * SPLIT * 2 ** np.arange(8), points)
    scale = np.float32(1.0 / math.sqrt(NX))
    cosines = np.stack([b[0] for b in bases]) * scale
    sines = np.stack([b[1] for b in bases]) * scale
    return [cosines, sines, steps[0], steps[1]]


def order_matrix(waves):
    matrix = np.zeros((waves, waves), np.float32)
    lanes = np.arange(waves)
    span = waves // SPLIT
    matrix[SPLIT * (lanes % span) + lanes // span, lanes] = 1.0
    return matrix


def spread_rows(half_modes, slab_rows):
    part, mode, y = np.meshgrid(
        np.arange(2), np.arange(half_modes), np.arange(slab_rows), indexing="ij"
    )
    count = part.size
    matrix = np.zeros((count, count), np.float32)
    source = (y * 2 + part) * half_modes + mode
    matrix[np.arange(count), source.ravel()] = 1.0
    return matrix


def gather_rows(half_modes, slab_rows):
    y, mode, part = np.meshgrid(
        np.arange(slab_rows), np.arange(half_modes), np.arange(2), indexing="ij"
    )
    count = part.size
    matrix = np.zeros((2 * count, count), np.float32)
    source = (part * half_modes + mode) * slab_rows + y
    other = ((1 - part) * half_modes + mode) * slab_rows + y
    matrix[np.arange(count), source.ravel()] = 1.0
    matrix[count + np.arange(count), other.ravel()] = np.where(part.ravel() == 0, -1.0, 1.0)
    return matrix


def grow(cos_ref, sin_ref, base, steps, rows):
    cos_ref[0:8, :] = base[0]
    sin_ref[0:8, :] = base[1]
    done = 8
    level = 0
    while done < rows:
        turn_cos = steps[0][level : level + 1, :]
        turn_sin = steps[1][level : level + 1, :]

        def block(index, carry, done=done, turn_cos=turn_cos, turn_sin=turn_sin):
            start = pl.multiple_of(index * 8, 8)
            old_cos = cos_ref[pl.ds(start, 8), :]
            old_sin = sin_ref[pl.ds(start, 8), :]
            cos_ref[pl.ds(done + start, 8), :] = old_cos * turn_cos - old_sin * turn_sin
            sin_ref[pl.ds(done + start, 8), :] = old_sin * turn_cos + old_cos * turn_sin
            return carry

        lax.fori_loop(0, done // 8, block, 0)
        done *= 2
        level += 1


def dot32(a, b):
    return jnp.dot(a, b, preferred_element_type=jnp.float32)


def spread_kernel(
    block_ref,
    group_ref,
    cell_ref,
    volume_ref,
    rate_ref,
    place_ref,
    motion_ref,
    seen_ref,
    base_cos_ref,
    base_sin_ref,
    step_cos_ref,
    step_sin_ref,
    order_ref,
    out_ref,
    field,
    table_cos,
    table_sin,
    table,
    left,
    amounts,
    phases,
    packed,
    out_sem,
    *,
    half_modes,
    pencil_modes,
    pencil_waves,
):
    tiles, size = cell_ref.shape
    strips = NX // CB
    group_rows = 2 * half_modes
    slab_rows = field.shape[1] // (3 * group_rows)
    component_rows = slab_rows * group_rows
    pz_count = half_modes // pencil_modes

    first = (group_ref[0] * half_modes + 1).astype(jnp.float32)
    for mode, (cosine, sine) in enumerate(turn_modes(place_ref[...], first, half_modes)):
        for piece in range(size // 128):
            lanes = slice(piece * 128, (piece + 1) * 128)
            for part, value in ((0, cosine), (1, -sine)):
                rows = pl.ds(part * half_modes + mode, tiles, stride=group_rows)
                phases[piece, rows, :] = value[:, lanes]

    upper = cell_ref[...] >= 128
    volume = volume_ref[...]
    pull = volume * rate_ref[...]
    for component in range(3):
        amount = pull * (seen_ref[component] - motion_ref[component])
        if component == 1:
            amount = amount - gravity * volume
        amounts[component] = jnp.where(upper, 0.0, amount)
        amounts[3 + component] = jnp.where(upper, amount, 0.0)

    grow(
        table_cos,
        table_sin,
        (base_cos_ref[...], base_sin_ref[...]),
        (step_cos_ref, step_sin_ref),
        POINTS,
    )
    for rest in range(SPLIT):
        lanes = slice(rest * WAVES, (rest + 1) * WAVES)
        table[rest, :, 0:WAVES] = table_cos[:, lanes].astype(jnp.bfloat16)
        table[rest, :, WAVES:] = table_sin[:, lanes].astype(jnp.bfloat16)

    def clear(index, carry):
        field[index] = jnp.zeros(field.shape[1:], jnp.float32)
        return carry

    lax.fori_loop(0, field.shape[0], clear, 0)

    cells = lax.broadcasted_iota(jnp.int32, (128, size), 0)

    def tile_group(group, carry):
        shares = []
        for offset in range(TILE_GROUP):
            tile = group * TILE_GROUP + offset
            row = pl.ds(tile, 1)
            rows_of_tile = pl.ds(pl.multiple_of(tile * group_rows, 8), group_rows)
            phase = jnp.concatenate(
                [phases[piece, rows_of_tile, :] for piece in range(size // 128)], axis=1
            )
            payload = jnp.concatenate([amounts[k, row, :] * phase for k in range(6)], axis=0)
            spot = cell_ref[row, :] % 128
            one_hot = (spot == cells).astype(jnp.float32).astype(jnp.bfloat16)
            shares.append(
                lax.dot_general(
                    payload.astype(jnp.bfloat16),
                    one_hot,
                    (((1,), (1,)), ((), ())),
                    preferred_element_type=jnp.float32,
                )
            )
        for offset in range(TILE_GROUP):
            block = block_ref[group * TILE_GROUP + offset]
            strip = block % strips
            y = block // strips
            for half in range(2):
                for component in range(3):
                    start = pl.multiple_of(component * component_rows + y * group_rows, 8)
                    own = (half * 3 + component) * group_rows
                    field[strip * 2 + half, pl.ds(start, group_rows), :] += shares[offset][
                        own : own + group_rows
                    ]
        return carry

    lax.fori_loop(0, tiles // TILE_GROUP, tile_group, 0)

    order = order_ref[...]
    def times_minus_i(value):
        lanes = value.shape[1]
        value = value.reshape(slab_rows, group_rows, lanes)
        part = lax.broadcasted_iota(jnp.int32, value.shape, 1) // half_modes
        moved = pltpu.roll(value, half_modes, 1)
        return jnp.where(part == 0, moved, -moved).reshape(component_rows, lanes)

    rest_waves = pencil_waves // SPLIT
    copies = []
    for component in range(3):
        rows = slice(component * component_rows, (component + 1) * component_rows)
        for strip in range(POINTS // 128):
            values = [field[strip + j * (POINTS // 128), rows, :] for j in range(SPLIT)]
            lanes = slice(strip * 128, (strip + 1) * 128)
            even_sum = values[0] + values[2]
            odd_sum = values[1] + values[3]
            even_gap = values[0] - values[2]
            odd_gap = times_minus_i(values[1] - values[3])
            left[0, :, lanes] = (even_sum + odd_sum).astype(jnp.bfloat16)
            left[1, :, lanes] = (even_gap + odd_gap).astype(jnp.bfloat16)
            left[2, :, lanes] = (even_sum - odd_sum).astype(jnp.bfloat16)
            left[3, :, lanes] = (even_gap - odd_gap).astype(jnp.bfloat16)
        spectra = []
        for rest in range(SPLIT):
            product = dot32(left[rest], table[rest])
            spectrum = product[:, :WAVES] + times_minus_i(product[:, WAVES:])
            spectra.append(dot32(order, spectrum.astype(jnp.bfloat16)).astype(jnp.bfloat16))
        for owner_px in range(KX // pencil_waves):
            own = slice(owner_px * rest_waves, (owner_px + 1) * rest_waves)
            joined = jnp.concatenate([spectrum[:, own] for spectrum in spectra], axis=1)
            for part in range(2):
                for mode in range(half_modes):
                    column = (
                        (component * pencil_modes + mode % pencil_modes) * 2 + part
                    ) * pencil_waves
                    row = (part * half_modes + mode) * slab_rows
                    packed[
                        owner_px * pz_count + mode // pencil_modes,
                        :,
                        column : column + pencil_waves,
                    ] = joined[row : row + slab_rows]
        span = 2 * pencil_modes * pencil_waves
        lanes = pl.ds(component * span, span)
        copy = pltpu.make_async_copy(
            packed.at[:, :, lanes], out_ref.at[:, :, lanes], out_sem.at[component]
        )
        copy.start()
        copies.append(copy)
    for copy in copies:
        copy.wait()


def table_kernel(base_cos_ref, base_sin_ref, step_cos_ref, step_sin_ref, out_ref, work_cos, work_sin):
    for rest in range(SPLIT):
        grow(
            work_cos,
            work_sin,
            (base_cos_ref[rest], base_sin_ref[rest]),
            (step_cos_ref, step_sin_ref),
            WAVES,
        )
        out_ref[rest, 0:WAVES, :] = work_cos[...].astype(jnp.bfloat16)
        out_ref[rest, WAVES:, :] = work_sin[...].astype(jnp.bfloat16)


def turn_modes(place, first, modes):
    cos_one = jnp.cos(place)
    sin_one = jnp.sin(place)
    cos_now = jnp.cos(place * first)
    sin_now = jnp.sin(place * first)
    turned = [(cos_now, sin_now)]
    for _ in range(modes - 1):
        cos_now, sin_now = (
            cos_now * cos_one - sin_now * sin_one,
            sin_now * cos_one + cos_now * sin_one,
        )
        turned.append((cos_now, sin_now))
    return turned


def phase_kernel(group_ref, place_ref, out_ref, *, half_modes):
    tiles, size = place_ref.shape
    first = (group_ref[0] * half_modes + 1).astype(jnp.float32)
    for mode, (cosine, sine) in enumerate(turn_modes(place_ref[...], first, half_modes)):
        for piece in range(size // 128):
            lanes = slice(piece * 128, (piece + 1) * 128)
            for part, value in ((0, cosine), (1, -sine)):
                rows = pl.ds(2 * mode + part, tiles, stride=2 * half_modes)
                out_ref[piece, rows, :] = value[:, lanes]


def split(value):
    high = value.astype(jnp.bfloat16)
    return high, (value - high.astype(jnp.float32)).astype(jnp.bfloat16)


def project_kernel(high_ref, low_ref, order_ref, state_ref, out_ref):
    order = order_ref[...]
    state_high, state_low = [
        dot32(value, order).astype(jnp.bfloat16) for value in split(state_ref[...])
    ]
    out_ref[...] = (
        dot32(high_ref[...], state_high)
        + dot32(high_ref[...], state_low)
        + dot32(low_ref[...], state_high)
    )


def solve_kernel(
    inverse_high_ref,
    basis_high_ref,
    basis_low_ref,
    damping_ref,
    state_ref,
    force_ref,
    out_ref,
    matrices,
    damping,
    state,
    results,
    sems,
    out_sems,
):
    rows, step = damping_ref.shape
    columns = force_ref.shape[-1]
    force_rows = force_ref[...].reshape(rows, columns)
    slab_shape = out_ref.shape[:2]
    spans = [pl.ds(start, step) for start in range(0, columns, step)]
    loads = [
        (inverse_high_ref, matrices.at[0]),
        (state_ref.at[:, spans[0]], state.at[:, spans[0]]),
        (damping_ref, damping),
        (basis_high_ref, matrices.at[1]),
        (basis_low_ref, matrices.at[2]),
    ] + [(state_ref.at[:, span], state.at[:, span]) for span in spans[1:]]
    copies = [
        pltpu.make_async_copy(source, target, sems.at[index])
        for index, (source, target) in enumerate(loads)
    ]
    for copy in copies:
        copy.start()
    stores = []
    for index, start in enumerate(range(0, columns, step)):
        lanes = slice(start, start + step)
        force = force_rows[:, lanes]
        if index == 0:
            copies[0].wait()
        pushed = dot32(matrices[0], force)
        copies[1 if index == 0 else 4 + index].wait()
        if index == 0:
            copies[2].wait()
        modal_high, modal_low = split((state[:, lanes] + time_step * pushed) * damping[...])
        if index == 0:
            copies[3].wait()
            copies[4].wait()
        solved = (
            dot32(matrices[1], modal_high)
            + dot32(matrices[1], modal_low)
            + dot32(matrices[2], modal_high)
        )
        results[:, :, lanes] = solved.astype(jnp.bfloat16).reshape(slab_shape + (step,))
        copy = pltpu.make_async_copy(
            results.at[:, :, spans[index]], out_ref.at[:, :, spans[index]], out_sems.at[index]
        )
        copy.start()
        stores.append(copy)
    for copy in stores:
        copy.wait()


def merge_rows(values):
    sublane = lax.broadcasted_iota(jnp.int32, (8, 128), 0)
    for bit in (4, 2, 1):
        keep = (sublane & bit) == 0
        half = len(values) // 2
        merged = []
        for index in range(half):
            a, b = values[index], values[index + half]
            own = jnp.where(keep, a, b)
            other = jnp.where(keep, b, a)
            if bit == 4:
                moved = pltpu.roll(other, 4, 0)
            else:
                moved = jnp.where(
                    keep, pltpu.roll(other, 8 - bit, 0), pltpu.roll(other, bit, 0)
                )
            merged.append(own + moved)
        values = merged
    return values[0]


def gather_kernel(
    block_ref,
    cell_ref,
    order_ref,
    table_ref,
    back_ref,
    phase_ref,
    planes_ref,
    part_ref,
    left,
    values,
    planes,
    sampled,
    phases,
    table,
    table_sem,
    phase_sem,
    plane_sem,
    *,
    half_modes,
    pencil_modes,
    pencil_waves,
):
    tiles, size = cell_ref.shape
    strips = NX // CB
    group_rows = 2 * half_modes
    slab_rows = back_ref.shape[1]
    pz_count = half_modes // pencil_modes
    component_rows = group_rows * slab_rows
    table_copies = [
        pltpu.make_async_copy(table_ref.at[rest], table.at[rest], table_sem.at[rest])
        for rest in range(SPLIT)
    ]
    for copy in table_copies:
        copy.start()
    phase_copy = pltpu.make_async_copy(phase_ref, phases, phase_sem)
    phase_copy.start()
    rest_waves = pencil_waves // SPLIT

    def times_i(value):
        shape = value.shape
        value = value.reshape(shape[0] // 8, 8, shape[1])
        part = lax.broadcasted_iota(jnp.int32, value.shape, 1) % 2
        return jnp.where(
            part == 0, -pltpu.roll(value, 7, 1), pltpu.roll(value, 1, 1)
        ).reshape(shape)

    copies = []
    for component in range(3):
        rows = []
        for part in range(2):
            for mode in range(half_modes):
                column = (
                    (component * pencil_modes + mode % pencil_modes) * 2 + part
                ) * pencil_waves
                sources = [
                    back_ref[
                        px * pz_count + mode // pencil_modes, :, column : column + pencil_waves
                    ]
                    for px in range(KX // pencil_waves)
                ]
                rows.append(
                    jnp.concatenate(
                        [
                            source[:, rest * rest_waves : (rest + 1) * rest_waves]
                            for rest in range(SPLIT)
                            for source in sources
                        ],
                        axis=1,
                    )
                )
        turned = dot32(order_ref[...], jnp.concatenate(rows, axis=0)).astype(jnp.bfloat16)
        results = []
        for rest in range(SPLIT):
            lanes = slice(rest * WAVES, (rest + 1) * WAVES)
            left[rest, :, 0:WAVES] = turned[0:component_rows, lanes]
            left[rest, :, WAVES:] = turned[component_rows:, lanes]
            if component == 0:
                table_copies[rest].wait()
            results.append(dot32(left[rest], table[rest]))
        even_sum = results[0] + results[2]
        odd_sum = results[1] + results[3]
        even_gap = results[0] - results[2]
        odd_gap = times_i(results[1] - results[3])
        quarters = [even_sum + odd_sum, even_gap + odd_gap, even_sum - odd_sum, even_gap - odd_gap]
        for side, quarter in enumerate(quarters):
            plane = quarter.astype(jnp.bfloat16)
            whole = plane.astype(jnp.float32)
            planes[:, component, :, :, side * POINTS : (side + 1) * POINTS] = plane.reshape(
                slab_rows, half_modes, 2, POINTS
            )
            for strip in range(POINTS // 128):
                values[
                    side * (POINTS // 128) + strip,
                    component * component_rows : (component + 1) * component_rows,
                    :,
                ] = whole[:, strip * 128 : (strip + 1) * 128]
        copy = pltpu.make_async_copy(
            planes.at[:, component], planes_ref.at[:, component], plane_sem.at[component]
        )
        copy.start()
        copies.append(copy)
    phase_copy.wait()

    def tile_group(group, carry):
        first_tile = pl.multiple_of(group * 8, 8)
        places = []
        for offset in range(8):
            block = block_ref[first_tile + offset]
            places.append((block % strips, block // strips))
        cells = cell_ref[pl.ds(first_tile, 8), :]
        for piece in range(size // 128):
            lanes = slice(piece * 128, (piece + 1) * 128)
            weighted = [[], [], []]
            for offset in range(8):
                strip, y = places[offset]
                cell = jnp.broadcast_to(cells[offset : offset + 1, lanes], (group_rows, 128))
                spot = cell % 128
                upper = cell >= 128
                rows_of_tile = pl.multiple_of((first_tile + offset) * group_rows, 8)
                phase = phases[piece, pl.ds(rows_of_tile, group_rows), :]
                for component in range(3):
                    start = pl.multiple_of(component * component_rows + y * group_rows, 8)
                    rows = pl.ds(start, group_rows)
                    low = jnp.take_along_axis(values[strip * 2, rows, :], spot, axis=1)
                    high = jnp.take_along_axis(values[strip * 2 + 1, rows, :], spot, axis=1)
                    product = jnp.where(upper, high, low) * phase
                    total = product[0:8]
                    for more in range(8, group_rows, 8):
                        total = total + product[more : more + 8]
                    weighted[component].append(total)
            for component in range(3):
                sampled[component, pl.ds(first_tile, 8), lanes] = merge_rows(weighted[component])
        return carry

    lax.fori_loop(0, tiles // 8, tile_group, 0)
    part_ref[...] = sampled[...].astype(jnp.bfloat16)
    for copy in copies:
        copy.wait()


def on_device(
    cell_index,
    block_index,
    volume,
    response_rate,
    spanwise_position,
    particle_velocity,
    seen_velocity,
    fluid_velocity,
    eigen_basis,
    eigen_inverse,
    eigenvalues,
):
    group_index = lax.axis_index("grp")
    px_count = lax.axis_size("px")
    pz_count = lax.axis_size("pz")
    rows = fluid_velocity.shape[0]
    pencil_modes = fluid_velocity.shape[2]
    pencil_waves = fluid_velocity.shape[4]
    half_modes = pencil_modes * pz_count
    slabs = px_count * pz_count
    slab_rows = rows // slabs
    strips = NX // CB
    tiles, size = cell_index.shape
    width = 6 * half_modes
    component_rows = 2 * half_modes * slab_rows
    columns = 6 * pencil_modes * pencil_waves
    pencil = pencil_modes * pencil_waves
    sizes = dict(half_modes=half_modes, pencil_modes=pencil_modes, pencil_waves=pencil_waves)

    vmem = pl.BlockSpec(memory_space=pltpu.VMEM)
    smem = pl.BlockSpec(memory_space=pltpu.SMEM)
    hbm = pl.BlockSpec(memory_space=pltpu.HBM)
    in_hbm = functools.partial(pltpu.with_memory_space_constraint, memory_space=pltpu.HBM)
    phase_shape = (size // 128, tiles * 2 * half_modes, 128)

    group = group_index.reshape(1).astype(jnp.int32)
    outgoing = pl.pallas_call(
        functools.partial(spread_kernel, **sizes),
        out_shape=jax.ShapeDtypeStruct((slabs, slab_rows, columns), jnp.bfloat16),
        in_specs=[smem, smem] + [vmem] * 11,
        out_specs=hbm,
        scratch_shapes=[
            pltpu.VMEM((NX // 128, slab_rows * width, 128), jnp.float32),
            pltpu.VMEM((POINTS, KX), jnp.float32),
            pltpu.VMEM((POINTS, KX), jnp.float32),
            pltpu.VMEM((SPLIT, POINTS, 2 * WAVES), jnp.bfloat16),
            pltpu.VMEM((SPLIT, component_rows, POINTS), jnp.bfloat16),
            pltpu.VMEM((6, tiles, size), jnp.float32),
            pltpu.VMEM(phase_shape, jnp.float32),
            pltpu.VMEM((slabs, slab_rows, columns), jnp.bfloat16),
            pltpu.SemaphoreType.DMA((3,)),
        ],
        name="spread",
    )(
        block_index,
        group,
        cell_index,
        volume,
        response_rate,
        spanwise_position,
        particle_velocity,
        seen_velocity,
        *[jnp.asarray(seed) for seed in forward_seeds()],
        jnp.asarray(spread_rows(half_modes, slab_rows), jnp.bfloat16),
    )
    force = lax.all_to_all(outgoing, ("px", "pz"), split_axis=0, concat_axis=0, tiled=True)

    def halves(matrix):
        high = lax.reduce_precision(matrix, 8, 7)
        return high.astype(jnp.bfloat16), (matrix - high).astype(jnp.bfloat16)

    inverse_high, inverse_low = halves(eigen_inverse)
    basis_high, basis_low = halves(eigen_basis)
    state = fluid_velocity.transpose(0, 1, 2, 3, 4).reshape(rows, columns)
    square = pl.BlockSpec((rows, rows), lambda i: (0, 0))
    strip_spec = pl.BlockSpec((rows, pencil_waves), lambda i: (0, i))
    projected = pl.pallas_call(
        project_kernel,
        grid=(columns // pencil_waves,),
        out_shape=jax.ShapeDtypeStruct((rows, columns), jnp.float32),
        in_specs=[
            square,
            square,
            pl.BlockSpec((pencil_waves, pencil_waves), lambda i: (0, 0)),
            strip_spec,
        ],
        out_specs=strip_spec,
        compiler_params=pltpu.CompilerParams(vmem_limit_bytes=24 << 20),
        name="project",
    )(inverse_high, inverse_low, jnp.asarray(order_matrix(pencil_waves), jnp.bfloat16), state)
    lane = jnp.arange(pencil_waves)
    rest_waves = pencil_waves // SPLIT
    wave = SPLIT * (lane % rest_waves) + lane // rest_waves
    stream_wave = (lax.axis_index("px") * pencil_waves + wave - KX // 2).astype(jnp.float32) * 0.5
    span_wave = (
        group_index * half_modes
        + lax.axis_index("pz") * pencil_modes
        + jnp.arange(pencil_modes)
        + 1
    ).astype(jnp.float32)
    wave_square = (
        stream_wave[None, :] * stream_wave[None, :] + span_wave[:, None] * span_wave[:, None]
    )
    wave_square = jnp.broadcast_to(wave_square[:, None, :], (pencil_modes, 2, pencil_waves))
    damping = 1.0 / (
        1.0 + viscosity * (eigenvalues[:, None] + wave_square.reshape(1, 2 * pencil))
    )
    table = pl.pallas_call(
        table_kernel,
        out_shape=jax.ShapeDtypeStruct((SPLIT, 2 * WAVES, POINTS), jnp.bfloat16),
        in_specs=[vmem] * 4,
        out_specs=vmem,
        scratch_shapes=[pltpu.VMEM((WAVES, POINTS), jnp.float32)] * 2,
        compiler_params=pltpu.CompilerParams(vmem_limit_bytes=24 << 20),
        name="waves",
    )(*[jnp.asarray(seed) for seed in inverse_seeds()])

    phases = pl.pallas_call(
        functools.partial(phase_kernel, half_modes=half_modes),
        out_shape=jax.ShapeDtypeStruct(phase_shape, jnp.float32),
        in_specs=[smem, vmem],
        out_specs=vmem,
        compiler_params=pltpu.CompilerParams(vmem_limit_bytes=24 << 20),
        name="phases",
    )(group, spanwise_position)

    solved = pl.pallas_call(
        solve_kernel,
        out_shape=jax.ShapeDtypeStruct((slabs, slab_rows, columns), jnp.bfloat16),
        in_specs=[hbm] * 5 + [vmem],
        out_specs=hbm,
        scratch_shapes=[
            pltpu.VMEM((3, rows, rows), jnp.bfloat16),
            pltpu.VMEM((rows, 2 * pencil), jnp.float32),
            pltpu.VMEM((rows, columns), jnp.float32),
            pltpu.VMEM((slabs, slab_rows, columns), jnp.bfloat16),
            pltpu.SemaphoreType.DMA((7,)),
            pltpu.SemaphoreType.DMA((3,)),
        ],
        compiler_params=pltpu.CompilerParams(vmem_limit_bytes=32 << 20),
        name="solve",
    )(
        in_hbm(inverse_high),
        in_hbm(basis_high),
        in_hbm(basis_low),
        in_hbm(damping),
        in_hbm(projected),
        force,
    )
    returned = lax.all_to_all(solved, ("px", "pz"), split_axis=0, concat_axis=0, tiled=True)
    velocity_planes, mode_part = pl.pallas_call(
        functools.partial(gather_kernel, **sizes),
        out_shape=(
            jax.ShapeDtypeStruct((slab_rows, 3, half_modes, 2, NX), jnp.bfloat16),
            jax.ShapeDtypeStruct((3, tiles, size), jnp.bfloat16),
        ),
        in_specs=[smem, vmem, vmem, hbm, vmem, hbm],
        out_specs=(hbm, vmem),
        scratch_shapes=[
            pltpu.VMEM((SPLIT, component_rows, 2 * WAVES), jnp.bfloat16),
            pltpu.VMEM((NX // 128, slab_rows * width, 128), jnp.float32),
            pltpu.VMEM((slab_rows, 3, half_modes, 2, NX), jnp.bfloat16),
            pltpu.VMEM((3, tiles, size), jnp.float32),
            pltpu.VMEM(phase_shape, jnp.float32),
            pltpu.VMEM((SPLIT, 2 * WAVES, POINTS), jnp.bfloat16),
            pltpu.SemaphoreType.DMA((SPLIT,)),
            pltpu.SemaphoreType.DMA,
            pltpu.SemaphoreType.DMA((3,)),
        ],
        compiler_params=pltpu.CompilerParams(vmem_limit_bytes=40 << 20),
        name="gather",
    )(
        block_index,
        cell_index,
        jnp.asarray(gather_rows(half_modes, slab_rows), jnp.bfloat16),
        in_hbm(table),
        returned,
        in_hbm(phases),
    )
    other_part = lax.ppermute(mode_part, "grp", [(0, 1), (1, 0)])
    fluid_at = mode_part.astype(jnp.float32) + other_part.astype(jnp.float32)
    upward = (jnp.arange(3) == 1).astype(jnp.float32)[:, None, None]
    updated_velocity = (
        particle_velocity
        + time_step * response_rate * (fluid_at - particle_velocity)
        - time_step * gravity * upward
    )
    return (velocity_planes, updated_velocity)


def solution(mesh):
    in_specs = (
        P(("px", "pz"), None),
        P(("px", "pz")),
        P(("px", "pz"), None),
        P(("px", "pz"), None),
        P(("px", "pz"), None),
        P(None, ("px", "pz"), None),
        P(None, ("px", "pz"), None),
        P(None, None, ("grp", "pz"), None, "px"),
        P(),
        P(),
        P(),
    )
    out_specs = (P(("px", "pz"), None, "grp", None, None), P(None, ("px", "pz"), None))
    return jax.shard_map(
        on_device, mesh=mesh, in_specs=in_specs, out_specs=out_specs, check_vma=False
    )
```

```python
import functools
import math

import jax
import jax.numpy as jnp
import numpy as np
from jax import lax
from jax.experimental import pallas as pl
from jax.experimental.pallas import tpu as pltpu
from jax.sharding import PartitionSpec as P

NX = 2048
KX = 1024
CB = 256
SPLIT = 4
POINTS = NX // SPLIT
WAVES = KX // SPLIT
TILE_GROUP = 8

time_step = 0.5
gravity = 0.8
viscosity = 0.0001


def turns(rows, columns):
    phase = np.mod(np.asarray(rows)[:, None] * np.asarray(columns)[None, :], NX)
    angles = phase.astype(np.float64) * (2.0 * math.pi / NX)
    return np.cos(angles).astype(np.float32), np.sin(angles).astype(np.float32)


def forward_seeds():
    waves = np.concatenate([SPLIT * np.arange(WAVES) + rest - KX // 2 for rest in range(SPLIT)])
    base = turns(np.arange(8), waves)
    steps = turns(8 * 2 ** np.arange(8), waves)
    scale = np.float32(1.0 / math.sqrt(NX))
    return [base[0] * scale, base[1] * scale, steps[0], steps[1]]


def inverse_seeds():
    points = np.arange(POINTS)
    bases = [
        turns(SPLIT * np.arange(8) + rest - KX // 2, points) for rest in range(SPLIT)
    ]
    steps = turns(8 * SPLIT * 2 ** np.arange(8), points)
    scale = np.float32(1.0 / math.sqrt(NX))
    cosines = np.stack([b[0] for b in bases]) * scale
    sines = np.stack([b[1] for b in bases]) * scale
    return [cosines, sines, steps[0], steps[1]]


def order_matrix(waves):
    matrix = np.zeros((waves, waves), np.float32)
    lanes = np.arange(waves)
    span = waves // SPLIT
    matrix[SPLIT * (lanes % span) + lanes // span, lanes] = 1.0
    return matrix


def spread_rows(half_modes, slab_rows):
    part, mode, y = np.meshgrid(
        np.arange(2), np.arange(half_modes), np.arange(slab_rows), indexing="ij"
    )
    count = part.size
    matrix = np.zeros((count, count), np.float32)
    source = (y * 2 + part) * half_modes + mode
    matrix[np.arange(count), source.ravel()] = 1.0
    return matrix


def gather_rows(half_modes, slab_rows):
    y, mode, part = np.meshgrid(
        np.arange(slab_rows), np.arange(half_modes), np.arange(2), indexing="ij"
    )
    count = part.size
    matrix = np.zeros((2 * count, count), np.float32)
    source = (part * half_modes + mode) * slab_rows + y
    other = ((1 - part) * half_modes + mode) * slab_rows + y
    matrix[np.arange(count), source.ravel()] = 1.0
    matrix[count + np.arange(count), other.ravel()] = np.where(part.ravel() == 0, -1.0, 1.0)
    return matrix


def grow(cos_ref, sin_ref, base, steps, rows):
    cos_ref[0:8, :] = base[0]
    sin_ref[0:8, :] = base[1]
    done = 8
    level = 0
    while done < rows:
        turn_cos = steps[0][level : level + 1, :]
        turn_sin = steps[1][level : level + 1, :]

        def block(index, carry, done=done, turn_cos=turn_cos, turn_sin=turn_sin):
            start = pl.multiple_of(index * 8, 8)
            old_cos = cos_ref[pl.ds(start, 8), :]
            old_sin = sin_ref[pl.ds(start, 8), :]
            cos_ref[pl.ds(done + start, 8), :] = old_cos * turn_cos - old_sin * turn_sin
            sin_ref[pl.ds(done + start, 8), :] = old_sin * turn_cos + old_cos * turn_sin
            return carry

        lax.fori_loop(0, done // 8, block, 0)
        done *= 2
        level += 1


def dot32(a, b):
    return jnp.dot(a, b, preferred_element_type=jnp.float32)


def spread_kernel(
    block_ref,
    group_ref,
    cell_in,
    volume_in,
    rate_in,
    place_in,
    motion_in,
    seen_in,
    base_cos_ref,
    base_sin_ref,
    step_cos_ref,
    step_sin_ref,
    order_ref,
    out_ref,
    field,
    table_cos,
    table_sin,
    table,
    left,
    amounts,
    phases,
    packed,
    cell_ref,
    volume_ref,
    rate_ref,
    place_ref,
    motion_ref,
    seen_ref,
    in_sem,
    out_sem,
    *,
    half_modes,
    pencil_modes,
    pencil_waves,
):
    tiles, size = cell_ref.shape
    strips = NX // CB
    group_rows = 2 * half_modes
    slab_rows = field.shape[1] // (3 * group_rows)
    component_rows = slab_rows * group_rows
    pz_count = half_modes // pencil_modes

    loads = [
        (place_in, place_ref),
        (cell_in, cell_ref),
        (volume_in, volume_ref),
        (rate_in, rate_ref),
        (motion_in, motion_ref),
        (seen_in, seen_ref),
    ]
    loads = [
        pltpu.make_async_copy(source, target, in_sem.at[index])
        for index, (source, target) in enumerate(loads)
    ]
    for load in loads:
        load.start()

    grow(
        table_cos,
        table_sin,
        (base_cos_ref[...], base_sin_ref[...]),
        (step_cos_ref, step_sin_ref),
        POINTS,
    )
    for rest in range(SPLIT):
        lanes = slice(rest * WAVES, (rest + 1) * WAVES)
        table[rest, :, 0:WAVES] = table_cos[:, lanes].astype(jnp.bfloat16)
        table[rest, :, WAVES:] = table_sin[:, lanes].astype(jnp.bfloat16)

    def clear(index, carry):
        field[index] = jnp.zeros(field.shape[1:], jnp.float32)
        return carry

    lax.fori_loop(0, field.shape[0], clear, 0)

    loads[0].wait()
    first = (group_ref[0] * half_modes + 1).astype(jnp.float32)
    for mode, (cosine, sine) in enumerate(turn_modes(place_ref[...], first, half_modes)):
        for piece in range(size // 128):
            lanes = slice(piece * 128, (piece + 1) * 128)
            for part, value in ((0, cosine), (1, -sine)):
                rows = pl.ds(part * half_modes + mode, tiles, stride=group_rows)
                phases[piece, rows, :] = value[:, lanes]

    for load in loads[1:]:
        load.wait()
    upper = cell_ref[...] >= 128
    volume = volume_ref[...]
    pull = volume * rate_ref[...]
    for component in range(3):
        amount = pull * (seen_ref[component] - motion_ref[component])
        if component == 1:
            amount = amount - gravity * volume
        amounts[component] = jnp.where(upper, 0.0, amount)
        amounts[3 + component] = jnp.where(upper, amount, 0.0)

    cells = lax.broadcasted_iota(jnp.int32, (128, size), 0)

    def tile_group(group, carry):
        shares = []
        for offset in range(TILE_GROUP):
            tile = group * TILE_GROUP + offset
            row = pl.ds(tile, 1)
            rows_of_tile = pl.ds(pl.multiple_of(tile * group_rows, 8), group_rows)
            phase = jnp.concatenate(
                [phases[piece, rows_of_tile, :] for piece in range(size // 128)], axis=1
            )
            payload = jnp.concatenate([amounts[k, row, :] * phase for k in range(6)], axis=0)
            spot = cell_ref[row, :] % 128
            one_hot = (spot == cells).astype(jnp.float32).astype(jnp.bfloat16)
            shares.append(
                lax.dot_general(
                    payload.astype(jnp.bfloat16),
                    one_hot,
                    (((1,), (1,)), ((), ())),
                    preferred_element_type=jnp.float32,
                )
            )
        for offset in range(TILE_GROUP):
            block = block_ref[group * TILE_GROUP + offset]
            strip = block % strips
            y = block // strips
            for half in range(2):
                for component in range(3):
                    start = pl.multiple_of(component * component_rows + y * group_rows, 8)
                    own = (half * 3 + component) * group_rows
                    field[strip * 2 + half, pl.ds(start, group_rows), :] += shares[offset][
                        own : own + group_rows
                    ]
        return carry

    lax.fori_loop(0, tiles // TILE_GROUP, tile_group, 0)

    order = order_ref[...]
    def times_minus_i(value):
        lanes = value.shape[1]
        value = value.reshape(slab_rows, group_rows, lanes)
        part = lax.broadcasted_iota(jnp.int32, value.shape, 1) // half_modes
        moved = pltpu.roll(value, half_modes, 1)
        return jnp.where(part == 0, moved, -moved).reshape(component_rows, lanes)

    rest_waves = pencil_waves // SPLIT
    copies = []
    for component in range(3):
        rows = slice(component * component_rows, (component + 1) * component_rows)
        for strip in range(POINTS // 128):
            values = [field[strip + j * (POINTS // 128), rows, :] for j in range(SPLIT)]
            lanes = slice(strip * 128, (strip + 1) * 128)
            even_sum = values[0] + values[2]
            odd_sum = values[1] + values[3]
            even_gap = values[0] - values[2]
            odd_gap = times_minus_i(values[1] - values[3])
            left[0, :, lanes] = (even_sum + odd_sum).astype(jnp.bfloat16)
            left[1, :, lanes] = (even_gap + odd_gap).astype(jnp.bfloat16)
            left[2, :, lanes] = (even_sum - odd_sum).astype(jnp.bfloat16)
            left[3, :, lanes] = (even_gap - odd_gap).astype(jnp.bfloat16)
        spectra = []
        for rest in range(SPLIT):
            product = dot32(left[rest], table[rest])
            spectrum = product[:, :WAVES] + times_minus_i(product[:, WAVES:])
            spectra.append(dot32(order, spectrum.astype(jnp.bfloat16)).astype(jnp.bfloat16))
        for owner_px in range(KX // pencil_waves):
            own = slice(owner_px * rest_waves, (owner_px + 1) * rest_waves)
            joined = jnp.concatenate([spectrum[:, own] for spectrum in spectra], axis=1)
            for part in range(2):
                for mode in range(half_modes):
                    column = (
                        (component * pencil_modes + mode % pencil_modes) * 2 + part
                    ) * pencil_waves
                    row = (part * half_modes + mode) * slab_rows
                    packed[
                        owner_px * pz_count + mode // pencil_modes,
                        :,
                        column : column + pencil_waves,
                    ] = joined[row : row + slab_rows]
        span = 2 * pencil_modes * pencil_waves
        lanes = pl.ds(component * span, span)
        copy = pltpu.make_async_copy(
            packed.at[:, :, lanes], out_ref.at[:, :, lanes], out_sem.at[component]
        )
        copy.start()
        copies.append(copy)
    for copy in copies:
        copy.wait()


def table_kernel(base_cos_ref, base_sin_ref, step_cos_ref, step_sin_ref, out_ref, work_cos, work_sin):
    for rest in range(SPLIT):
        grow(
            work_cos,
            work_sin,
            (base_cos_ref[rest], base_sin_ref[rest]),
            (step_cos_ref, step_sin_ref),
            WAVES,
        )
        out_ref[rest, 0:WAVES, :] = work_cos[...].astype(jnp.bfloat16)
        out_ref[rest, WAVES:, :] = work_sin[...].astype(jnp.bfloat16)


def turn_modes(place, first, modes):
    cos_one = jnp.cos(place)
    sin_one = jnp.sin(place)
    cos_now = jnp.cos(place * first)
    sin_now = jnp.sin(place * first)
    turned = [(cos_now, sin_now)]
    for _ in range(modes - 1):
        cos_now, sin_now = (
            cos_now * cos_one - sin_now * sin_one,
            sin_now * cos_one + cos_now * sin_one,
        )
        turned.append((cos_now, sin_now))
    return turned


def phase_kernel(group_ref, place_ref, out_ref, *, half_modes):
    tiles, size = place_ref.shape
    first = (group_ref[0] * half_modes + 1).astype(jnp.float32)
    for mode, (cosine, sine) in enumerate(turn_modes(place_ref[...], first, half_modes)):
        for piece in range(size // 128):
            lanes = slice(piece * 128, (piece + 1) * 128)
            for part, value in ((0, cosine), (1, -sine)):
                rows = pl.ds(2 * mode + part, tiles, stride=2 * half_modes)
                out_ref[piece, rows, :] = value[:, lanes]


def split(value):
    high = value.astype(jnp.bfloat16)
    return high, (value - high.astype(jnp.float32)).astype(jnp.bfloat16)


def project_kernel(high_ref, low_ref, order_ref, state_ref, out_ref):
    order = order_ref[...]
    state_high, state_low = [
        dot32(value, order).astype(jnp.bfloat16) for value in split(state_ref[...])
    ]
    out_ref[...] = (
        dot32(high_ref[...], state_high)
        + dot32(high_ref[...], state_low)
        + dot32(low_ref[...], state_high)
    )


def solve_kernel(
    inverse_ref,
    basis_high_ref,
    basis_low_ref,
    damping_ref,
    state_ref,
    force_ref,
    out_ref,
    inverse,
    basis,
    damping,
    state,
    pushed,
    modal,
    results,
    sems,
    out_sems,
    *,
    pencil_waves,
):
    rows = inverse.shape[0]
    columns = force_ref.shape[-1]
    step = columns // 3
    slab_shape = out_ref.shape[:2]
    spans = [pl.ds(start, step) for start in range(0, columns, step)]
    loads = [
        (inverse_ref, inverse),
        (state_ref.at[:, spans[0]], state.at[:, spans[0]]),
        (damping_ref, damping),
        (basis_high_ref, basis.at[:, pl.ds(0, rows)]),
        (basis_high_ref, basis.at[:, pl.ds(rows, rows)]),
        (basis_low_ref, basis.at[:, pl.ds(2 * rows, rows)]),
        (state_ref.at[:, spans[1]], state.at[:, spans[1]]),
        (state_ref.at[:, spans[2]], state.at[:, spans[2]]),
    ]
    copies = [
        pltpu.make_async_copy(source, target, sems.at[index])
        for index, (source, target) in enumerate(loads)
    ]
    for copy in copies:
        copy.start()
    copies[0].wait()
    pushed[...] = dot32(inverse[...], force_ref[...].reshape(rows, columns))
    stores = []
    for index in range(3):
        lanes = slice(index * step, (index + 1) * step)
        copies[1 if index == 0 else 5 + index].wait()
        if index == 0:
            copies[2].wait()
        for block in range(step // pencil_waves):
            own = slice(block * pencil_waves, (block + 1) * pencil_waves)
            column = slice(index * step + own.start, index * step + own.stop)
            mode = slice((block // 2) * pencil_waves, (block // 2 + 1) * pencil_waves)
            damped = (state[:, column] + time_step * pushed[:, column]) * damping[:, mode]
            high, low = split(damped)
            modal[0:rows, own] = high
            modal[rows : 2 * rows, own] = low
            modal[2 * rows : 3 * rows, own] = high
        if index == 0:
            for copy in copies[3:6]:
                copy.wait()
        solved = dot32(basis[...], modal[...])
        results[:, :, lanes] = solved.astype(jnp.bfloat16).reshape(slab_shape + (step,))
        copy = pltpu.make_async_copy(
            results.at[:, :, spans[index]], out_ref.at[:, :, spans[index]], out_sems.at[index]
        )
        copy.start()
        stores.append(copy)
    for copy in stores:
        copy.wait()


def merge_rows(values):
    sublane = lax.broadcasted_iota(jnp.int32, (8, 128), 0)
    for bit in (4, 2, 1):
        keep = (sublane & bit) == 0
        half = len(values) // 2
        merged = []
        for index in range(half):
            a, b = values[index], values[index + half]
            own = jnp.where(keep, a, b)
            other = jnp.where(keep, b, a)
            if bit == 4:
                moved = pltpu.roll(other, 4, 0)
            else:
                moved = jnp.where(
                    keep, pltpu.roll(other, 8 - bit, 0), pltpu.roll(other, bit, 0)
                )
            merged.append(own + moved)
        values = merged
    return values[0]


def gather_kernel(
    block_ref,
    cell_ref,
    order_ref,
    table_ref,
    back_ref,
    phase_ref,
    planes_ref,
    part_ref,
    left,
    values,
    planes,
    sampled,
    phases,
    table,
    table_sem,
    phase_sem,
    plane_sem,
    *,
    half_modes,
    pencil_modes,
    pencil_waves,
):
    tiles, size = cell_ref.shape
    strips = NX // CB
    group_rows = 2 * half_modes
    slab_rows = back_ref.shape[1]
    pz_count = half_modes // pencil_modes
    component_rows = group_rows * slab_rows
    table_copies = [
        pltpu.make_async_copy(table_ref.at[rest], table.at[rest], table_sem.at[rest])
        for rest in range(SPLIT)
    ]
    for copy in table_copies:
        copy.start()
    phase_copy = pltpu.make_async_copy(phase_ref, phases, phase_sem)
    phase_copy.start()
    rest_waves = pencil_waves // SPLIT

    def times_i(value):
        shape = value.shape
        value = value.reshape(shape[0] // 8, 8, shape[1])
        part = lax.broadcasted_iota(jnp.int32, value.shape, 1) % 2
        return jnp.where(
            part == 0, -pltpu.roll(value, 7, 1), pltpu.roll(value, 1, 1)
        ).reshape(shape)

    copies = []
    for component in range(3):
        rows = []
        for part in range(2):
            for mode in range(half_modes):
                column = (
                    (component * pencil_modes + mode % pencil_modes) * 2 + part
                ) * pencil_waves
                sources = [
                    back_ref[
                        px * pz_count + mode // pencil_modes, :, column : column + pencil_waves
                    ]
                    for px in range(KX // pencil_waves)
                ]
                rows.append(
                    jnp.concatenate(
                        [
                            source[:, rest * rest_waves : (rest + 1) * rest_waves]
                            for rest in range(SPLIT)
                            for source in sources
                        ],
                        axis=1,
                    )
                )
        turned = dot32(order_ref[...], jnp.concatenate(rows, axis=0)).astype(jnp.bfloat16)
        results = []
        for rest in range(SPLIT):
            lanes = slice(rest * WAVES, (rest + 1) * WAVES)
            left[rest, :, 0:WAVES] = turned[0:component_rows, lanes]
            left[rest, :, WAVES:] = turned[component_rows:, lanes]
            if component == 0:
                table_copies[rest].wait()
            results.append(dot32(left[rest], table[rest]))
        even_sum = results[0] + results[2]
        odd_sum = results[1] + results[3]
        even_gap = results[0] - results[2]
        odd_gap = times_i(results[1] - results[3])
        quarters = [even_sum + odd_sum, even_gap + odd_gap, even_sum - odd_sum, even_gap - odd_gap]
        for side, quarter in enumerate(quarters):
            plane = quarter.astype(jnp.bfloat16)
            whole = plane.astype(jnp.float32)
            planes[:, component, :, :, side * POINTS : (side + 1) * POINTS] = plane.reshape(
                slab_rows, half_modes, 2, POINTS
            )
            for strip in range(POINTS // 128):
                values[
                    side * (POINTS // 128) + strip,
                    component * component_rows : (component + 1) * component_rows,
                    :,
                ] = whole[:, strip * 128 : (strip + 1) * 128]
        copy = pltpu.make_async_copy(
            planes.at[:, component], planes_ref.at[:, component], plane_sem.at[component]
        )
        copy.start()
        copies.append(copy)
    phase_copy.wait()

    def tile_group(group, carry):
        first_tile = pl.multiple_of(group * 8, 8)
        places = []
        for offset in range(8):
            block = block_ref[first_tile + offset]
            places.append((block % strips, block // strips))
        cells = cell_ref[pl.ds(first_tile, 8), :]
        for piece in range(size // 128):
            lanes = slice(piece * 128, (piece + 1) * 128)
            weighted = [[], [], []]
            for offset in range(8):
                strip, y = places[offset]
                cell = jnp.broadcast_to(cells[offset : offset + 1, lanes], (group_rows, 128))
                spot = cell % 128
                upper = cell >= 128
                rows_of_tile = pl.multiple_of((first_tile + offset) * group_rows, 8)
                phase = phases[piece, pl.ds(rows_of_tile, group_rows), :]
                for component in range(3):
                    start = pl.multiple_of(component * component_rows + y * group_rows, 8)
                    rows = pl.ds(start, group_rows)
                    low = jnp.take_along_axis(values[strip * 2, rows, :], spot, axis=1)
                    high = jnp.take_along_axis(values[strip * 2 + 1, rows, :], spot, axis=1)
                    product = jnp.where(upper, high, low) * phase
                    total = product[0:8]
                    for more in range(8, group_rows, 8):
                        total = total + product[more : more + 8]
                    weighted[component].append(total)
            for component in range(3):
                sampled[component, pl.ds(first_tile, 8), lanes] = merge_rows(weighted[component])
        return carry

    lax.fori_loop(0, tiles // 8, tile_group, 0)
    part_ref[...] = sampled[...].astype(jnp.bfloat16)
    for copy in copies:
        copy.wait()


def on_device(
    cell_index,
    block_index,
    volume,
    response_rate,
    spanwise_position,
    particle_velocity,
    seen_velocity,
    fluid_velocity,
    eigen_basis,
    eigen_inverse,
    eigenvalues,
):
    group_index = lax.axis_index("grp")
    px_count = lax.axis_size("px")
    pz_count = lax.axis_size("pz")
    rows = fluid_velocity.shape[0]
    pencil_modes = fluid_velocity.shape[2]
    pencil_waves = fluid_velocity.shape[4]
    half_modes = pencil_modes * pz_count
    slabs = px_count * pz_count
    slab_rows = rows // slabs
    strips = NX // CB
    tiles, size = cell_index.shape
    width = 6 * half_modes
    component_rows = 2 * half_modes * slab_rows
    columns = 6 * pencil_modes * pencil_waves
    pencil = pencil_modes * pencil_waves
    sizes = dict(half_modes=half_modes, pencil_modes=pencil_modes, pencil_waves=pencil_waves)

    vmem = pl.BlockSpec(memory_space=pltpu.VMEM)
    smem = pl.BlockSpec(memory_space=pltpu.SMEM)
    hbm = pl.BlockSpec(memory_space=pltpu.HBM)
    in_hbm = functools.partial(pltpu.with_memory_space_constraint, memory_space=pltpu.HBM)
    phase_shape = (size // 128, tiles * 2 * half_modes, 128)

    group = group_index.reshape(1).astype(jnp.int32)
    outgoing = pl.pallas_call(
        functools.partial(spread_kernel, **sizes),
        out_shape=jax.ShapeDtypeStruct((slabs, slab_rows, columns), jnp.bfloat16),
        in_specs=[smem, smem] + [hbm] * 6 + [vmem] * 5,
        out_specs=hbm,
        scratch_shapes=[
            pltpu.VMEM((NX // 128, slab_rows * width, 128), jnp.float32),
            pltpu.VMEM((POINTS, KX), jnp.float32),
            pltpu.VMEM((POINTS, KX), jnp.float32),
            pltpu.VMEM((SPLIT, POINTS, 2 * WAVES), jnp.bfloat16),
            pltpu.VMEM((SPLIT, component_rows, POINTS), jnp.bfloat16),
            pltpu.VMEM((6, tiles, size), jnp.float32),
            pltpu.VMEM(phase_shape, jnp.float32),
            pltpu.VMEM((slabs, slab_rows, columns), jnp.bfloat16),
            pltpu.VMEM((tiles, size), jnp.int32),
        ]
        + [pltpu.VMEM((tiles, size), jnp.float32)] * 3
        + [pltpu.VMEM((3, tiles, size), jnp.float32)] * 2
        + [pltpu.SemaphoreType.DMA((6,)), pltpu.SemaphoreType.DMA((3,))],
        name="spread",
    )(
        block_index,
        group,
        cell_index,
        volume,
        response_rate,
        spanwise_position,
        particle_velocity,
        seen_velocity,
        *[jnp.asarray(seed) for seed in forward_seeds()],
        jnp.asarray(spread_rows(half_modes, slab_rows), jnp.bfloat16),
    )
    force = lax.all_to_all(outgoing, ("px", "pz"), split_axis=0, concat_axis=0, tiled=True)

    def halves(matrix):
        high = lax.reduce_precision(matrix, 8, 7)
        return high.astype(jnp.bfloat16), (matrix - high).astype(jnp.bfloat16)

    inverse_high, inverse_low = halves(eigen_inverse)
    basis_high, basis_low = halves(eigen_basis)
    state = fluid_velocity.transpose(0, 1, 2, 3, 4).reshape(rows, columns)
    square = pl.BlockSpec((rows, rows), lambda i: (0, 0))
    strip_spec = pl.BlockSpec((rows, pencil_waves), lambda i: (0, i))
    projected = pl.pallas_call(
        project_kernel,
        grid=(columns // pencil_waves,),
        out_shape=jax.ShapeDtypeStruct((rows, columns), jnp.float32),
        in_specs=[
            square,
            square,
            pl.BlockSpec((pencil_waves, pencil_waves), lambda i: (0, 0)),
            strip_spec,
        ],
        out_specs=strip_spec,
        compiler_params=pltpu.CompilerParams(vmem_limit_bytes=24 << 20),
        name="project",
    )(inverse_high, inverse_low, jnp.asarray(order_matrix(pencil_waves), jnp.bfloat16), state)
    lane = jnp.arange(pencil_waves)
    rest_waves = pencil_waves // SPLIT
    wave = SPLIT * (lane % rest_waves) + lane // rest_waves
    stream_wave = (lax.axis_index("px") * pencil_waves + wave - KX // 2).astype(jnp.float32) * 0.5
    span_wave = (
        group_index * half_modes
        + lax.axis_index("pz") * pencil_modes
        + jnp.arange(pencil_modes)
        + 1
    ).astype(jnp.float32)
    wave_square = (
        stream_wave[None, :] * stream_wave[None, :] + span_wave[:, None] * span_wave[:, None]
    )
    wave_square = jnp.broadcast_to(
        wave_square[None, :, None, :], (3, pencil_modes, 2, pencil_waves)
    ).reshape(1, columns)
    damping = 1.0 / (1.0 + viscosity * (eigenvalues[:, None] + wave_square))
    table = pl.pallas_call(
        table_kernel,
        out_shape=jax.ShapeDtypeStruct((SPLIT, 2 * WAVES, POINTS), jnp.bfloat16),
        in_specs=[vmem] * 4,
        out_specs=vmem,
        scratch_shapes=[pltpu.VMEM((WAVES, POINTS), jnp.float32)] * 2,
        compiler_params=pltpu.CompilerParams(vmem_limit_bytes=24 << 20),
        name="waves",
    )(*[jnp.asarray(seed) for seed in inverse_seeds()])

    phases = pl.pallas_call(
        functools.partial(phase_kernel, half_modes=half_modes),
        out_shape=jax.ShapeDtypeStruct(phase_shape, jnp.float32),
        in_specs=[smem, vmem],
        out_specs=vmem,
        compiler_params=pltpu.CompilerParams(vmem_limit_bytes=24 << 20),
        name="phases",
    )(group, spanwise_position)

    pushed = jnp.dot(
        inverse_high, force.reshape(rows, columns), preferred_element_type=jnp.float32
    )
    modal = (projected + time_step * pushed) * damping
    solved = jnp.dot(eigen_basis, modal, precision=lax.Precision.HIGH).astype(jnp.bfloat16)
    solved = solved.reshape(slabs, slab_rows, columns)
    returned = lax.all_to_all(solved, ("px", "pz"), split_axis=0, concat_axis=0, tiled=True)
    velocity_planes, mode_part = pl.pallas_call(
        functools.partial(gather_kernel, **sizes),
        out_shape=(
            jax.ShapeDtypeStruct((slab_rows, 3, half_modes, 2, NX), jnp.bfloat16),
            jax.ShapeDtypeStruct((3, tiles, size), jnp.bfloat16),
        ),
        in_specs=[smem, vmem, vmem, hbm, vmem, hbm],
        out_specs=(hbm, vmem),
        scratch_shapes=[
            pltpu.VMEM((SPLIT, component_rows, 2 * WAVES), jnp.bfloat16),
            pltpu.VMEM((NX // 128, slab_rows * width, 128), jnp.float32),
            pltpu.VMEM((slab_rows, 3, half_modes, 2, NX), jnp.bfloat16),
            pltpu.VMEM((3, tiles, size), jnp.float32),
            pltpu.VMEM(phase_shape, jnp.float32),
            pltpu.VMEM((SPLIT, 2 * WAVES, POINTS), jnp.bfloat16),
            pltpu.SemaphoreType.DMA((SPLIT,)),
            pltpu.SemaphoreType.DMA,
            pltpu.SemaphoreType.DMA((3,)),
        ],
        compiler_params=pltpu.CompilerParams(vmem_limit_bytes=40 << 20),
        name="gather",
    )(
        block_index,
        cell_index,
        jnp.asarray(gather_rows(half_modes, slab_rows), jnp.bfloat16),
        in_hbm(table),
        returned,
        in_hbm(phases),
    )
    other_part = lax.ppermute(mode_part, "grp", [(0, 1), (1, 0)])
    fluid_at = mode_part.astype(jnp.float32) + other_part.astype(jnp.float32)
    upward = (jnp.arange(3) == 1).astype(jnp.float32)[:, None, None]
    updated_velocity = (
        particle_velocity
        + time_step * response_rate * (fluid_at - particle_velocity)
        - time_step * gravity * upward
    )
    return (velocity_planes, updated_velocity)


def solution(mesh):
    in_specs = (
        P(("px", "pz"), None),
        P(("px", "pz")),
        P(("px", "pz"), None),
        P(("px", "pz"), None),
        P(("px", "pz"), None),
        P(None, ("px", "pz"), None),
        P(None, ("px", "pz"), None),
        P(None, None, ("grp", "pz"), None, "px"),
        P(),
        P(),
        P(),
    )
    out_specs = (P(("px", "pz"), None, "grp", None, None), P(None, ("px", "pz"), None))
    return jax.shard_map(
        on_device, mesh=mesh, in_specs=in_specs, out_specs=out_specs, check_vma=False
    )
```

```python
import functools
import math

import jax
import jax.numpy as jnp
import numpy as np
from jax import lax
from jax.experimental import pallas as pl
from jax.experimental.pallas import tpu as pltpu
from jax.sharding import PartitionSpec as P

NX = 2048
KX = 1024
CB = 256
SPLIT = 4
POINTS = NX // SPLIT
WAVES = KX // SPLIT
TILE_GROUP = 8

time_step = 0.5
gravity = 0.8
viscosity = 0.0001


def turns(rows, columns):
    phase = np.mod(np.asarray(rows)[:, None] * np.asarray(columns)[None, :], NX)
    angles = phase.astype(np.float64) * (2.0 * math.pi / NX)
    return np.cos(angles).astype(np.float32), np.sin(angles).astype(np.float32)


def forward_seeds():
    waves = np.concatenate([SPLIT * np.arange(WAVES) + rest - KX // 2 for rest in range(SPLIT)])
    base = turns(np.arange(8), waves)
    steps = turns(8 * 2 ** np.arange(8), waves)
    scale = np.float32(1.0 / math.sqrt(NX))
    return [base[0] * scale, base[1] * scale, steps[0], steps[1]]


def inverse_seeds():
    points = np.arange(POINTS)
    bases = [
        turns(SPLIT * np.arange(8) + rest - KX // 2, points) for rest in range(SPLIT)
    ]
    steps = turns(8 * SPLIT * 2 ** np.arange(8), points)
    scale = np.float32(1.0 / math.sqrt(NX))
    cosines = np.stack([b[0] for b in bases]) * scale
    sines = np.stack([b[1] for b in bases]) * scale
    return [cosines, sines, steps[0], steps[1]]


def order_matrix(waves):
    matrix = np.zeros((waves, waves), np.float32)
    lanes = np.arange(waves)
    span = waves // SPLIT
    matrix[SPLIT * (lanes % span) + lanes // span, lanes] = 1.0
    return matrix


def spread_rows(half_modes, slab_rows):
    part, mode, y = np.meshgrid(
        np.arange(2), np.arange(half_modes), np.arange(slab_rows), indexing="ij"
    )
    count = part.size
    matrix = np.zeros((count, count), np.float32)
    source = (y * 2 + part) * half_modes + mode
    matrix[np.arange(count), source.ravel()] = 1.0
    return matrix


def gather_rows(half_modes, slab_rows):
    y, mode, part = np.meshgrid(
        np.arange(slab_rows), np.arange(half_modes), np.arange(2), indexing="ij"
    )
    count = part.size
    matrix = np.zeros((2 * count, count), np.float32)
    source = (part * half_modes + mode) * slab_rows + y
    other = ((1 - part) * half_modes + mode) * slab_rows + y
    matrix[np.arange(count), source.ravel()] = 1.0
    matrix[count + np.arange(count), other.ravel()] = np.where(part.ravel() == 0, -1.0, 1.0)
    return matrix


def grow(cos_ref, sin_ref, base, steps, rows):
    cos_ref[0:8, :] = base[0]
    sin_ref[0:8, :] = base[1]
    done = 8
    level = 0
    while done < rows:
        turn_cos = steps[0][level : level + 1, :]
        turn_sin = steps[1][level : level + 1, :]

        def block(index, carry, done=done, turn_cos=turn_cos, turn_sin=turn_sin):
            start = pl.multiple_of(index * 8, 8)
            old_cos = cos_ref[pl.ds(start, 8), :]
            old_sin = sin_ref[pl.ds(start, 8), :]
            cos_ref[pl.ds(done + start, 8), :] = old_cos * turn_cos - old_sin * turn_sin
            sin_ref[pl.ds(done + start, 8), :] = old_sin * turn_cos + old_cos * turn_sin
            return carry

        lax.fori_loop(0, done // 8, block, 0)
        done *= 2
        level += 1


def dot32(a, b):
    return jnp.dot(a, b, preferred_element_type=jnp.float32)


def spread_kernel(
    block_ref,
    group_ref,
    cell_in,
    volume_in,
    rate_in,
    place_in,
    motion_in,
    seen_in,
    base_cos_ref,
    base_sin_ref,
    step_cos_ref,
    step_sin_ref,
    order_ref,
    out_ref,
    field,
    table_cos,
    table_sin,
    table,
    left,
    amounts,
    phases,
    packed,
    cell_ref,
    volume_ref,
    rate_ref,
    place_ref,
    motion_ref,
    seen_ref,
    in_sem,
    out_sem,
    *,
    half_modes,
    pencil_modes,
    pencil_waves,
):
    tiles, size = cell_ref.shape
    strips = NX // CB
    group_rows = 2 * half_modes
    slab_rows = field.shape[1] // (3 * group_rows)
    component_rows = slab_rows * group_rows
    pz_count = half_modes // pencil_modes

    loads = [
        (place_in, place_ref),
        (cell_in, cell_ref),
        (volume_in, volume_ref),
        (rate_in, rate_ref),
        (motion_in, motion_ref),
        (seen_in, seen_ref),
    ]
    loads = [
        pltpu.make_async_copy(source, target, in_sem.at[index])
        for index, (source, target) in enumerate(loads)
    ]
    for load in loads:
        load.start()

    grow(
        table_cos,
        table_sin,
        (base_cos_ref[...], base_sin_ref[...]),
        (step_cos_ref, step_sin_ref),
        POINTS,
    )
    for rest in range(SPLIT):
        lanes = slice(rest * WAVES, (rest + 1) * WAVES)
        table[rest, :, 0:WAVES] = table_cos[:, lanes].astype(jnp.bfloat16)
        table[rest, :, WAVES:] = table_sin[:, lanes].astype(jnp.bfloat16)

    def clear(index, carry):
        field[index] = jnp.zeros(field.shape[1:], jnp.float32)
        return carry

    lax.fori_loop(0, field.shape[0], clear, 0)

    loads[0].wait()
    first = (group_ref[0] * half_modes + 1).astype(jnp.float32)
    for mode, (cosine, sine) in enumerate(turn_modes(place_ref[...], first, half_modes)):
        for piece in range(size // 128):
            lanes = slice(piece * 128, (piece + 1) * 128)
            for part, value in ((0, cosine), (1, -sine)):
                rows = pl.ds(part * half_modes + mode, tiles, stride=group_rows)
                phases[piece, rows, :] = value[:, lanes]

    for load in loads[1:]:
        load.wait()
    upper = cell_ref[...] >= 128
    volume = volume_ref[...]
    pull = volume * rate_ref[...]
    for component in range(3):
        amount = pull * (seen_ref[component] - motion_ref[component])
        if component == 1:
            amount = amount - gravity * volume
        amounts[component] = jnp.where(upper, 0.0, amount)
        amounts[3 + component] = jnp.where(upper, amount, 0.0)

    cells = lax.broadcasted_iota(jnp.int32, (128, size), 0)

    def tile_group(group, carry):
        shares = []
        for offset in range(TILE_GROUP):
            tile = group * TILE_GROUP + offset
            row = pl.ds(tile, 1)
            rows_of_tile = pl.ds(pl.multiple_of(tile * group_rows, 8), group_rows)
            phase = jnp.concatenate(
                [phases[piece, rows_of_tile, :] for piece in range(size // 128)], axis=1
            )
            payload = jnp.concatenate([amounts[k, row, :] * phase for k in range(6)], axis=0)
            spot = cell_ref[row, :] % 128
            one_hot = (spot == cells).astype(jnp.float32).astype(jnp.bfloat16)
            shares.append(
                lax.dot_general(
                    payload.astype(jnp.bfloat16),
                    one_hot,
                    (((1,), (1,)), ((), ())),
                    preferred_element_type=jnp.float32,
                )
            )
        for offset in range(TILE_GROUP):
            block = block_ref[group * TILE_GROUP + offset]
            strip = block % strips
            y = block // strips
            for half in range(2):
                for component in range(3):
                    start = pl.multiple_of(component * component_rows + y * group_rows, 8)
                    own = (half * 3 + component) * group_rows
                    field[strip * 2 + half, pl.ds(start, group_rows), :] += shares[offset][
                        own : own + group_rows
                    ]
        return carry

    lax.fori_loop(0, tiles // TILE_GROUP, tile_group, 0)

    order = order_ref[...]
    def times_minus_i(value):
        lanes = value.shape[1]
        rows = value.shape[0]
        value = value.reshape(rows // group_rows, group_rows, lanes)
        part = lax.broadcasted_iota(jnp.int32, value.shape, 1) // half_modes
        moved = pltpu.roll(value, half_modes, 1)
        return jnp.where(part == 0, moved, -moved).reshape(rows, lanes)

    rest_waves = pencil_waves // SPLIT
    for strip in range(POINTS // 128):
        values = [field[strip + j * (POINTS // 128)] for j in range(SPLIT)]
        lanes = slice(strip * 128, (strip + 1) * 128)
        even_sum = values[0] + values[2]
        odd_sum = values[1] + values[3]
        even_gap = values[0] - values[2]
        odd_gap = times_minus_i(values[1] - values[3])
        left[0, :, lanes] = (even_sum + odd_sum).astype(jnp.bfloat16)
        left[1, :, lanes] = (even_gap + odd_gap).astype(jnp.bfloat16)
        left[2, :, lanes] = (even_sum - odd_sum).astype(jnp.bfloat16)
        left[3, :, lanes] = (even_gap - odd_gap).astype(jnp.bfloat16)
    all_spectra = []
    for rest in range(SPLIT):
        product = dot32(left[rest], table[rest])
        spectrum = product[:, :WAVES] + times_minus_i(product[:, WAVES:])
        all_spectra.append(spectrum.astype(jnp.bfloat16))
    copies = []
    for component in range(3):
        rows = slice(component * component_rows, (component + 1) * component_rows)
        spectra = [
            dot32(order, spectrum[rows]).astype(jnp.bfloat16) for spectrum in all_spectra
        ]
        for owner_px in range(KX // pencil_waves):
            own = slice(owner_px * rest_waves, (owner_px + 1) * rest_waves)
            joined = jnp.concatenate([spectrum[:, own] for spectrum in spectra], axis=1)
            for part in range(2):
                for mode in range(half_modes):
                    column = (
                        (component * pencil_modes + mode % pencil_modes) * 2 + part
                    ) * pencil_waves
                    row = (part * half_modes + mode) * slab_rows
                    packed[
                        owner_px * pz_count + mode // pencil_modes,
                        :,
                        column : column + pencil_waves,
                    ] = joined[row : row + slab_rows]
        span = 2 * pencil_modes * pencil_waves
        lanes = pl.ds(component * span, span)
        copy = pltpu.make_async_copy(
            packed.at[:, :, lanes], out_ref.at[:, :, lanes], out_sem.at[component]
        )
        copy.start()
        copies.append(copy)
    for copy in copies:
        copy.wait()


def table_kernel(base_cos_ref, base_sin_ref, step_cos_ref, step_sin_ref, out_ref, work_cos, work_sin):
    for rest in range(SPLIT):
        grow(
            work_cos,
            work_sin,
            (base_cos_ref[rest], base_sin_ref[rest]),
            (step_cos_ref, step_sin_ref),
            WAVES,
        )
        out_ref[rest, 0:WAVES, :] = work_cos[...].astype(jnp.bfloat16)
        out_ref[rest, WAVES:, :] = work_sin[...].astype(jnp.bfloat16)


def turn_modes(place, first, modes):
    cos_one = jnp.cos(place)
    sin_one = jnp.sin(place)
    cos_now = jnp.cos(place * first)
    sin_now = jnp.sin(place * first)
    turned = [(cos_now, sin_now)]
    for _ in range(modes - 1):
        cos_now, sin_now = (
            cos_now * cos_one - sin_now * sin_one,
            sin_now * cos_one + cos_now * sin_one,
        )
        turned.append((cos_now, sin_now))
    return turned


def phase_kernel(group_ref, place_ref, out_ref, *, half_modes):
    tiles, size = place_ref.shape
    first = (group_ref[0] * half_modes + 1).astype(jnp.float32)
    for mode, (cosine, sine) in enumerate(turn_modes(place_ref[...], first, half_modes)):
        for piece in range(size // 128):
            lanes = slice(piece * 128, (piece + 1) * 128)
            for part, value in ((0, cosine), (1, -sine)):
                rows = pl.ds(2 * mode + part, tiles, stride=2 * half_modes)
                out_ref[piece, rows, :] = value[:, lanes]


def split(value):
    high = value.astype(jnp.bfloat16)
    return high, (value - high.astype(jnp.float32)).astype(jnp.bfloat16)


def project_kernel(high_ref, low_ref, order_ref, state_ref, out_ref):
    order = order_ref[...]
    state_high, state_low = [
        dot32(value, order).astype(jnp.bfloat16) for value in split(state_ref[...])
    ]
    out_ref[...] = (
        dot32(high_ref[...], state_high)
        + dot32(high_ref[...], state_low)
        + dot32(low_ref[...], state_high)
    )


def solve_kernel(
    inverse_ref,
    basis_high_ref,
    basis_low_ref,
    damping_ref,
    state_ref,
    force_ref,
    out_ref,
    inverse,
    basis,
    damping,
    state,
    pushed,
    modal,
    results,
    sems,
    out_sems,
    *,
    pencil_waves,
):
    rows = inverse.shape[0]
    columns = force_ref.shape[-1]
    step = columns // 3
    slab_shape = out_ref.shape[:2]
    spans = [pl.ds(start, step) for start in range(0, columns, step)]
    loads = [
        (inverse_ref, inverse),
        (state_ref.at[:, spans[0]], state.at[:, spans[0]]),
        (damping_ref, damping),
        (basis_high_ref, basis.at[:, pl.ds(0, rows)]),
        (basis_high_ref, basis.at[:, pl.ds(rows, rows)]),
        (basis_low_ref, basis.at[:, pl.ds(2 * rows, rows)]),
        (state_ref.at[:, spans[1]], state.at[:, spans[1]]),
        (state_ref.at[:, spans[2]], state.at[:, spans[2]]),
    ]
    copies = [
        pltpu.make_async_copy(source, target, sems.at[index])
        for index, (source, target) in enumerate(loads)
    ]
    for copy in copies:
        copy.start()
    copies[0].wait()
    pushed[...] = dot32(inverse[...], force_ref[...].reshape(rows, columns))
    stores = []
    for index in range(3):
        lanes = slice(index * step, (index + 1) * step)
        copies[1 if index == 0 else 5 + index].wait()
        if index == 0:
            copies[2].wait()
        for block in range(step // pencil_waves):
            own = slice(block * pencil_waves, (block + 1) * pencil_waves)
            column = slice(index * step + own.start, index * step + own.stop)
            mode = slice((block // 2) * pencil_waves, (block // 2 + 1) * pencil_waves)
            damped = (state[:, column] + time_step * pushed[:, column]) * damping[:, mode]
            high, low = split(damped)
            modal[0:rows, own] = high
            modal[rows : 2 * rows, own] = low
            modal[2 * rows : 3 * rows, own] = high
        if index == 0:
            for copy in copies[3:6]:
                copy.wait()
        solved = dot32(basis[...], modal[...])
        results[:, :, lanes] = solved.astype(jnp.bfloat16).reshape(slab_shape + (step,))
        copy = pltpu.make_async_copy(
            results.at[:, :, spans[index]], out_ref.at[:, :, spans[index]], out_sems.at[index]
        )
        copy.start()
        stores.append(copy)
    for copy in stores:
        copy.wait()


def merge_rows(values):
    sublane = lax.broadcasted_iota(jnp.int32, (8, 128), 0)
    for bit in (4, 2, 1):
        keep = (sublane & bit) == 0
        half = len(values) // 2
        merged = []
        for index in range(half):
            a, b = values[index], values[index + half]
            own = jnp.where(keep, a, b)
            other = jnp.where(keep, b, a)
            if bit == 4:
                moved = pltpu.roll(other, 4, 0)
            else:
                moved = jnp.where(
                    keep, pltpu.roll(other, 8 - bit, 0), pltpu.roll(other, bit, 0)
                )
            merged.append(own + moved)
        values = merged
    return values[0]


def gather_kernel(
    block_ref,
    cell_ref,
    order_ref,
    table_ref,
    back_ref,
    phase_ref,
    planes_ref,
    part_ref,
    left,
    values,
    planes,
    sampled,
    phases,
    table,
    table_sem,
    phase_sem,
    plane_sem,
    *,
    half_modes,
    pencil_modes,
    pencil_waves,
):
    tiles, size = cell_ref.shape
    strips = NX // CB
    group_rows = 2 * half_modes
    slab_rows = back_ref.shape[1]
    pz_count = half_modes // pencil_modes
    component_rows = group_rows * slab_rows
    table_copies = [
        pltpu.make_async_copy(table_ref.at[rest], table.at[rest], table_sem.at[rest])
        for rest in range(SPLIT)
    ]
    for copy in table_copies:
        copy.start()
    phase_copy = pltpu.make_async_copy(phase_ref, phases, phase_sem)
    phase_copy.start()
    rest_waves = pencil_waves // SPLIT

    def times_i(value):
        shape = value.shape
        value = value.reshape(shape[0] // 8, 8, shape[1])
        part = lax.broadcasted_iota(jnp.int32, value.shape, 1) % 2
        return jnp.where(
            part == 0, -pltpu.roll(value, 7, 1), pltpu.roll(value, 1, 1)
        ).reshape(shape)

    copies = []
    for component in range(3):
        rows = []
        for part in range(2):
            for mode in range(half_modes):
                column = (
                    (component * pencil_modes + mode % pencil_modes) * 2 + part
                ) * pencil_waves
                sources = [
                    back_ref[
                        px * pz_count + mode // pencil_modes, :, column : column + pencil_waves
                    ]
                    for px in range(KX // pencil_waves)
                ]
                rows.append(
                    jnp.concatenate(
                        [
                            source[:, rest * rest_waves : (rest + 1) * rest_waves]
                            for rest in range(SPLIT)
                            for source in sources
                        ],
                        axis=1,
                    )
                )
        turned = dot32(order_ref[...], jnp.concatenate(rows, axis=0)).astype(jnp.bfloat16)
        results = []
        for rest in range(SPLIT):
            lanes = slice(rest * WAVES, (rest + 1) * WAVES)
            left[rest, :, 0:WAVES] = turned[0:component_rows, lanes]
            left[rest, :, WAVES:] = turned[component_rows:, lanes]
            if component == 0:
                table_copies[rest].wait()
            results.append(dot32(left[rest], table[rest]))
        even_sum = results[0] + results[2]
        odd_sum = results[1] + results[3]
        even_gap = results[0] - results[2]
        odd_gap = times_i(results[1] - results[3])
        quarters = [even_sum + odd_sum, even_gap + odd_gap, even_sum - odd_sum, even_gap - odd_gap]
        for side, quarter in enumerate(quarters):
            plane = quarter.astype(jnp.bfloat16)
            whole = plane.astype(jnp.float32)
            planes[:, component, :, :, side * POINTS : (side + 1) * POINTS] = plane.reshape(
                slab_rows, half_modes, 2, POINTS
            )
            for strip in range(POINTS // 128):
                values[
                    side * (POINTS // 128) + strip,
                    component * component_rows : (component + 1) * component_rows,
                    :,
                ] = whole[:, strip * 128 : (strip + 1) * 128]
        copy = pltpu.make_async_copy(
            planes.at[:, component], planes_ref.at[:, component], plane_sem.at[component]
        )
        copy.start()
        copies.append(copy)
    phase_copy.wait()

    def tile_group(group, carry):
        first_tile = pl.multiple_of(group * 8, 8)
        places = []
        for offset in range(8):
            block = block_ref[first_tile + offset]
            places.append((block % strips, block // strips))
        cells = cell_ref[pl.ds(first_tile, 8), :]
        for piece in range(size // 128):
            lanes = slice(piece * 128, (piece + 1) * 128)
            weighted = [[], [], []]
            for offset in range(8):
                strip, y = places[offset]
                cell = jnp.broadcast_to(cells[offset : offset + 1, lanes], (group_rows, 128))
                spot = cell % 128
                upper = cell >= 128
                rows_of_tile = pl.multiple_of((first_tile + offset) * group_rows, 8)
                phase = phases[piece, pl.ds(rows_of_tile, group_rows), :]
                for component in range(3):
                    start = pl.multiple_of(component * component_rows + y * group_rows, 8)
                    rows = pl.ds(start, group_rows)
                    low = jnp.take_along_axis(values[strip * 2, rows, :], spot, axis=1)
                    high = jnp.take_along_axis(values[strip * 2 + 1, rows, :], spot, axis=1)
                    product = jnp.where(upper, high, low) * phase
                    total = product[0:8]
                    for more in range(8, group_rows, 8):
                        total = total + product[more : more + 8]
                    weighted[component].append(total)
            for component in range(3):
                sampled[component, pl.ds(first_tile, 8), lanes] = merge_rows(weighted[component])
        return carry

    lax.fori_loop(0, tiles // 8, tile_group, 0)
    part_ref[...] = sampled[...].astype(jnp.bfloat16)
    for copy in copies:
        copy.wait()


def on_device(
    cell_index,
    block_index,
    volume,
    response_rate,
    spanwise_position,
    particle_velocity,
    seen_velocity,
    fluid_velocity,
    eigen_basis,
    eigen_inverse,
    eigenvalues,
):
    group_index = lax.axis_index("grp")
    px_count = lax.axis_size("px")
    pz_count = lax.axis_size("pz")
    rows = fluid_velocity.shape[0]
    pencil_modes = fluid_velocity.shape[2]
    pencil_waves = fluid_velocity.shape[4]
    half_modes = pencil_modes * pz_count
    slabs = px_count * pz_count
    slab_rows = rows // slabs
    strips = NX // CB
    tiles, size = cell_index.shape
    width = 6 * half_modes
    component_rows = 2 * half_modes * slab_rows
    columns = 6 * pencil_modes * pencil_waves
    pencil = pencil_modes * pencil_waves
    sizes = dict(half_modes=half_modes, pencil_modes=pencil_modes, pencil_waves=pencil_waves)

    vmem = pl.BlockSpec(memory_space=pltpu.VMEM)
    smem = pl.BlockSpec(memory_space=pltpu.SMEM)
    hbm = pl.BlockSpec(memory_space=pltpu.HBM)
    in_hbm = functools.partial(pltpu.with_memory_space_constraint, memory_space=pltpu.HBM)
    phase_shape = (size // 128, tiles * 2 * half_modes, 128)

    group = group_index.reshape(1).astype(jnp.int32)
    outgoing = pl.pallas_call(
        functools.partial(spread_kernel, **sizes),
        out_shape=jax.ShapeDtypeStruct((slabs, slab_rows, columns), jnp.bfloat16),
        in_specs=[smem, smem] + [hbm] * 6 + [vmem] * 5,
        out_specs=hbm,
        scratch_shapes=[
            pltpu.VMEM((NX // 128, slab_rows * width, 128), jnp.float32),
            pltpu.VMEM((POINTS, KX), jnp.float32),
            pltpu.VMEM((POINTS, KX), jnp.float32),
            pltpu.VMEM((SPLIT, POINTS, 2 * WAVES), jnp.bfloat16),
            pltpu.VMEM((SPLIT, 3 * component_rows, POINTS), jnp.bfloat16),
            pltpu.VMEM((6, tiles, size), jnp.float32),
            pltpu.VMEM(phase_shape, jnp.float32),
            pltpu.VMEM((slabs, slab_rows, columns), jnp.bfloat16),
            pltpu.VMEM((tiles, size), jnp.int32),
        ]
        + [pltpu.VMEM((tiles, size), jnp.float32)] * 3
        + [pltpu.VMEM((3, tiles, size), jnp.float32)] * 2
        + [pltpu.SemaphoreType.DMA((6,)), pltpu.SemaphoreType.DMA((3,))],
        name="spread",
    )(
        block_index,
        group,
        cell_index,
        volume,
        response_rate,
        spanwise_position,
        particle_velocity,
        seen_velocity,
        *[jnp.asarray(seed) for seed in forward_seeds()],
        jnp.asarray(spread_rows(half_modes, slab_rows), jnp.bfloat16),
    )
    force = lax.all_to_all(outgoing, ("px", "pz"), split_axis=0, concat_axis=0, tiled=True)

    def halves(matrix):
        high = lax.reduce_precision(matrix, 8, 7)
        return high.astype(jnp.bfloat16), (matrix - high).astype(jnp.bfloat16)

    inverse_high, inverse_low = halves(eigen_inverse)
    basis_high, basis_low = halves(eigen_basis)
    state = fluid_velocity.transpose(0, 1, 2, 3, 4).reshape(rows, columns)
    square = pl.BlockSpec((rows, rows), lambda i: (0, 0))
    strip_spec = pl.BlockSpec((rows, pencil_waves), lambda i: (0, i))
    projected = pl.pallas_call(
        project_kernel,
        grid=(columns // pencil_waves,),
        out_shape=jax.ShapeDtypeStruct((rows, columns), jnp.float32),
        in_specs=[
            square,
            square,
            pl.BlockSpec((pencil_waves, pencil_waves), lambda i: (0, 0)),
            strip_spec,
        ],
        out_specs=strip_spec,
        compiler_params=pltpu.CompilerParams(vmem_limit_bytes=24 << 20),
        name="project",
    )(inverse_high, inverse_low, jnp.asarray(order_matrix(pencil_waves), jnp.bfloat16), state)
    lane = jnp.arange(pencil_waves)
    rest_waves = pencil_waves // SPLIT
    wave = SPLIT * (lane % rest_waves) + lane // rest_waves
    stream_wave = (lax.axis_index("px") * pencil_waves + wave - KX // 2).astype(jnp.float32) * 0.5
    span_wave = (
        group_index * half_modes
        + lax.axis_index("pz") * pencil_modes
        + jnp.arange(pencil_modes)
        + 1
    ).astype(jnp.float32)
    wave_square = (
        stream_wave[None, :] * stream_wave[None, :] + span_wave[:, None] * span_wave[:, None]
    )
    wave_square = jnp.broadcast_to(
        wave_square[None, :, None, :], (3, pencil_modes, 2, pencil_waves)
    ).reshape(1, columns)
    damping = 1.0 / (1.0 + viscosity * (eigenvalues[:, None] + wave_square))
    table = pl.pallas_call(
        table_kernel,
        out_shape=jax.ShapeDtypeStruct((SPLIT, 2 * WAVES, POINTS), jnp.bfloat16),
        in_specs=[vmem] * 4,
        out_specs=vmem,
        scratch_shapes=[pltpu.VMEM((WAVES, POINTS), jnp.float32)] * 2,
        compiler_params=pltpu.CompilerParams(vmem_limit_bytes=24 << 20),
        name="waves",
    )(*[jnp.asarray(seed) for seed in inverse_seeds()])

    phases = pl.pallas_call(
        functools.partial(phase_kernel, half_modes=half_modes),
        out_shape=jax.ShapeDtypeStruct(phase_shape, jnp.float32),
        in_specs=[smem, vmem],
        out_specs=vmem,
        compiler_params=pltpu.CompilerParams(vmem_limit_bytes=24 << 20),
        name="phases",
    )(group, spanwise_position)

    pushed = jnp.dot(
        inverse_high, force.reshape(rows, columns), preferred_element_type=jnp.float32
    )
    modal = (projected + time_step * pushed) * damping
    solved = jnp.dot(eigen_basis, modal, precision=lax.Precision.HIGH).astype(jnp.bfloat16)
    solved = solved.reshape(slabs, slab_rows, columns)
    returned = lax.all_to_all(solved, ("px", "pz"), split_axis=0, concat_axis=0, tiled=True)
    velocity_planes, mode_part = pl.pallas_call(
        functools.partial(gather_kernel, **sizes),
        out_shape=(
            jax.ShapeDtypeStruct((slab_rows, 3, half_modes, 2, NX), jnp.bfloat16),
            jax.ShapeDtypeStruct((3, tiles, size), jnp.bfloat16),
        ),
        in_specs=[smem, vmem, vmem, hbm, vmem, hbm],
        out_specs=(hbm, vmem),
        scratch_shapes=[
            pltpu.VMEM((SPLIT, component_rows, 2 * WAVES), jnp.bfloat16),
            pltpu.VMEM((NX // 128, slab_rows * width, 128), jnp.float32),
            pltpu.VMEM((slab_rows, 3, half_modes, 2, NX), jnp.bfloat16),
            pltpu.VMEM((3, tiles, size), jnp.float32),
            pltpu.VMEM(phase_shape, jnp.float32),
            pltpu.VMEM((SPLIT, 2 * WAVES, POINTS), jnp.bfloat16),
            pltpu.SemaphoreType.DMA((SPLIT,)),
            pltpu.SemaphoreType.DMA,
            pltpu.SemaphoreType.DMA((3,)),
        ],
        compiler_params=pltpu.CompilerParams(vmem_limit_bytes=40 << 20),
        name="gather",
    )(
        block_index,
        cell_index,
        jnp.asarray(gather_rows(half_modes, slab_rows), jnp.bfloat16),
        in_hbm(table),
        returned,
        in_hbm(phases),
    )
    other_part = lax.ppermute(mode_part, "grp", [(0, 1), (1, 0)])
    fluid_at = mode_part.astype(jnp.float32) + other_part.astype(jnp.float32)
    upward = (jnp.arange(3) == 1).astype(jnp.float32)[:, None, None]
    updated_velocity = (
        particle_velocity
        + time_step * response_rate * (fluid_at - particle_velocity)
        - time_step * gravity * upward
    )
    return (velocity_planes, updated_velocity)


def solution(mesh):
    in_specs = (
        P(("px", "pz"), None),
        P(("px", "pz")),
        P(("px", "pz"), None),
        P(("px", "pz"), None),
        P(("px", "pz"), None),
        P(None, ("px", "pz"), None),
        P(None, ("px", "pz"), None),
        P(None, None, ("grp", "pz"), None, "px"),
        P(),
        P(),
        P(),
    )
    out_specs = (P(("px", "pz"), None, "grp", None, None), P(None, ("px", "pz"), None))
    return jax.shard_map(
        on_device, mesh=mesh, in_specs=in_specs, out_specs=out_specs, check_vma=False
    )
```

```python
import functools
import math

import jax
import jax.numpy as jnp
import numpy as np
from jax import lax
from jax.experimental import pallas as pl
from jax.experimental.pallas import tpu as pltpu
from jax.sharding import PartitionSpec as P

NX = 2048
KX = 1024
CB = 256
SPLIT = 4
POINTS = NX // SPLIT
WAVES = KX // SPLIT
TILE_GROUP = 16

time_step = 0.5
gravity = 0.8
viscosity = 0.0001


def turns(rows, columns):
    phase = np.mod(np.asarray(rows)[:, None] * np.asarray(columns)[None, :], NX)
    angles = phase.astype(np.float64) * (2.0 * math.pi / NX)
    return np.cos(angles).astype(np.float32), np.sin(angles).astype(np.float32)


def forward_seeds():
    waves = np.concatenate([SPLIT * np.arange(WAVES) + rest - KX // 2 for rest in range(SPLIT)])
    base = turns(np.arange(8), waves)
    steps = turns(8 * 2 ** np.arange(8), waves)
    scale = np.float32(1.0 / math.sqrt(NX))
    return [base[0] * scale, base[1] * scale, steps[0], steps[1]]


def inverse_seeds():
    points = np.arange(POINTS)
    bases = [
        turns(SPLIT * np.arange(8) + rest - KX // 2, points) for rest in range(SPLIT)
    ]
    steps = turns(8 * SPLIT * 2 ** np.arange(8), points)
    scale = np.float32(1.0 / math.sqrt(NX))
    cosines = np.stack([b[0] for b in bases]) * scale
    sines = np.stack([b[1] for b in bases]) * scale
    return [cosines, sines, steps[0], steps[1]]


def order_matrix(waves):
    matrix = np.zeros((waves, waves), np.float32)
    lanes = np.arange(waves)
    span = waves // SPLIT
    matrix[SPLIT * (lanes % span) + lanes // span, lanes] = 1.0
    return matrix


def spread_rows(half_modes, slab_rows):
    part, mode, y = np.meshgrid(
        np.arange(2), np.arange(half_modes), np.arange(slab_rows), indexing="ij"
    )
    count = part.size
    matrix = np.zeros((count, count), np.float32)
    source = (y * 2 + part) * half_modes + mode
    matrix[np.arange(count), source.ravel()] = 1.0
    return matrix


def gather_rows(half_modes, slab_rows):
    y, mode, part = np.meshgrid(
        np.arange(slab_rows), np.arange(half_modes), np.arange(2), indexing="ij"
    )
    count = part.size
    matrix = np.zeros((2 * count, count), np.float32)
    source = (part * half_modes + mode) * slab_rows + y
    other = ((1 - part) * half_modes + mode) * slab_rows + y
    matrix[np.arange(count), source.ravel()] = 1.0
    matrix[count + np.arange(count), other.ravel()] = np.where(part.ravel() == 0, -1.0, 1.0)
    return matrix


def grow(cos_ref, sin_ref, base, steps, rows):
    cos_ref[0:8, :] = base[0]
    sin_ref[0:8, :] = base[1]
    done = 8
    level = 0
    while done < rows:
        turn_cos = steps[0][level : level + 1, :]
        turn_sin = steps[1][level : level + 1, :]

        def block(index, carry, done=done, turn_cos=turn_cos, turn_sin=turn_sin):
            start = pl.multiple_of(index * 8, 8)
            old_cos = cos_ref[pl.ds(start, 8), :]
            old_sin = sin_ref[pl.ds(start, 8), :]
            cos_ref[pl.ds(done + start, 8), :] = old_cos * turn_cos - old_sin * turn_sin
            sin_ref[pl.ds(done + start, 8), :] = old_sin * turn_cos + old_cos * turn_sin
            return carry

        lax.fori_loop(0, done // 8, block, 0)
        done *= 2
        level += 1


def dot32(a, b):
    return jnp.dot(a, b, preferred_element_type=jnp.float32)


def spread_kernel(
    block_ref,
    group_ref,
    cell_in,
    volume_in,
    rate_in,
    place_in,
    motion_in,
    seen_in,
    base_cos_ref,
    base_sin_ref,
    step_cos_ref,
    step_sin_ref,
    order_ref,
    out_ref,
    field,
    table_cos,
    table_sin,
    table,
    left,
    amounts,
    phases,
    packed,
    cell_ref,
    volume_ref,
    rate_ref,
    place_ref,
    motion_ref,
    seen_ref,
    in_sem,
    out_sem,
    *,
    half_modes,
    pencil_modes,
    pencil_waves,
):
    tiles, size = cell_ref.shape
    strips = NX // CB
    group_rows = 2 * half_modes
    slab_rows = field.shape[1] // (3 * group_rows)
    component_rows = slab_rows * group_rows
    pz_count = half_modes // pencil_modes

    loads = [
        (place_in, place_ref),
        (cell_in, cell_ref),
        (volume_in, volume_ref),
        (rate_in, rate_ref),
        (motion_in, motion_ref),
        (seen_in, seen_ref),
    ]
    loads = [
        pltpu.make_async_copy(source, target, in_sem.at[index])
        for index, (source, target) in enumerate(loads)
    ]
    for load in loads:
        load.start()

    grow(
        table_cos,
        table_sin,
        (base_cos_ref[...], base_sin_ref[...]),
        (step_cos_ref, step_sin_ref),
        POINTS,
    )
    for rest in range(SPLIT):
        lanes = slice(rest * WAVES, (rest + 1) * WAVES)
        table[rest, :, 0:WAVES] = table_cos[:, lanes].astype(jnp.bfloat16)
        table[rest, :, WAVES:] = table_sin[:, lanes].astype(jnp.bfloat16)

    def clear(index, carry):
        field[index] = jnp.zeros(field.shape[1:], jnp.float32)
        return carry

    lax.fori_loop(0, field.shape[0], clear, 0)

    loads[0].wait()
    first = (group_ref[0] * half_modes + 1).astype(jnp.float32)
    for mode, (cosine, sine) in enumerate(turn_modes(place_ref[...], first, half_modes)):
        for piece in range(size // 128):
            lanes = slice(piece * 128, (piece + 1) * 128)
            for part, value in ((0, cosine), (1, -sine)):
                rows = pl.ds(part * half_modes + mode, tiles, stride=group_rows)
                phases[piece, rows, :] = value[:, lanes]

    for load in loads[1:]:
        load.wait()
    upper = cell_ref[...] >= 128
    volume = volume_ref[...]
    pull = volume * rate_ref[...]
    for component in range(3):
        amount = pull * (seen_ref[component] - motion_ref[component])
        if component == 1:
            amount = amount - gravity * volume
        amounts[component] = jnp.where(upper, 0.0, amount)
        amounts[3 + component] = jnp.where(upper, amount, 0.0)

    cells = lax.broadcasted_iota(jnp.int32, (128, size), 0)

    def tile_group(group, carry):
        shares = []
        for offset in range(TILE_GROUP):
            tile = group * TILE_GROUP + offset
            row = pl.ds(tile, 1)
            rows_of_tile = pl.ds(pl.multiple_of(tile * group_rows, 8), group_rows)
            phase = jnp.concatenate(
                [phases[piece, rows_of_tile, :] for piece in range(size // 128)], axis=1
            )
            payload = jnp.concatenate([amounts[k, row, :] * phase for k in range(6)], axis=0)
            spot = cell_ref[row, :] % 128
            one_hot = (spot == cells).astype(jnp.float32).astype(jnp.bfloat16)
            shares.append(
                lax.dot_general(
                    payload.astype(jnp.bfloat16),
                    one_hot,
                    (((1,), (1,)), ((), ())),
                    preferred_element_type=jnp.float32,
                )
            )
        for offset in range(TILE_GROUP):
            block = block_ref[group * TILE_GROUP + offset]
            strip = block % strips
            y = block // strips
            for half in range(2):
                for component in range(3):
                    start = pl.multiple_of(component * component_rows + y * group_rows, 8)
                    own = (half * 3 + component) * group_rows
                    field[strip * 2 + half, pl.ds(start, group_rows), :] += shares[offset][
                        own : own + group_rows
                    ]
        return carry

    lax.fori_loop(0, tiles // TILE_GROUP, tile_group, 0)

    order = order_ref[...]
    def times_minus_i(value):
        lanes = value.shape[1]
        rows = value.shape[0]
        value = value.reshape(rows // group_rows, group_rows, lanes)
        part = lax.broadcasted_iota(jnp.int32, value.shape, 1) // half_modes
        moved = pltpu.roll(value, half_modes, 1)
        return jnp.where(part == 0, moved, -moved).reshape(rows, lanes)

    rest_waves = pencil_waves // SPLIT
    for strip in range(POINTS // 128):
        values = [field[strip + j * (POINTS // 128)] for j in range(SPLIT)]
        lanes = slice(strip * 128, (strip + 1) * 128)
        even_sum = values[0] + values[2]
        odd_sum = values[1] + values[3]
        even_gap = values[0] - values[2]
        odd_gap = times_minus_i(values[1] - values[3])
        left[0, :, lanes] = (even_sum + odd_sum).astype(jnp.bfloat16)
        left[1, :, lanes] = (even_gap + odd_gap).astype(jnp.bfloat16)
        left[2, :, lanes] = (even_sum - odd_sum).astype(jnp.bfloat16)
        left[3, :, lanes] = (even_gap - odd_gap).astype(jnp.bfloat16)
    all_spectra = []
    for rest in range(SPLIT):
        product = dot32(left[rest], table[rest])
        spectrum = product[:, :WAVES] + times_minus_i(product[:, WAVES:])
        all_spectra.append(spectrum.astype(jnp.bfloat16))
    copies = []
    for component in range(3):
        rows = slice(component * component_rows, (component + 1) * component_rows)
        spectra = [
            dot32(order, spectrum[rows]).astype(jnp.bfloat16) for spectrum in all_spectra
        ]
        for owner_px in range(KX // pencil_waves):
            own = slice(owner_px * rest_waves, (owner_px + 1) * rest_waves)
            joined = jnp.concatenate([spectrum[:, own] for spectrum in spectra], axis=1)
            for part in range(2):
                for mode in range(half_modes):
                    column = (
                        (component * pencil_modes + mode % pencil_modes) * 2 + part
                    ) * pencil_waves
                    row = (part * half_modes + mode) * slab_rows
                    packed[
                        owner_px * pz_count + mode // pencil_modes,
                        :,
                        column : column + pencil_waves,
                    ] = joined[row : row + slab_rows]
        span = 2 * pencil_modes * pencil_waves
        lanes = pl.ds(component * span, span)
        copy = pltpu.make_async_copy(
            packed.at[:, :, lanes], out_ref.at[:, :, lanes], out_sem.at[component]
        )
        copy.start()
        copies.append(copy)
    for copy in copies:
        copy.wait()


def table_kernel(base_cos_ref, base_sin_ref, step_cos_ref, step_sin_ref, out_ref, work_cos, work_sin):
    for rest in range(SPLIT):
        grow(
            work_cos,
            work_sin,
            (base_cos_ref[rest], base_sin_ref[rest]),
            (step_cos_ref, step_sin_ref),
            WAVES,
        )
        out_ref[rest, 0:WAVES, :] = work_cos[...].astype(jnp.bfloat16)
        out_ref[rest, WAVES:, :] = work_sin[...].astype(jnp.bfloat16)


def turn_modes(place, first, modes):
    cos_one = jnp.cos(place)
    sin_one = jnp.sin(place)
    cos_now = jnp.cos(place * first)
    sin_now = jnp.sin(place * first)
    turned = [(cos_now, sin_now)]
    for _ in range(modes - 1):
        cos_now, sin_now = (
            cos_now * cos_one - sin_now * sin_one,
            sin_now * cos_one + cos_now * sin_one,
        )
        turned.append((cos_now, sin_now))
    return turned


def phase_kernel(group_ref, place_ref, out_ref, *, half_modes):
    tiles, size = place_ref.shape
    first = (group_ref[0] * half_modes + 1).astype(jnp.float32)
    for mode, (cosine, sine) in enumerate(turn_modes(place_ref[...], first, half_modes)):
        for piece in range(size // 128):
            lanes = slice(piece * 128, (piece + 1) * 128)
            for part, value in ((0, cosine), (1, -sine)):
                rows = pl.ds(2 * mode + part, tiles, stride=2 * half_modes)
                out_ref[piece, rows, :] = value[:, lanes]


def split(value):
    high = value.astype(jnp.bfloat16)
    return high, (value - high.astype(jnp.float32)).astype(jnp.bfloat16)


def project_kernel(high_ref, low_ref, order_ref, state_ref, out_ref):
    order = order_ref[...]
    state_high, state_low = [
        dot32(value, order).astype(jnp.bfloat16) for value in split(state_ref[...])
    ]
    out_ref[...] = (
        dot32(high_ref[...], state_high)
        + dot32(high_ref[...], state_low)
        + dot32(low_ref[...], state_high)
    )


def solve_kernel(
    inverse_ref,
    basis_high_ref,
    basis_low_ref,
    damping_ref,
    state_ref,
    force_ref,
    out_ref,
    inverse,
    basis,
    damping,
    state,
    pushed,
    modal,
    results,
    sems,
    out_sems,
    *,
    pencil_waves,
):
    rows = inverse.shape[0]
    columns = force_ref.shape[-1]
    step = columns // 3
    slab_shape = out_ref.shape[:2]
    spans = [pl.ds(start, step) for start in range(0, columns, step)]
    loads = [
        (inverse_ref, inverse),
        (state_ref.at[:, spans[0]], state.at[:, spans[0]]),
        (damping_ref, damping),
        (basis_high_ref, basis.at[:, pl.ds(0, rows)]),
        (basis_high_ref, basis.at[:, pl.ds(rows, rows)]),
        (basis_low_ref, basis.at[:, pl.ds(2 * rows, rows)]),
        (state_ref.at[:, spans[1]], state.at[:, spans[1]]),
        (state_ref.at[:, spans[2]], state.at[:, spans[2]]),
    ]
    copies = [
        pltpu.make_async_copy(source, target, sems.at[index])
        for index, (source, target) in enumerate(loads)
    ]
    for copy in copies:
        copy.start()
    copies[0].wait()
    pushed[...] = dot32(inverse[...], force_ref[...].reshape(rows, columns))
    stores = []
    for index in range(3):
        lanes = slice(index * step, (index + 1) * step)
        copies[1 if index == 0 else 5 + index].wait()
        if index == 0:
            copies[2].wait()
        for block in range(step // pencil_waves):
            own = slice(block * pencil_waves, (block + 1) * pencil_waves)
            column = slice(index * step + own.start, index * step + own.stop)
            mode = slice((block // 2) * pencil_waves, (block // 2 + 1) * pencil_waves)
            damped = (state[:, column] + time_step * pushed[:, column]) * damping[:, mode]
            high, low = split(damped)
            modal[0:rows, own] = high
            modal[rows : 2 * rows, own] = low
            modal[2 * rows : 3 * rows, own] = high
        if index == 0:
            for copy in copies[3:6]:
                copy.wait()
        solved = dot32(basis[...], modal[...])
        results[:, :, lanes] = solved.astype(jnp.bfloat16).reshape(slab_shape + (step,))
        copy = pltpu.make_async_copy(
            results.at[:, :, spans[index]], out_ref.at[:, :, spans[index]], out_sems.at[index]
        )
        copy.start()
        stores.append(copy)
    for copy in stores:
        copy.wait()


def merge_rows(values):
    sublane = lax.broadcasted_iota(jnp.int32, (8, 128), 0)
    for bit in (4, 2, 1):
        keep = (sublane & bit) == 0
        half = len(values) // 2
        merged = []
        for index in range(half):
            a, b = values[index], values[index + half]
            own = jnp.where(keep, a, b)
            other = jnp.where(keep, b, a)
            if bit == 4:
                moved = pltpu.roll(other, 4, 0)
            else:
                moved = jnp.where(
                    keep, pltpu.roll(other, 8 - bit, 0), pltpu.roll(other, bit, 0)
                )
            merged.append(own + moved)
        values = merged
    return values[0]


def gather_kernel(
    block_ref,
    cell_ref,
    order_ref,
    table_ref,
    back_ref,
    phase_ref,
    planes_ref,
    part_ref,
    left,
    values,
    planes,
    sampled,
    phases,
    table,
    table_sem,
    phase_sem,
    plane_sem,
    *,
    half_modes,
    pencil_modes,
    pencil_waves,
):
    tiles, size = cell_ref.shape
    strips = NX // CB
    group_rows = 2 * half_modes
    slab_rows = back_ref.shape[1]
    pz_count = half_modes // pencil_modes
    component_rows = group_rows * slab_rows
    table_copies = [
        pltpu.make_async_copy(table_ref.at[rest], table.at[rest], table_sem.at[rest])
        for rest in range(SPLIT)
    ]
    for copy in table_copies:
        copy.start()
    phase_copy = pltpu.make_async_copy(phase_ref, phases, phase_sem)
    phase_copy.start()
    rest_waves = pencil_waves // SPLIT

    def times_i(value):
        shape = value.shape
        value = value.reshape(shape[0] // 8, 8, shape[1])
        part = lax.broadcasted_iota(jnp.int32, value.shape, 1) % 2
        return jnp.where(
            part == 0, -pltpu.roll(value, 7, 1), pltpu.roll(value, 1, 1)
        ).reshape(shape)

    copies = []
    for component in range(3):
        rows = []
        for part in range(2):
            for mode in range(half_modes):
                column = (
                    (component * pencil_modes + mode % pencil_modes) * 2 + part
                ) * pencil_waves
                sources = [
                    back_ref[
                        px * pz_count + mode // pencil_modes, :, column : column + pencil_waves
                    ]
                    for px in range(KX // pencil_waves)
                ]
                rows.append(
                    jnp.concatenate(
                        [
                            source[:, rest * rest_waves : (rest + 1) * rest_waves]
                            for rest in range(SPLIT)
                            for source in sources
                        ],
                        axis=1,
                    )
                )
        turned = dot32(order_ref[...], jnp.concatenate(rows, axis=0)).astype(jnp.bfloat16)
        results = []
        for rest in range(SPLIT):
            lanes = slice(rest * WAVES, (rest + 1) * WAVES)
            left[rest, :, 0:WAVES] = turned[0:component_rows, lanes]
            left[rest, :, WAVES:] = turned[component_rows:, lanes]
            if component == 0:
                table_copies[rest].wait()
            results.append(dot32(left[rest], table[rest]))
        even_sum = results[0] + results[2]
        odd_sum = results[1] + results[3]
        even_gap = results[0] - results[2]
        odd_gap = times_i(results[1] - results[3])
        quarters = [even_sum + odd_sum, even_gap + odd_gap, even_sum - odd_sum, even_gap - odd_gap]
        for side, quarter in enumerate(quarters):
            plane = quarter.astype(jnp.bfloat16)
            whole = plane.astype(jnp.float32)
            planes[:, component, :, :, side * POINTS : (side + 1) * POINTS] = plane.reshape(
                slab_rows, half_modes, 2, POINTS
            )
            for strip in range(POINTS // 128):
                values[
                    side * (POINTS // 128) + strip,
                    component * component_rows : (component + 1) * component_rows,
                    :,
                ] = whole[:, strip * 128 : (strip + 1) * 128]
        copy = pltpu.make_async_copy(
            planes.at[:, component], planes_ref.at[:, component], plane_sem.at[component]
        )
        copy.start()
        copies.append(copy)
    phase_copy.wait()

    def tile_group(group, carry):
        first_tile = pl.multiple_of(group * 8, 8)
        places = []
        for offset in range(8):
            block = block_ref[first_tile + offset]
            places.append((block % strips, block // strips))
        cells = cell_ref[pl.ds(first_tile, 8), :]
        for piece in range(size // 128):
            lanes = slice(piece * 128, (piece + 1) * 128)
            weighted = [[], [], []]
            for offset in range(8):
                strip, y = places[offset]
                cell = jnp.broadcast_to(cells[offset : offset + 1, lanes], (group_rows, 128))
                spot = cell % 128
                upper = cell >= 128
                rows_of_tile = pl.multiple_of((first_tile + offset) * group_rows, 8)
                phase = phases[piece, pl.ds(rows_of_tile, group_rows), :]
                for component in range(3):
                    start = pl.multiple_of(component * component_rows + y * group_rows, 8)
                    rows = pl.ds(start, group_rows)
                    low = jnp.take_along_axis(values[strip * 2, rows, :], spot, axis=1)
                    high = jnp.take_along_axis(values[strip * 2 + 1, rows, :], spot, axis=1)
                    product = jnp.where(upper, high, low) * phase
                    total = product[0:8]
                    for more in range(8, group_rows, 8):
                        total = total + product[more : more + 8]
                    weighted[component].append(total)
            for component in range(3):
                sampled[component, pl.ds(first_tile, 8), lanes] = merge_rows(weighted[component])
        return carry

    lax.fori_loop(0, tiles // 8, tile_group, 0)
    part_ref[...] = sampled[...].astype(jnp.bfloat16)
    for copy in copies:
        copy.wait()


def on_device(
    cell_index,
    block_index,
    volume,
    response_rate,
    spanwise_position,
    particle_velocity,
    seen_velocity,
    fluid_velocity,
    eigen_basis,
    eigen_inverse,
    eigenvalues,
):
    group_index = lax.axis_index("grp")
    px_count = lax.axis_size("px")
    pz_count = lax.axis_size("pz")
    rows = fluid_velocity.shape[0]
    pencil_modes = fluid_velocity.shape[2]
    pencil_waves = fluid_velocity.shape[4]
    half_modes = pencil_modes * pz_count
    slabs = px_count * pz_count
    slab_rows = rows // slabs
    strips = NX // CB
    tiles, size = cell_index.shape
    width = 6 * half_modes
    component_rows = 2 * half_modes * slab_rows
    columns = 6 * pencil_modes * pencil_waves
    pencil = pencil_modes * pencil_waves
    sizes = dict(half_modes=half_modes, pencil_modes=pencil_modes, pencil_waves=pencil_waves)

    vmem = pl.BlockSpec(memory_space=pltpu.VMEM)
    smem = pl.BlockSpec(memory_space=pltpu.SMEM)
    hbm = pl.BlockSpec(memory_space=pltpu.HBM)
    in_hbm = functools.partial(pltpu.with_memory_space_constraint, memory_space=pltpu.HBM)
    phase_shape = (size // 128, tiles * 2 * half_modes, 128)

    group = group_index.reshape(1).astype(jnp.int32)
    outgoing = pl.pallas_call(
        functools.partial(spread_kernel, **sizes),
        out_shape=jax.ShapeDtypeStruct((slabs, slab_rows, columns), jnp.bfloat16),
        in_specs=[smem, smem] + [hbm] * 6 + [vmem] * 5,
        out_specs=hbm,
        scratch_shapes=[
            pltpu.VMEM((NX // 128, slab_rows * width, 128), jnp.float32),
            pltpu.VMEM((POINTS, KX), jnp.float32),
            pltpu.VMEM((POINTS, KX), jnp.float32),
            pltpu.VMEM((SPLIT, POINTS, 2 * WAVES), jnp.bfloat16),
            pltpu.VMEM((SPLIT, 3 * component_rows, POINTS), jnp.bfloat16),
            pltpu.VMEM((6, tiles, size), jnp.float32),
            pltpu.VMEM(phase_shape, jnp.float32),
            pltpu.VMEM((slabs, slab_rows, columns), jnp.bfloat16),
            pltpu.VMEM((tiles, size), jnp.int32),
        ]
        + [pltpu.VMEM((tiles, size), jnp.float32)] * 3
        + [pltpu.VMEM((3, tiles, size), jnp.float32)] * 2
        + [pltpu.SemaphoreType.DMA((6,)), pltpu.SemaphoreType.DMA((3,))],
        name="spread",
    )(
        block_index,
        group,
        cell_index,
        volume,
        response_rate,
        spanwise_position,
        particle_velocity,
        seen_velocity,
        *[jnp.asarray(seed) for seed in forward_seeds()],
        jnp.asarray(spread_rows(half_modes, slab_rows), jnp.bfloat16),
    )
    force = lax.all_to_all(outgoing, ("px", "pz"), split_axis=0, concat_axis=0, tiled=True)

    def halves(matrix):
        high = lax.reduce_precision(matrix, 8, 7)
        return high.astype(jnp.bfloat16), (matrix - high).astype(jnp.bfloat16)

    inverse_high, inverse_low = halves(eigen_inverse)
    basis_high, basis_low = halves(eigen_basis)
    state = fluid_velocity.transpose(0, 1, 2, 3, 4).reshape(rows, columns)
    square = pl.BlockSpec((rows, rows), lambda i: (0, 0))
    strip_spec = pl.BlockSpec((rows, pencil_waves), lambda i: (0, i))
    projected = pl.pallas_call(
        project_kernel,
        grid=(columns // pencil_waves,),
        out_shape=jax.ShapeDtypeStruct((rows, columns), jnp.float32),
        in_specs=[
            square,
            square,
            pl.BlockSpec((pencil_waves, pencil_waves), lambda i: (0, 0)),
            strip_spec,
        ],
        out_specs=strip_spec,
        compiler_params=pltpu.CompilerParams(vmem_limit_bytes=24 << 20),
        name="project",
    )(inverse_high, inverse_low, jnp.asarray(order_matrix(pencil_waves), jnp.bfloat16), state)
    lane = jnp.arange(pencil_waves)
    rest_waves = pencil_waves // SPLIT
    wave = SPLIT * (lane % rest_waves) + lane // rest_waves
    stream_wave = (lax.axis_index("px") * pencil_waves + wave - KX // 2).astype(jnp.float32) * 0.5
    span_wave = (
        group_index * half_modes
        + lax.axis_index("pz") * pencil_modes
        + jnp.arange(pencil_modes)
        + 1
    ).astype(jnp.float32)
    wave_square = (
        stream_wave[None, :] * stream_wave[None, :] + span_wave[:, None] * span_wave[:, None]
    )
    wave_square = jnp.broadcast_to(
        wave_square[None, :, None, :], (3, pencil_modes, 2, pencil_waves)
    ).reshape(1, columns)
    damping = 1.0 / (1.0 + viscosity * (eigenvalues[:, None] + wave_square))
    table = pl.pallas_call(
        table_kernel,
        out_shape=jax.ShapeDtypeStruct((SPLIT, 2 * WAVES, POINTS), jnp.bfloat16),
        in_specs=[vmem] * 4,
        out_specs=vmem,
        scratch_shapes=[pltpu.VMEM((WAVES, POINTS), jnp.float32)] * 2,
        compiler_params=pltpu.CompilerParams(vmem_limit_bytes=24 << 20),
        name="waves",
    )(*[jnp.asarray(seed) for seed in inverse_seeds()])

    phases = pl.pallas_call(
        functools.partial(phase_kernel, half_modes=half_modes),
        out_shape=jax.ShapeDtypeStruct(phase_shape, jnp.float32),
        in_specs=[smem, vmem],
        out_specs=vmem,
        compiler_params=pltpu.CompilerParams(vmem_limit_bytes=24 << 20),
        name="phases",
    )(group, spanwise_position)

    pushed = jnp.dot(
        inverse_high, force.reshape(rows, columns), preferred_element_type=jnp.float32
    )
    modal = (projected + time_step * pushed) * damping
    solved = jnp.dot(eigen_basis, modal, precision=lax.Precision.HIGH).astype(jnp.bfloat16)
    solved = solved.reshape(slabs, slab_rows, columns)
    returned = lax.all_to_all(solved, ("px", "pz"), split_axis=0, concat_axis=0, tiled=True)
    velocity_planes, mode_part = pl.pallas_call(
        functools.partial(gather_kernel, **sizes),
        out_shape=(
            jax.ShapeDtypeStruct((slab_rows, 3, half_modes, 2, NX), jnp.bfloat16),
            jax.ShapeDtypeStruct((3, tiles, size), jnp.bfloat16),
        ),
        in_specs=[smem, vmem, vmem, hbm, vmem, hbm],
        out_specs=(hbm, vmem),
        scratch_shapes=[
            pltpu.VMEM((SPLIT, component_rows, 2 * WAVES), jnp.bfloat16),
            pltpu.VMEM((NX // 128, slab_rows * width, 128), jnp.float32),
            pltpu.VMEM((slab_rows, 3, half_modes, 2, NX), jnp.bfloat16),
            pltpu.VMEM((3, tiles, size), jnp.float32),
            pltpu.VMEM(phase_shape, jnp.float32),
            pltpu.VMEM((SPLIT, 2 * WAVES, POINTS), jnp.bfloat16),
            pltpu.SemaphoreType.DMA((SPLIT,)),
            pltpu.SemaphoreType.DMA,
            pltpu.SemaphoreType.DMA((3,)),
        ],
        compiler_params=pltpu.CompilerParams(vmem_limit_bytes=40 << 20),
        name="gather",
    )(
        block_index,
        cell_index,
        jnp.asarray(gather_rows(half_modes, slab_rows), jnp.bfloat16),
        in_hbm(table),
        returned,
        in_hbm(phases),
    )
    other_part = lax.ppermute(mode_part, "grp", [(0, 1), (1, 0)])
    fluid_at = mode_part.astype(jnp.float32) + other_part.astype(jnp.float32)
    upward = (jnp.arange(3) == 1).astype(jnp.float32)[:, None, None]
    updated_velocity = (
        particle_velocity
        + time_step * response_rate * (fluid_at - particle_velocity)
        - time_step * gravity * upward
    )
    return (velocity_planes, updated_velocity)


def solution(mesh):
    in_specs = (
        P(("px", "pz"), None),
        P(("px", "pz")),
        P(("px", "pz"), None),
        P(("px", "pz"), None),
        P(("px", "pz"), None),
        P(None, ("px", "pz"), None),
        P(None, ("px", "pz"), None),
        P(None, None, ("grp", "pz"), None, "px"),
        P(),
        P(),
        P(),
    )
    out_specs = (P(("px", "pz"), None, "grp", None, None), P(None, ("px", "pz"), None))
    return jax.shard_map(
        on_device, mesh=mesh, in_specs=in_specs, out_specs=out_specs, check_vma=False
    )
```
